32 devices in a mesh: seq: 8 (over z, x), exp: 4 (over y, core).
Axes of the slice: x: 2, y: 2, z: 4, core: 2. Of those that a mesh axis runs over, the one named last changes fastest.
Arguments:
- tokens: bfloat16 [8192, 2560], P(('seq', 'exp')), may hold values from -6 to 6
- routes: int32 [8192, 1], P(('seq', 'exp')), may hold values from 0 to 15; in each aligned block of 256 rows (0 to 255, 256 to 511, ...) at most 32 rows name the same one
- gate_inner_weight: bfloat16 [2560, 2, 3072], P(None, None, 'exp'), may hold values from -0.125 to 0.125
- state_map_weight: bfloat16 [2560, 256], replicated, may hold values from -0.125 to 0.125
- step_size_weight: bfloat16 [2560, 48], P(None, 'exp'), may hold values from -0.125 to 0.125
- adapter_down_weight: bfloat16 [2560, 128], P(None, 'exp'), may hold values from -0.125 to 0.125
- adapter_up_weight: bfloat16 [128, 2, 3072], P(None, None, 'exp'), may hold values from -1.5 to 1.5
- inner_conv_taps: float32 [4, 3072], P(None, 'exp'), may hold values from -3 to 3
- state_map_taps: float32 [4, 256], replicated, may hold values from -3 to 3
- inner_conv_bias: float32 [3072], P('exp'), may hold values from -3 to 3
- state_map_conv_bias: float32 [256], replicated, may hold values from -3 to 3
- step_size_bias: float32 [48], P('exp'), may hold values from -6 to -3
- head_decay_rate: float32 [48], P('exp'), may hold values from 7.4505806e-05 to 8
- direct_head_scale: float32 [48], P('exp'), may hold values from 0.5 to 2
- gated_norm_scale: float32 [3072], P('exp'), may hold values from 0.5 to 1.5
Outputs:
- mixed: bfloat16 [8192, 3072], P('seq', 'exp')
The draws below stay inside these ranges and needn't reach their ends.
Inputs may be any that keep to these rules, and one draw needn't show every extreme that they name: `routes`: among the rows of one device no expert is named more than 32 times.
All inputs are finite; a program needn't handle non-finite values.
Results may differ from the reference program's by a relative error of at most 0.0034.
Values may be sent and summed in bfloat16 or wider, within the bound.
No kernel may reach another device: no remote copies, remote signals or barrier semaphores. Data moves between devices by JAX's collectives and lax.ppermute only.
A program may use at most 64 MiB of HBM per device.

```python
import math
import jax
import jax.numpy as jnp
import numpy as np
from jax import lax

MODEL_WIDTH = 2560
STATE = 128
HEADDIM = 64
KERNEL = 4
H = 48
ADAPTER_EXPERTS = 16
EXPERT_RANK = 8
GROUP = 256
TOK_DEV = 1024
SEQ_LEN = 8192
INNER_WIDTH = 3072
CAPACITY = 32
N_EXP = 4


def draw_head_decay_rate(key, part):
    lowest = math.log(5000.0 / SEQ_LEN ** 2)
    highest = math.log(8.0)
    spread = jax.random.uniform(key, (H,), jnp.float32)
    return jnp.exp(lowest + (highest - lowest) * spread)


def block_scale(rng, shape, split, smallest, top_value):
    factor_of = 1.0
    for position, parts in split:
        heights = jax.random.uniform(jax.random.fold_in(jax.random.fold_in(rng, 6), position), (parts,), jnp.float32, smallest / len(split), top_value / len(split))
        factor_of = factor_of * jnp.repeat(jnp.exp(heights), shape[position] // parts).reshape((-1,) + (1,) * (len(shape) - 1 - position))
    return factor_of


def shared_out(key, own, number, rows, number_of, top, reach, skew):
    ranking = jax.random.permutation(key, number_of)
    crowded, ordinary = load_shares(number_of, rows * top, reach, skew, True), load_shares(number_of, rows * top, reach, skew, False)
    places = jnp.arange(number_of)

    def named(sizes, turn):
        used = int((sizes > 0).sum())
        fixed = max(1, used // 4)
        moved = fixed + (places - fixed + turn * (used - fixed)) % max(1, number_of - fixed)
        return jnp.zeros((number_of,), jnp.int32).at[ranking[jnp.where(places < fixed, places, moved)]].set(jnp.asarray(sizes, jnp.int32))

    sizes = jnp.where(number % 4 == 0, named(crowded, number // 4), named(ordinary, number - number // 4 - 1))
    mixed = jax.random.permutation(jax.random.fold_in(own, 3), number_of)
    donor, receiver = mixed[0:number_of // 2 * 2:2], mixed[1:number_of // 2 * 2:2]
    slack = jnp.minimum(sizes[donor] - 1, reach - sizes[receiver]) // 2
    slack = jnp.where((donor == ranking[0]) | (receiver == ranking[0]) | (sizes[receiver] == 0), 0, jnp.maximum(slack, 0))
    moved = jax.random.randint(jax.random.fold_in(own, 4), (number_of // 2,), 0, 1 << 20) % (slack + 1)
    sizes = sizes.at[donor].add(-moved).at[receiver].add(moved)
    items = jnp.searchsorted(jnp.cumsum(sizes), jnp.arange(rows * top), side="right").astype(jnp.int32)
    listing = items.reshape(top, rows).T
    listing = listing[jax.random.permutation(jax.random.fold_in(own, 1), rows)]
    turn = jax.random.randint(jax.random.fold_in(own, 2), (rows, 1), 0, top)
    return jnp.take_along_axis(listing, (jnp.arange(top)[None, :] + turn) % top, axis=1)


def load_shares(number_of, total, reach, lean, full):
    weights = [(1 << 20) // math.isqrt(rank ** lean) + 1 for rank in range(1, number_of + 1)]
    largest = reach if full else min(reach, max(-(-total // number_of), total * weights[0] // sum(weights)))
    least = 1 if total - largest >= number_of - 1 else 0
    holding, surplus = [largest] + [least] * (number_of - 1), total - largest - least * (number_of - 1)
    while surplus > 0:
        movable = [i for i in range(1, number_of) if holding[i] < largest] or [i for i in range(1, number_of) if holding[i] < reach]
        whole, left = sum([weights[i] for i in movable]), surplus
        for i in movable:
            more = min(reach - holding[i], max(1, left * weights[i] // whole), surplus)
            holding[i] = holding[i] + more
            surplus = surplus - more
    return np.array(holding)


def noise(rng, extent, scale, most, cuts=(), held_as=jnp.bfloat16):
    gain = block_scale(rng, extent, cuts, -0.22, 0.18) if cuts else 1.0
    array = jax.random.normal(rng, extent, jnp.float32) * scale * gain
    return jnp.minimum(jnp.maximum(array, -most), most).astype(held_as)


def setup_inputs(seed: int = 0) -> dict:
    keys = jax.random.split(jax.random.key(seed), 16)
    tokens = noise(keys[0], (SEQ_LEN, MODEL_WIDTH), 1.0, 6.0, ((0, 32),))
    routes_keys = jax.random.split(jax.random.fold_in(keys[1], 1), SEQ_LEN // (TOK_DEV // N_EXP))
    routes_turns = jax.random.permutation(jax.random.fold_in(keys[1], 3), SEQ_LEN // (TOK_DEV // N_EXP))
    routes = jax.vmap(lambda own, number: shared_out(jax.random.fold_in(keys[1], 2), own, number, TOK_DEV // N_EXP, ADAPTER_EXPERTS, 1, CAPACITY, 2))(routes_keys, routes_turns).reshape((SEQ_LEN, 1))
    gate_inner_weight = noise(keys[2], (MODEL_WIDTH, 2, INNER_WIDTH), MODEL_WIDTH ** -0.5, 0.125, ((2, 4),))
    state_map_weight = noise(keys[3], (MODEL_WIDTH, 2 * STATE), MODEL_WIDTH ** -0.5, 0.125)
    step_size_weight = noise(keys[4], (MODEL_WIDTH, H), MODEL_WIDTH ** -0.5, 0.125, ((1, 4),))
    adapter_down_weight = noise(keys[5], (MODEL_WIDTH, ADAPTER_EXPERTS * EXPERT_RANK), MODEL_WIDTH ** -0.5, 0.125, ((1, 4),))
    adapter_up_weight = noise(keys[6], (ADAPTER_EXPERTS * EXPERT_RANK, 2, INNER_WIDTH), (2 * EXPERT_RANK) ** -0.5, 1.5, ((2, 4),))
    inner_conv_taps = noise(keys[7], (KERNEL, INNER_WIDTH), KERNEL ** -0.5, 3.0, ((1, 4),), jnp.float32)
    state_map_taps = noise(keys[8], (KERNEL, 2 * STATE), KERNEL ** -0.5, 3.0, (), jnp.float32)
    inner_conv_bias = noise(keys[9], (INNER_WIDTH,), 0.5, 3.0, ((0, 4),), jnp.float32)
    state_map_conv_bias = noise(keys[10], (2 * STATE,), 0.5, 3.0, (), jnp.float32)
    step_size_bias = jnp.clip(-6.0 + 3.0 * jax.random.uniform(keys[11], (H,), jnp.float32) ** block_scale(keys[11], (H,), ((0, 4),), -0.2, 0.2), -6.0, -3.0)
    head_decay_rate = draw_head_decay_rate(jax.random.fold_in(keys[15], 71), 0)
    direct_head_scale = jnp.clip(0.5 + 1.5 * jax.random.uniform(keys[13], (H,), jnp.float32) ** block_scale(keys[13], (H,), ((0, 4),), -0.2, 0.2), 0.5, 2.0)
    gated_norm_scale = jnp.clip(1.0 + 0.1 * jax.random.normal(keys[14], (INNER_WIDTH,), jnp.float32), 0.5, 1.5)
    return dict(tokens=tokens, routes=routes, gate_inner_weight=gate_inner_weight, state_map_weight=state_map_weight, step_size_weight=step_size_weight, adapter_down_weight=adapter_down_weight, adapter_up_weight=adapter_up_weight, inner_conv_taps=inner_conv_taps, state_map_taps=state_map_taps, inner_conv_bias=inner_conv_bias, state_map_conv_bias=state_map_conv_bias, step_size_bias=step_size_bias, head_decay_rate=head_decay_rate, direct_head_scale=direct_head_scale, gated_norm_scale=gated_norm_scale)


HIGH = lax.Precision.HIGHEST

def block_step(state, items):
    inner, bmap, cmap, step, decay = items
    cumul = jnp.cumsum(decay, axis=0)
    length = decay.shape[0]
    rows = lax.broadcasted_iota(jnp.int32, (length, length), 0)
    cols = lax.broadcasted_iota(jnp.int32, (length, length), 1)
    causal = (rows >= cols)[:, :, None]
    differ = jnp.where(causal, cumul[:, None, :] - cumul[None, :, :], 0.0)
    segment = jnp.where(causal, jnp.exp(differ), 0.0)
    gram = jnp.dot(cmap, bmap.T, precision=HIGH)
    weights = gram[:, :, None] * segment * step[None, :, :]
    output = jnp.einsum('ijh,jhp->ihp', weights, inner, precision=HIGH)
    output = output + jnp.exp(cumul)[:, :, None] * jnp.einsum('in,hnp->ihp', cmap, state, precision=HIGH)
    final = cumul[-1]
    carried = jnp.exp(final[None, :] - cumul) * step
    update = jnp.einsum('jn,jhp->hnp', bmap, carried[:, :, None] * inner, precision=HIGH)
    return (jnp.exp(final)[:, None, None] * state + update, output)

def run_blocks(inner, bmap, cmap, step, decay, state, block):
    total = inner.shape[0]
    count_blocks = total // block
    items = (inner.reshape(count_blocks, block, inner.shape[1], inner.shape[2]), bmap.reshape(count_blocks, block, bmap.shape[1]), cmap.reshape(count_blocks, block, cmap.shape[1]), step.reshape(count_blocks, block, step.shape[1]), decay.reshape(count_blocks, block, decay.shape[1]))
    final, output = lax.scan(block_step, state, items)
    return (final, output.reshape(total, inner.shape[1], inner.shape[2]))

def causal_conv(extended, weights, bias):
    length = extended.shape[0] - weights.shape[0] + 1
    output = bias[None, :] + jnp.zeros((length, weights.shape[1]), jnp.float32)
    for shift_idx in range(weights.shape[0]):
        output = output + weights[shift_idx][None, :] * extended[shift_idx:shift_idx + length]
    return jax.nn.silu(output)

def pick_ranks(partial_columns, route, first, experts, width):
    column_expert = first + lax.broadcasted_iota(jnp.int32, (experts * width,), 0) // width
    masked = jnp.where(route[:, None] == column_expert[None, :], partial_columns, 0.0)
    return lax.optimization_barrier(jnp.sum(masked.reshape(partial_columns.shape[0], experts, width), axis=1))

def lift_ranks(ranks, route, experts):
    width = ranks.shape[1]
    column_expert = lax.broadcasted_iota(jnp.int32, (experts * width,), 0) // width
    repeated_tiles = jnp.tile(ranks, (1, experts))
    return jnp.where(route[:, None] == column_expert[None, :], repeated_tiles, jnp.zeros_like(repeated_tiles))

def reference(tokens, routes, gate_inner_weight, state_map_weight, step_size_weight, adapter_down_weight, adapter_up_weight, inner_conv_taps, state_map_taps, inner_conv_bias, state_map_conv_bias, step_size_bias, head_decay_rate, direct_head_scale, gated_norm_scale):
    route = routes[:, 0]
    length = tokens.shape[0]
    partial_columns = jnp.dot(tokens, adapter_down_weight, preferred_element_type=jnp.float32)
    ranks = pick_ranks(partial_columns, route, 0, ADAPTER_EXPERTS, EXPERT_RANK).astype(jnp.bfloat16)
    raised_values = lift_ranks(ranks, route, ADAPTER_EXPERTS)
    gate_inner_values = jnp.dot(tokens, gate_inner_weight.reshape(MODEL_WIDTH, 2 * INNER_WIDTH), preferred_element_type=jnp.float32)
    gate_inner_values = gate_inner_values + jnp.dot(raised_values, adapter_up_weight.reshape(ADAPTER_EXPERTS * EXPERT_RANK, 2 * INNER_WIDTH), preferred_element_type=jnp.float32)
    gate = gate_inner_values[:, :INNER_WIDTH]
    inner = gate_inner_values[:, INNER_WIDTH:]
    bc_raw = jnp.dot(tokens, state_map_weight, preferred_element_type=jnp.float32)
    dt_raw = jnp.dot(tokens, step_size_weight, preferred_element_type=jnp.float32)
    margin = KERNEL - 1
    xconv = causal_conv(jnp.pad(inner, ((margin, 0), (0, 0))), inner_conv_taps, inner_conv_bias)
    bconv = causal_conv(jnp.pad(bc_raw, ((margin, 0), (0, 0))), state_map_taps, state_map_conv_bias)
    bmap = bconv[:, :STATE]
    cmap = bconv[:, STATE:]
    step = jax.nn.softplus(dt_raw + step_size_bias[None, :])
    decay = -head_decay_rate[None, :] * step
    heads_in = xconv.reshape(length, H, HEADDIM)
    start = jnp.zeros((H, STATE, HEADDIM), jnp.float32)
    final, output = run_blocks(heads_in, bmap, cmap, step, decay, start, GROUP)
    output = output + direct_head_scale[None, :, None] * heads_in
    gated = output.reshape(length, INNER_WIDTH) * jax.nn.silu(gate)
    meansq = lax.optimization_barrier(jnp.mean(gated * gated, axis=1, keepdims=True))
    return (gated * lax.rsqrt(meansq + 1e-05) * gated_norm_scale[None, :]).astype(jnp.bfloat16)
```

```python
import functools

import jax
import jax.numpy as jnp
from jax import lax
from jax.experimental import pallas as pl
from jax.experimental.pallas import tpu as pltpu
from jax.sharding import PartitionSpec as P

STATE = 128
HEADDIM = 64
PIECE = 64
CHUNK = 128
LANES = 128
F32 = jnp.float32
BF16 = jnp.bfloat16


def swap(block, axis, mask):
    return lax.ppermute(block, axis, [(i, i ^ mask) for i in range(lax.axis_size(axis))])


def split3(value):
    hi = value.astype(BF16)
    rest = value - hi.astype(F32)
    mid = rest.astype(BF16)
    lo = (rest - mid.astype(F32)).astype(BF16)
    return hi, mid, lo


def split2(value):
    hi = value.astype(BF16)
    return hi, (value - hi.astype(F32)).astype(BF16)


def mm(a, b):
    return jnp.dot(a, b, preferred_element_type=F32)


def mm_nt(a, b):
    return lax.dot_general(a, b, (((1,), (1,)), ((), ())), preferred_element_type=F32)


def silu(v):
    return v / (1.0 + jnp.exp(-v))


def route_mask(index_ref, route_row, experts_dev, rank):
    e = index_ref[0]
    column = lax.broadcasted_iota(jnp.int32, (LANES, route_row.shape[1]), 0)
    per_dev = experts_dev * rank
    expert = ((column // per_dev) ^ e) * experts_dev + (column % per_dev) // rank
    return jnp.where(expert == route_row, 1.0, 0.0).astype(F32)


def project_kernel(experts_dev, rank, inner_tiles, counts, index_ref, *refs):
    x_refs = refs[: len(counts)]
    refs = refs[len(counts):]
    route_ref, wsm_ref, w_ref, up_ref = refs[:4]
    z_ref, dt_ref, lift_ref, x_scr = refs[-4:]
    tile = pl.program_id(0)

    @pl.when(tile == 0)
    def _():
        at = 0
        for x_ref, n in zip(x_refs, counts):
            x_scr[at : at + n, :] = x_ref[...]
            at += n
        small = mm_nt(x_scr[...], wsm_ref[...])
        columns = small[:, :LANES]
        masks = []
        for row in range(route_ref.shape[0]):
            for part in range(route_ref.shape[1] // LANES):
                block = route_ref[row : row + 1, part * LANES : (part + 1) * LANES]
                masks.append(route_mask(index_ref, block, experts_dev, rank).T)
        if route_ref.shape[1] % LANES:
            pair = jnp.concatenate([route_ref[0:1, :], route_ref[1:2, :]], axis=1)
            masks.append(route_mask(index_ref, pair, experts_dev, rank).T)
        mask = masks[0] if len(masks) == 1 else jnp.concatenate(masks, axis=0)
        lift_ref[...] = jnp.where(mask > 0.5, columns, 0.0).astype(BF16)
        pad = jnp.zeros((small.shape[0], LANES - (small.shape[1] - LANES)), F32)
        dt_ref[...] = jnp.concatenate([small[:, LANES:], pad], axis=1)

    @pl.when(tile < inner_tiles)
    def _():
        z_ref[...] = mm(x_scr[...], w_ref[...]) + mm(lift_ref[...], up_ref[...])

    @pl.when(tile >= inner_tiles)
    def _():
        z_ref[...] = mm(x_scr[...], w_ref[...])


def project(index, xs, route, wsm, wbig, up, rank, total, row_block, buffers):
    counts = tuple(x.shape[0] for x in xs)
    rows = sum(counts)
    width = wbig.shape[1]
    inner = up.shape[1]
    tn = 256 if inner % 256 == 0 and width % 256 == 0 else 128
    inner_tiles = inner // tn
    features = wbig.shape[0]
    const = lambda t, i: (0, 0)
    in_specs = [pl.BlockSpec(x.shape, const) for x in xs] + [
        pl.BlockSpec(route.shape, const),
        pl.BlockSpec(wsm.shape, const),
        pl.BlockSpec((features, tn), lambda t, i: (0, t)),
        pl.BlockSpec((up.shape[0], tn), lambda t, i: (0, jnp.minimum(t, inner_tiles - 1))),
    ]
    args = list(xs) + [route, wsm, wbig, up]
    aliases = {}
    if buffers is not None:
        for n, buffer in enumerate(buffers):
            aliases[1 + len(args)] = n
            args.append(buffer)
            in_specs.append(pl.BlockSpec(memory_space=pl.ANY))
    experts_dev = LANES // rank // lax.axis_size("exp")
    return pl.pallas_call(
        functools.partial(project_kernel, experts_dev, rank, inner_tiles, counts),
        out_shape=(
            jax.ShapeDtypeStruct((total, width), F32),
            jax.ShapeDtypeStruct((total, LANES), F32),
            jax.ShapeDtypeStruct((total, LANES), BF16),
        ),
        grid_spec=pltpu.PrefetchScalarGridSpec(
            num_scalar_prefetch=1,
            grid=(width // tn,),
            in_specs=in_specs,
            out_specs=(
                pl.BlockSpec((rows, tn), lambda t, i: (row_block, t)),
                pl.BlockSpec((rows, LANES), lambda t, i: (row_block, 0)),
                pl.BlockSpec((rows, LANES), lambda t, i: (row_block, 0)),
            ),
            scratch_shapes=[pltpu.VMEM((rows, features), BF16)],
        ),
        input_output_aliases=aliases,
        cost_estimate=pl.CostEstimate(
            flops=2 * rows * features * (width + 256),
            transcendentals=0,
            bytes_accessed=2 * features * (width + rows) + 4 * rows * width,
        ),
        compiler_params=pltpu.CompilerParams(dimension_semantics=("arbitrary",)),
        name="project",
    )(index, *args)


def gate_kernel(counts, *refs):
    x_refs = refs[: len(counts)]
    lift_ref, w_ref, up_ref, g_ref, x_scr = refs[len(counts):]

    @pl.when(pl.program_id(0) == 0)
    def _():
        at = 0
        for x_ref, n in zip(x_refs, counts):
            x_scr[at : at + n, :] = x_ref[...]
            at += n

    g_ref[...] = mm(x_scr[...], w_ref[...]) + mm(lift_ref[...], up_ref[...])


def gate_project(xs, lift, w, up):
    counts = tuple(x.shape[0] for x in xs)
    rows = sum(counts)
    features, width = w.shape
    tn = 256 if width % 256 == 0 else 128
    const = lambda t: (0, 0)
    return pl.pallas_call(
        functools.partial(gate_kernel, counts),
        out_shape=jax.ShapeDtypeStruct((rows, width), F32),
        grid=(width // tn,),
        in_specs=[pl.BlockSpec(x.shape, const) for x in xs]
        + [
            pl.BlockSpec(lift.shape, const),
            pl.BlockSpec((features, tn), lambda t: (0, t)),
            pl.BlockSpec((up.shape[0], tn), lambda t: (0, t)),
        ],
        out_specs=pl.BlockSpec((rows, tn), lambda t: (0, t)),
        scratch_shapes=[pltpu.VMEM((rows, features), BF16)],
        cost_estimate=pl.CostEstimate(
            flops=2 * rows * features * width,
            transcendentals=0,
            bytes_accessed=2 * features * (width + rows) + 4 * rows * width,
        ),
        compiler_params=pltpu.CompilerParams(dimension_semantics=("arbitrary",)),
        name="gate_project",
    )(*xs, lift, w, up)


def expand_matrix(parts, width):
    head = lax.broadcasted_iota(jnp.int32, (parts * LANES, width), 0) % LANES
    lane = lax.broadcasted_iota(jnp.int32, (parts * LANES, width), 1) // HEADDIM
    return jnp.where(head == lane, 1.0, 0.0).astype(BF16)


def expand(value, matrix):
    return mm(jnp.concatenate(split3(value), axis=1), matrix)


def state_kernel(
    width, index_ref, z0, z1, d0, d1, rim_ref, taps_ref, bias_ref, dtb_ref, rate_ref,
    xc_ref, cum_ref, cumfull_ref, step_ref, local_ref, final_ref, log_ref, send_ref,
    ext, state, offset, matrix,
):
    c = pl.program_id(0)

    @pl.when(c == 0)
    def _():
        ext[0:8, :] = rim_ref[...]
        state[...] = jnp.zeros_like(state)
        offset[...] = jnp.zeros_like(offset)
        matrix[...] = expand_matrix(3, width)

    ext[8 : 8 + PIECE, :] = z0[...]
    ext[8 + PIECE : 8 + 2 * PIECE, :] = z1[...]
    taps = taps_ref.shape[0]
    acc = bias_ref[...] + taps_ref[taps - 1 : taps, :] * ext[8 : 8 + CHUNK, :]
    for k in range(taps - 1):
        start = 8 - (taps - 1) + k
        acc = acc + taps_ref[k : k + 1, :] * ext[start : start + CHUNK, :]
    xc = silu(acc)
    xc_ref[...] = xc
    ext[0:8, :] = ext[CHUNK : CHUNK + 8, :]

    raw = jnp.concatenate([d0[...], d1[...]], axis=0) + dtb_ref[...]
    step = jnp.maximum(raw, 0.0) + jnp.log1p(jnp.exp(-jnp.abs(raw)))
    decay = -rate_ref[...] * step
    rows = lax.broadcasted_iota(jnp.int32, (CHUNK, CHUNK), 0)
    cols = lax.broadcasted_iota(jnp.int32, (CHUNK, CHUNK), 1)
    lower = jnp.where(rows >= cols, 1.0, 0.0).astype(BF16)
    sums = mm(lower, jnp.concatenate(split3(decay), axis=1))
    cum = sums[:, :LANES] + sums[:, LANES : 2 * LANES] + sums[:, 2 * LANES :]
    total = cum[CHUNK - 1 : CHUNK, :]
    before = offset[0:1, :]
    cum_ref[...] = cum
    cumfull_ref[...] = cum + before
    step_ref[...] = step
    offset[...] = jnp.broadcast_to(before + total, offset.shape)

    carried = expand(jnp.exp(total - cum) * step, matrix[...])
    xs_hi, xs_lo = split2(carried * xc[:, :width])
    b_hi, b_lo = split2(xc[:, width : width + STATE].T)
    update = mm(
        jnp.concatenate([b_hi, b_lo, b_hi], axis=1),
        jnp.concatenate([xs_hi, xs_hi, xs_lo], axis=0),
    )
    keep = expand(jnp.broadcast_to(jnp.exp(total), (8, LANES)), matrix[...])
    old = state[...]
    local_ref[0] = old.astype(BF16)
    new = keep[0:1, :] * old + update
    state[...] = new

    @pl.when(c == pl.num_programs(0) - 1)
    def _():
        final_ref[...] = new
        hi, mid, lo = split3(offset[...])
        one = matrix[0:LANES, :]
        e_hi, e_mid, e_lo = mm(hi, one), mm(mid, one), mm(lo, one)
        log_ref[...] = e_hi + e_mid + e_lo
        row = lax.broadcasted_iota(jnp.int32, e_hi.shape, 0)
        packed = jnp.where(row == 0, e_hi, jnp.where(row == 1, e_mid, jnp.where(row == 2, e_lo, 0.0)))
        send_ref[...] = jnp.concatenate([new, packed], axis=0).astype(BF16)


def piece_index(block, q, e, per):
    r = block ^ e
    far = 2 * per + ((r // 2 - 1) * per + q) * 2 + r % 2
    return jnp.where(r < 2, r * per + q, far)


def piece_map(k, chunks_per_block, per):
    def index(c, index_ref):
        block = c // chunks_per_block
        q = (c % chunks_per_block) * (CHUNK // PIECE) + k
        return (piece_index(block, q, index_ref[0], per), 0)

    return index


def run_states(index, z, dt, rim, taps, bias, dtb, rate, width, local):
    total, wide = z.shape
    chunks = total // CHUNK
    per = local // PIECE
    cpb = local // CHUNK
    const = lambda c, i: (0, 0)
    row = lambda c, i: (c, 0)
    return pl.pallas_call(
        functools.partial(state_kernel, width),
        out_shape=(
            jax.ShapeDtypeStruct((total, wide), F32),
            jax.ShapeDtypeStruct((total, LANES), F32),
            jax.ShapeDtypeStruct((total, LANES), F32),
            jax.ShapeDtypeStruct((total, LANES), F32),
            jax.ShapeDtypeStruct((chunks, STATE, width), BF16),
            jax.ShapeDtypeStruct((STATE, width), F32),
            jax.ShapeDtypeStruct((8, width), F32),
            jax.ShapeDtypeStruct((STATE + 8, width), BF16),
        ),
        grid_spec=pltpu.PrefetchScalarGridSpec(
            num_scalar_prefetch=1,
            grid=(chunks,),
            in_specs=[
                pl.BlockSpec((PIECE, wide), piece_map(0, cpb, per)),
                pl.BlockSpec((PIECE, wide), piece_map(1, cpb, per)),
                pl.BlockSpec((PIECE, LANES), piece_map(0, cpb, per)),
                pl.BlockSpec((PIECE, LANES), piece_map(1, cpb, per)),
                pl.BlockSpec(rim.shape, const),
                pl.BlockSpec(taps.shape, const),
                pl.BlockSpec(bias.shape, const),
                pl.BlockSpec(dtb.shape, const),
                pl.BlockSpec(rate.shape, const),
            ],
            out_specs=(
                pl.BlockSpec((CHUNK, wide), row),
                pl.BlockSpec((CHUNK, LANES), row),
                pl.BlockSpec((CHUNK, LANES), row),
                pl.BlockSpec((CHUNK, LANES), row),
                pl.BlockSpec((1, STATE, width), lambda c, i: (c, 0, 0)),
                pl.BlockSpec((STATE, width), const),
                pl.BlockSpec((8, width), const),
                pl.BlockSpec((STATE + 8, width), const),
            ),
            scratch_shapes=[
                pltpu.VMEM((CHUNK + 8, wide), F32),
                pltpu.VMEM((STATE, width), F32),
                pltpu.VMEM((8, LANES), F32),
                pltpu.VMEM((3 * LANES, width), BF16),
            ],
        ),
        cost_estimate=pl.CostEstimate(
            flops=2 * total * width * 1000, transcendentals=total * wide, bytes_accessed=12 * total * wide
        ),
        compiler_params=pltpu.CompilerParams(dimension_semantics=("arbitrary",)),
        name="run_states",
    )(index, z, z, dt, dt, rim, taps, bias, dtb, rate)


def output_kernel(
    width, index_ref, xc_ref, cum_ref, cumfull_ref, step_ref, local_ref, g0, g1, direct_ref,
    a_ref, b_ref, c_ref, matrix,
):
    @pl.when(pl.program_id(0) == 0)
    def _():
        matrix[...] = expand_matrix(3, width)

    x = xc_ref[:, :width]
    bmap = xc_ref[:, width : width + STATE]
    cmap = xc_ref[:, width + STATE :]
    cum = cum_ref[...]
    b_hi, b_lo = split2(bmap)
    c_hi, c_lo = split2(cmap)
    c_ref[...] = c_hi
    gram = mm_nt(
        jnp.concatenate([c_hi, c_lo, c_hi], axis=1), jnp.concatenate([b_hi, b_hi, b_lo], axis=1)
    )
    cum_t = cum.T
    step_t = step_ref[...].T
    rows = lax.broadcasted_iota(jnp.int32, (CHUNK, CHUNK), 0)
    cols = lax.broadcasted_iota(jnp.int32, (CHUNK, CHUNK), 1)
    causal = rows >= cols
    left = lax.broadcasted_iota(jnp.int32, (CHUNK, 2 * HEADDIM), 1) < HEADDIM
    parts = []
    for p in range(width // (2 * HEADDIM)):
        ws = []
        for h in (2 * p, 2 * p + 1):
            differ = jnp.where(causal, cum[:, h : h + 1] - cum_t[h : h + 1, :], -jnp.inf)
            ws.append((jnp.exp(differ) * (gram * step_t[h : h + 1, :])).astype(BF16))
        xp = x[:, p * 2 * HEADDIM : (p + 1) * 2 * HEADDIM]
        xb = jnp.concatenate([jnp.where(left, xp, 0.0), jnp.where(left, 0.0, xp)], axis=0)
        parts.append(mm(jnp.concatenate(ws, axis=1), xb.astype(BF16)))
    inside = jnp.concatenate(parts, axis=1)
    y = inside + expand(jnp.exp(cum), matrix[...]) * mm(c_hi, local_ref[0]) + direct_ref[...] * x
    gate = silu(jnp.concatenate([g0[...], g1[...]], axis=0))
    a_ref[...] = y * gate
    b_ref[...] = expand(jnp.exp(cumfull_ref[...]), matrix[...]) * gate


def run_outputs(index, xc, cum, cumfull, step, local_states, gate, direct, local):
    total, wide = xc.shape
    width = gate.shape[1]
    chunks = total // CHUNK
    per = local // PIECE
    cpb = local // CHUNK
    const = lambda c, i: (0, 0)
    row = lambda c, i: (c, 0)
    return pl.pallas_call(
        functools.partial(output_kernel, width),
        out_shape=(
            jax.ShapeDtypeStruct((total, width), F32),
            jax.ShapeDtypeStruct((total, width), F32),
            jax.ShapeDtypeStruct((total, STATE), BF16),
        ),
        grid_spec=pltpu.PrefetchScalarGridSpec(
            num_scalar_prefetch=1,
            grid=(chunks,),
            in_specs=[
                pl.BlockSpec((CHUNK, wide), row),
                pl.BlockSpec((CHUNK, LANES), row),
                pl.BlockSpec((CHUNK, LANES), row),
                pl.BlockSpec((CHUNK, LANES), row),
                pl.BlockSpec((1, STATE, width), lambda c, i: (c, 0, 0)),
                pl.BlockSpec((PIECE, width), piece_map(0, cpb, per)),
                pl.BlockSpec((PIECE, width), piece_map(1, cpb, per)),
                pl.BlockSpec(direct.shape, const),
            ],
            out_specs=(
                pl.BlockSpec((CHUNK, width), row),
                pl.BlockSpec((CHUNK, width), row),
                pl.BlockSpec((CHUNK, STATE), row),
            ),
            scratch_shapes=[pltpu.VMEM((3 * LANES, width), BF16)],
        ),
        cost_estimate=pl.CostEstimate(
            flops=2 * total * width * 1500, transcendentals=total * width * 4, bytes_accessed=16 * total * width
        ),
        compiler_params=pltpu.CompilerParams(dimension_semantics=("arbitrary",)),
        name="run_outputs",
    )(index, xc, cum, cumfull, step, local_states, gate, gate, direct)


def join_kernel(a_ref, b_ref, c_ref, s_ref, o_ref, ss_ref):
    gated = a_ref[...] + b_ref[...] * mm(c_ref[...], s_ref[...])
    o_ref[...] = gated
    hi, lo = split2(gated * gated)
    ones = jnp.ones((8, 2 * hi.shape[1]), BF16)
    ss_ref[...] = mm_nt(ones, jnp.concatenate([hi, lo], axis=1))


def join(a, b, c, entering):
    total, width = a.shape
    rows = 256
    row = lambda i: (i, 0)
    return pl.pallas_call(
        join_kernel,
        out_shape=(jax.ShapeDtypeStruct((total, width), F32), jax.ShapeDtypeStruct((8, total), F32)),
        grid=(total // rows,),
        in_specs=[
            pl.BlockSpec((rows, width), row),
            pl.BlockSpec((rows, width), row),
            pl.BlockSpec((rows, STATE), row),
            pl.BlockSpec(entering.shape, lambda i: (0, 0)),
        ],
        out_specs=(pl.BlockSpec((rows, width), row), pl.BlockSpec((8, rows), lambda i: (0, i))),
        compiler_params=pltpu.CompilerParams(dimension_semantics=("arbitrary",)),
        name="join",
    )(a, b, c, entering)


def norm_kernel(inner_width, g_ref, ss_ref, gain_ref, o_ref):
    scale = lax.rsqrt(ss_ref[0:1, :] / inner_width + 1e-05)
    width = g_ref.shape[1]
    for part in range(g_ref.shape[0] // LANES):
        rows = slice(part * LANES, (part + 1) * LANES)
        column = jnp.broadcast_to(scale[:, rows], (LANES, LANES)).T
        for lane in range(width // LANES):
            lanes = slice(lane * LANES, (lane + 1) * LANES)
            o_ref[rows, lanes] = (g_ref[rows, lanes] * column * gain_ref[:, lanes]).astype(BF16)


def norm(gated, squares, gain, inner_width):
    total, width = gated.shape
    rows = 256
    return pl.pallas_call(
        functools.partial(norm_kernel, inner_width),
        out_shape=jax.ShapeDtypeStruct((total, width), BF16),
        grid=(total // rows,),
        in_specs=[
            pl.BlockSpec((rows, width), lambda i: (i, 0)),
            pl.BlockSpec((squares.shape[0], rows), lambda i: (0, i)),
            pl.BlockSpec(gain.shape, lambda i: (0, 0)),
        ],
        out_specs=pl.BlockSpec((rows, width), lambda i: (i, 0)),
        compiler_params=pltpu.CompilerParams(dimension_semantics=("arbitrary",)),
        name="norm",
    )(gated, squares, gain)


def entering_state(final, log_total, send):
    n = lax.axis_size("seq")
    place = lax.axis_index("seq")
    group, group_log = final, log_total[0:1]
    prefix = jnp.zeros_like(final)
    prefix_log = jnp.zeros_like(group_log)
    d = 1
    while d < n:
        got = swap(send, "seq", d).astype(F32)
        other = got[:STATE]
        other_log = got[STATE : STATE + 1] + got[STATE + 1 : STATE + 2] + got[STATE + 2 : STATE + 3]
        upper = (place & d) != 0
        prefix = jnp.where(upper, prefix + jnp.exp(prefix_log) * other, prefix)
        prefix_log = jnp.where(upper, prefix_log + other_log, prefix_log)
        late = jnp.where(upper, group, other)
        early = jnp.where(upper, other, group)
        late_log = jnp.where(upper, group_log, other_log)
        group = late + jnp.exp(late_log) * early
        group_log = group_log + other_log
        d *= 2
        if d < n:
            hi = group_log.astype(BF16).astype(F32)
            mid = (group_log - hi).astype(BF16).astype(F32)
            lo = group_log - hi - mid
            pad = jnp.zeros((5, group.shape[1]), F32)
            send = jnp.concatenate([group, hi, mid, lo, pad], axis=0).astype(BF16)
    return prefix.astype(BF16)


def body(
    tokens,
    routes,
    gate_inner_weight,
    state_map_weight,
    step_size_weight,
    adapter_down_weight,
    adapter_up_weight,
    inner_conv_taps,
    state_map_taps,
    inner_conv_bias,
    state_map_conv_bias,
    step_size_bias,
    head_decay_rate,
    direct_head_scale,
    gated_norm_scale,
):
    n = lax.axis_size("exp")
    local, features = tokens.shape
    total = local * n
    width = gate_inner_weight.shape[2]
    heads = head_decay_rate.shape[0]
    experts = adapter_up_weight.shape[0]
    cols = experts // n
    rank = 8
    e = lax.axis_index("exp")
    index = jnp.full((1,), e, jnp.int32)
    per = local // PIECE

    far = {}
    for k in range(2, n, 2):
        for q in reversed(range(per)):
            far[k, q] = swap(tokens[q * PIECE : (q + 1) * PIECE], "exp", k)
    sibling = swap(tokens, "exp", 1)
    route_row = routes.reshape(1, local)
    route_rel = {0: route_row}
    for k in range(1, n):
        route_rel[k] = swap(route_row, "exp", k)
    down_t = adapter_down_weight.T
    down_rel = {0: down_t, 1: swap(down_t, "exp", 1)}
    for k in range(2, n, 2):
        down_rel[k] = swap(down_t, "exp", k)
        down_rel[k + 1] = swap(down_rel[k], "exp", 1)
    dt_t = jnp.pad(step_size_weight.T, ((0, 16 - heads), (0, 0)))
    wsm = jnp.concatenate([down_rel[k] for k in range(n)] + [dt_t], axis=0)
    wgate = gate_inner_weight[:, 0, :]
    wbig = jnp.concatenate([gate_inner_weight[:, 1, :], state_map_weight], axis=1)
    up3 = adapter_up_weight.reshape(n, cols, 2, width)
    up_rel = jnp.concatenate(
        [lax.dynamic_index_in_dim(up3, e ^ k, 0, keepdims=False) for k in range(n)], axis=0
    )
    up_gate, up_inner = up_rel[:, 0, :], up_rel[:, 1, :]

    call = functools.partial(project, index, wsm=wsm, wbig=wbig, up=up_inner, rank=rank, total=total)
    route_near = jnp.concatenate([route_rel[0], route_rel[1]], axis=0)
    buffers = call([tokens, sibling], route_near, row_block=0, buffers=None)
    xs = [tokens, sibling]
    far_rows = {}
    for k in range(2, n, 2):
        for q in reversed(range(per)):
            mine = far[k, q]
            other = swap(mine, "exp", 1)
            lanes = slice(q * PIECE, (q + 1) * PIECE)
            route = jnp.concatenate([route_rel[k][:, lanes], route_rel[k + 1][:, lanes]], axis=0)
            place = (2 * per + ((k // 2 - 1) * per + q) * 2) // 2
            buffers = call([mine, other], route, row_block=place, buffers=buffers)
            far_rows[k, q] = (mine, other)
    for k in range(2, n, 2):
        for q in range(per):
            xs.extend(far_rows[k, q])
    z, dt, lift = buffers

    last = n - 1
    tail = piece_index(jnp.int32(last), per - 1, e, per) * PIECE + PIECE - 8
    rim = lax.ppermute(
        lax.dynamic_slice(z, (tail, 0), (8, z.shape[1])),
        "seq",
        [(i, (i + 1) % lax.axis_size("seq")) for i in range(lax.axis_size("seq"))],
    )
    rim = jnp.where(lax.axis_index("seq") == 0, 0.0, rim)

    taps = jnp.concatenate([inner_conv_taps, state_map_taps], axis=1)
    bias = jnp.concatenate([inner_conv_bias, state_map_conv_bias])[None, :]
    pad_heads = lambda v: jnp.pad(v, (0, LANES - heads))[None, :]
    xc, cum, cumfull, step, states, final, log_total, send = run_states(
        index, z, dt, rim, taps, bias, pad_heads(step_size_bias), pad_heads(head_decay_rate), width, local
    )
    entering = entering_state(final, log_total, send)
    gate = gate_project(xs, lift, wgate, up_gate)
    direct = jnp.repeat(direct_head_scale, HEADDIM)[None, :]
    a, b, c = run_outputs(index, xc, cum, cumfull, step, states, gate, direct, local)
    gated, squares = join(a, b, c, entering)
    squares = squares[0:1]
    d = 1
    while d < n:
        squares = squares + swap(squares, "exp", d)
        d *= 2
    return norm(gated, squares, gated_norm_scale[None, :], width * n)


def solution(mesh):
    in_specs = (
        P(("seq", "exp"), None),
        P(("seq", "exp"), None),
        P(None, None, "exp"),
        P(),
        P(None, "exp"),
        P(None, "exp"),
        P(None, None, "exp"),
        P(None, "exp"),
        P(),
        P("exp"),
        P(),
        P("exp"),
        P("exp"),
        P("exp"),
        P("exp"),
    )
    out_specs = P("seq", "exp")
    return jax.shard_map(body, mesh=mesh, in_specs=in_specs, out_specs=out_specs, check_vma=False)
```

```python
import functools

import jax
import jax.numpy as jnp
from jax import lax
from jax.experimental import pallas as pl
from jax.experimental.pallas import tpu as pltpu
from jax.sharding import PartitionSpec as P


STATE = 128
HEADDIM = 64
CHUNK = 128
LANES = 128
F32 = jnp.float32
BF16 = jnp.bfloat16


def swap(block, axis, mask):
    return lax.ppermute(block, axis, [(i, i ^ mask) for i in range(lax.axis_size(axis))])


def split3(value):
    hi = value.astype(BF16)
    rest = value - hi.astype(F32)
    mid = rest.astype(BF16)
    lo = (rest - mid.astype(F32)).astype(BF16)
    return hi, mid, lo


def split2(value):
    hi = value.astype(BF16)
    return hi, (value - hi.astype(F32)).astype(BF16)


def mm(a, b):
    return jnp.dot(a, b, preferred_element_type=F32)


def mm_nt(a, b):
    return lax.dot_general(a, b, (((1,), (1,)), ((), ())), preferred_element_type=F32)


def silu(v):
    return v / (1.0 + jnp.exp(-v))


def route_mask(e, route_row, experts_dev, rank):
    column = lax.broadcasted_iota(jnp.int32, (LANES, route_row.shape[1]), 0)
    per_dev = experts_dev * rank
    expert = ((column // per_dev) ^ e) * experts_dev + (column % per_dev) // rank
    return jnp.where(expert.astype(F32) == route_row, 1.0, 0.0)


def once(shape, const):
    return pl.BlockSpec(shape, const, pipeline_mode=pl.Buffered(1))


def up_specs(up, devices, tn, column):
    cols = up.shape[0] // devices
    return [
        pl.BlockSpec((cols, tn), lambda t, i, r=r: (i[0] ^ r, column(t))) for r in range(devices)
    ]


def project_kernel(cfg, index_ref, *refs):
    counts, route_from, devices, cols, rank, inner_tiles, aliased, pair = cfg
    x_refs, refs = refs[: len(counts)], refs[len(counts):]
    d_refs, refs = refs[:devices], refs[devices:]
    dt_ref, w_ref, wbc_ref = refs[:3]
    up_refs, refs = refs[3 : 3 + devices], refs[3 + devices:]
    z_ref, dto_ref, lift_ref, tail_ref, x_scr, w_scr = refs[aliased:]
    tile = pl.program_id(0)
    e = index_ref[0]

    @pl.when(tile == 0)
    def _():
        at = 0
        for x_ref, n in zip(x_refs, counts):
            x_scr[at : at + n, :] = x_ref[...]
            at += n
        w_scr[LANES:, :] = jnp.zeros((w_scr.shape[0] - LANES, w_scr.shape[1]), BF16)
        w_scr[LANES : LANES + dt_ref.shape[0], :] = dt_ref[...]
        for r in range(devices):
            w_scr[r * cols : (r + 1) * cols, :] = d_refs[r][0:cols, :]
        small = mm_nt(x_scr[...], w_scr[...])
        masks = []
        for r, first, n in route_from:
            for lane in range(first, first + n, LANES):
                row = d_refs[r][cols : cols + 1, lane : lane + LANES].astype(F32)
                masks.append(route_mask(e, row, cols // rank, rank).T)
        mask = jnp.concatenate(masks, axis=0)
        lift_ref[...] = jnp.where(mask > 0.5, small[:, :LANES], 0.0).astype(BF16)
        pad = jnp.zeros((small.shape[0], 2 * LANES - small.shape[1]), F32)
        dto_ref[...] = jnp.concatenate([small[:, LANES:], pad], axis=1)

    @pl.when(tile < inner_tiles)
    def _():
        up = jnp.concatenate([r[...] for r in up_refs], axis=0)
        z_ref[...] = mm(x_scr[...], w_ref[...]) + mm(lift_ref[...], up)

    @pl.when(tile >= inner_tiles)
    def _():
        z_ref[...] = mm(x_scr[...], wbc_ref[...])

    half = counts[0]
    start = ((devices - 1) ^ e) % 2 * half + half - 8
    tail = z_ref[pl.ds(pl.multiple_of(start, 8), 8), :]
    if aliased == 4:
        old_ref = refs[3]
        tail = jnp.where(((devices - 1) ^ e) // 2 == pair, tail, old_ref[...])
    tail_ref[...] = tail


def project(index, xs, route_from, downs, dt_t, wz, wbc, up, rank, total, row_block, buffers, tail, pair):
    counts = tuple(x.shape[0] for x in xs)
    rows = sum(counts)
    features = wz.shape[0]
    inner = up.shape[1] // 2
    width = inner + wbc.shape[1]
    tn = 256 if inner % 256 == 0 and width % 256 == 0 else 128
    inner_tiles = inner // tn
    devices = len(downs)
    const = lambda t, i: (0, 0)
    in_specs = (
        [once(x.shape, const) for x in xs]
        + [once(d.shape, const) for d in downs]
        + [
            once(dt_t.shape, const),
            pl.BlockSpec((features, tn), lambda t, i: (0, inner_tiles + jnp.minimum(t, inner_tiles - 1))),
            pl.BlockSpec((features, tn), lambda t, i: (0, jnp.maximum(t - inner_tiles, 0))),
        ]
        + up_specs(up, devices, tn, lambda t: inner_tiles + jnp.minimum(t, inner_tiles - 1))
    )
    args = list(xs) + list(downs) + [dt_t, wz, wbc] + [up] * devices
    aliases = {}
    if buffers is not None:
        for n, buffer in enumerate(buffers):
            aliases[1 + len(args)] = n
            args.append(buffer)
            in_specs.append(pl.BlockSpec(memory_space=pl.ANY))
    extra = len(aliases)
    if tail is not None:
        args.append(tail)
        in_specs.append(pl.BlockSpec((8, tn), lambda t, i: (0, t)))
        extra += 1
    cfg = (counts, route_from, devices, LANES // devices, rank, inner_tiles, extra, pair)
    return pl.pallas_call(
        functools.partial(project_kernel, cfg),
        out_shape=(
            jax.ShapeDtypeStruct((total, width), F32),
            jax.ShapeDtypeStruct((total, LANES), F32),
            jax.ShapeDtypeStruct((total, LANES), BF16),
            jax.ShapeDtypeStruct((8, width), F32),
        ),
        grid_spec=pltpu.PrefetchScalarGridSpec(
            num_scalar_prefetch=1,
            grid=(width // tn,),
            in_specs=in_specs,
            out_specs=(
                pl.BlockSpec((rows, tn), lambda t, i: (row_block, t)),
                pl.BlockSpec((rows, LANES), lambda t, i: (row_block, 0)),
                pl.BlockSpec((rows, LANES), lambda t, i: (row_block, 0)),
                pl.BlockSpec((8, tn), lambda t, i: (0, t)),
            ),
            scratch_shapes=[
                pltpu.VMEM((rows, features), BF16),
                pltpu.VMEM((LANES + 16, features), BF16),
            ],
        ),
        input_output_aliases=aliases,
        cost_estimate=pl.CostEstimate(
            flops=2 * rows * features * (width + 256),
            transcendentals=0,
            bytes_accessed=2 * features * (width + rows) + 4 * rows * width,
        ),
        compiler_params=pltpu.CompilerParams(
            dimension_semantics=("arbitrary",), vmem_limit_bytes=16 << 20
        ),
        name="project",
    )(index, *args)


def gate_kernel(counts, devices, index_ref, *refs):
    x_refs, refs = refs[: len(counts)], refs[len(counts):]
    lift_ref, w_ref = refs[:2]
    up_refs = refs[2 : 2 + devices]
    g_ref, x_scr = refs[-2:]

    @pl.when(pl.program_id(0) == 0)
    def _():
        at = 0
        for x_ref, n in zip(x_refs, counts):
            x_scr[at : at + n, :] = x_ref[...]
            at += n

    up = jnp.concatenate([r[...] for r in up_refs], axis=0)
    g_ref[...] = mm(x_scr[...], w_ref[...]) + mm(lift_ref[...], up)


def gate_project(index, xs, lift, wz, up, devices, total, row_block, buffer):
    counts = tuple(x.shape[0] for x in xs)
    rows = sum(counts)
    features = wz.shape[0]
    width = up.shape[1] // 2
    tn = 256 if width % 256 == 0 else 128
    const = lambda t, i: (0, 0)
    in_specs = [once(x.shape, const) for x in xs] + [
        pl.BlockSpec((rows, lift.shape[1]), lambda t, i: (row_block, 0), pipeline_mode=pl.Buffered(1)),
        pl.BlockSpec((features, tn), lambda t, i: (0, t)),
    ]
    in_specs += up_specs(up, devices, tn, lambda t: t)
    args = list(xs) + [lift, wz] + [up] * devices
    aliases = {}
    if buffer is not None:
        aliases[1 + len(args)] = 0
        args.append(buffer)
        in_specs.append(pl.BlockSpec(memory_space=pl.ANY))
    return pl.pallas_call(
        functools.partial(gate_kernel, counts, devices),
        out_shape=jax.ShapeDtypeStruct((total, width), F32),
        grid_spec=pltpu.PrefetchScalarGridSpec(
            num_scalar_prefetch=1,
            grid=(width // tn,),
            in_specs=in_specs,
            out_specs=pl.BlockSpec((rows, tn), lambda t, i: (row_block, t)),
            scratch_shapes=[pltpu.VMEM((rows, features), BF16)],
        ),
        input_output_aliases=aliases,
        cost_estimate=pl.CostEstimate(
            flops=2 * rows * features * width,
            transcendentals=0,
            bytes_accessed=2 * features * (width + rows) + 4 * rows * width,
        ),
        compiler_params=pltpu.CompilerParams(
            dimension_semantics=("arbitrary",), vmem_limit_bytes=12 << 20
        ),
        name="gate_project",
    )(index, *args)


def spread(value, width):
    rows = value.shape[0]
    left = lax.broadcasted_iota(jnp.int32, (rows, LANES), 1) < HEADDIM
    parts = []
    for p in range(width // LANES):
        a = jnp.broadcast_to(value[:, 2 * p : 2 * p + 1], (rows, LANES))
        b = jnp.broadcast_to(value[:, 2 * p + 1 : 2 * p + 2], (rows, LANES))
        parts.append(jnp.where(left, a, b))
    return jnp.concatenate(parts, axis=1)


def pad_lanes(row):
    return jnp.concatenate([row, jnp.zeros((1, LANES - row.shape[1]), F32)], axis=1)


def state_kernel(
    width, index_ref, z_ref, d_ref, rim_ref, taps_ref, mtaps_ref, bias_ref, mbias_ref, dtb_ref, rate_ref,
    xc_ref, cum_ref, step_ref, before_ref, local_ref, final_ref, log_ref, send_ref, prefix_ref, plog_ref,
    ext, state, offset,
):
    c = pl.program_id(0)

    @pl.when(c == 0)
    def _():
        ext[0:8, :] = jnp.where(index_ref[1] == 0, 0.0, rim_ref[...])
        state[...] = jnp.zeros_like(state)
        offset[...] = jnp.zeros_like(offset)

    ext[8 : 8 + CHUNK, :] = z_ref[...]
    taps = taps_ref.shape[0]
    outs = []
    for tr, br, lanes in (
        (taps_ref, bias_ref, slice(0, width)),
        (mtaps_ref, mbias_ref, slice(width, width + 2 * STATE)),
    ):
        acc = br[...] + tr[taps - 1 : taps, :] * ext[8 : 8 + CHUNK, lanes]
        for k in range(taps - 1):
            start = 8 - (taps - 1) + k
            acc = acc + tr[k : k + 1, :] * ext[start : start + CHUNK, lanes]
        out = silu(acc)
        xc_ref[:, lanes] = out
        outs.append(out)
    x, maps = outs
    ext[0:8, :] = ext[CHUNK : CHUNK + 8, :]

    raw = d_ref[...] + pad_lanes(dtb_ref[...])
    step = jnp.maximum(raw, 0.0) + jnp.log1p(jnp.exp(-jnp.abs(raw)))
    decay = -pad_lanes(rate_ref[...]) * step
    rows = lax.broadcasted_iota(jnp.int32, (CHUNK, CHUNK), 0)
    cols = lax.broadcasted_iota(jnp.int32, (CHUNK, CHUNK), 1)
    lower = jnp.where(rows >= cols, 1.0, 0.0).astype(BF16)
    sums = mm(lower, jnp.concatenate(split3(decay), axis=1))
    cum = sums[:, :LANES] + sums[:, LANES : 2 * LANES] + sums[:, 2 * LANES :]
    total = cum[CHUNK - 1 : CHUNK, :]
    before = offset[0:1, :]
    cum_ref[...] = cum
    step_ref[...] = step
    before_ref[0] = offset[...]
    after = jnp.broadcast_to(before + total, offset.shape)
    offset[...] = after

    xs = (spread(jnp.exp(total - cum) * step, width) * x).astype(BF16)
    b_hi, b_lo = split2(maps[:, :STATE].T)
    update = mm(jnp.concatenate([b_hi, b_lo], axis=1), jnp.concatenate([xs, xs], axis=0))
    old = state[...]
    local_ref[0] = old.astype(BF16)
    new = spread(jnp.broadcast_to(jnp.exp(total), (8, LANES)), width)[0:1, :] * old + update
    state[...] = new

    @pl.when(c == pl.num_programs(0) - 1)
    def _():
        final_ref[...] = new
        wide = spread(after, width)
        log_ref[...] = wide
        send_ref[0:STATE, :] = new.astype(BF16)
        send_ref[STATE : STATE + 8, :] = pack_logs(wide)
        prefix_ref[...] = jnp.zeros_like(new)
        plog_ref[...] = jnp.zeros_like(wide)


def piece_index(block, q, e, per):
    r = block ^ e
    far = 2 * per + ((r // 2 - 1) * per + q) * 2 + r % 2
    return jnp.where(r < 2, r * per + q, far)


def piece_map(per):
    def index(c, index_ref):
        return (piece_index(c // per, c % per, index_ref[0], per), 0)

    return index


def run_states(index, z, dt, rim, params, width, local):
    total, wide = z.shape
    chunks = total // CHUNK
    per = local // CHUNK
    const = lambda c, i: (0, 0)
    row = lambda c, i: (c, 0)
    deep = lambda c, i: (c, 0, 0)
    return pl.pallas_call(
        functools.partial(state_kernel, width),
        out_shape=(
            jax.ShapeDtypeStruct((total, wide), F32),
            jax.ShapeDtypeStruct((total, LANES), F32),
            jax.ShapeDtypeStruct((total, LANES), F32),
            jax.ShapeDtypeStruct((chunks, 8, LANES), F32),
            jax.ShapeDtypeStruct((chunks, STATE, width), BF16),
            jax.ShapeDtypeStruct((STATE, width), F32),
            jax.ShapeDtypeStruct((8, width), F32),
            jax.ShapeDtypeStruct((STATE + 8, width), BF16),
            jax.ShapeDtypeStruct((STATE, width), F32),
            jax.ShapeDtypeStruct((8, width), F32),
        ),
        grid_spec=pltpu.PrefetchScalarGridSpec(
            num_scalar_prefetch=1,
            grid=(chunks,),
            in_specs=[
                pl.BlockSpec((CHUNK, wide), piece_map(per)),
                pl.BlockSpec((CHUNK, LANES), piece_map(per)),
                pl.BlockSpec(rim.shape, const),
            ]
            + [pl.BlockSpec(p.shape, const) for p in params],
            out_specs=(
                pl.BlockSpec((CHUNK, wide), row),
                pl.BlockSpec((CHUNK, LANES), row),
                pl.BlockSpec((CHUNK, LANES), row),
                pl.BlockSpec((1, 8, LANES), deep),
                pl.BlockSpec((1, STATE, width), deep),
                pl.BlockSpec((STATE, width), const),
                pl.BlockSpec((8, width), const),
                pl.BlockSpec((STATE + 8, width), const),
                pl.BlockSpec((STATE, width), const),
                pl.BlockSpec((8, width), const),
            ),
            scratch_shapes=[
                pltpu.VMEM((CHUNK + 8, wide), F32),
                pltpu.VMEM((STATE, width), F32),
                pltpu.VMEM((8, LANES), F32),
            ],
        ),
        cost_estimate=pl.CostEstimate(
            flops=2 * total * width * 1000, transcendentals=total * wide, bytes_accessed=12 * total * wide
        ),
        compiler_params=pltpu.CompilerParams(
            dimension_semantics=("arbitrary",), vmem_limit_bytes=12 << 20
        ),
        name="run_states",
    )(index, z, dt, rim, *params)


def output_kernel(
    width, index_ref, xc_ref, cum_ref, step_ref, before_ref, local_ref, g_ref, direct_ref,
    a_ref, b_ref, c_ref,
):
    bmap = xc_ref[:, width : width + STATE]
    cmap = xc_ref[:, width + STATE :]
    cum = cum_ref[...]
    b_hi, b_lo = split2(bmap)
    c_hi, c_lo = split2(cmap)
    c_ref[...] = c_hi
    gram = mm_nt(jnp.concatenate([c_hi, c_lo], axis=1), jnp.concatenate([b_hi, b_hi], axis=1))
    gram = gram + mm_nt(c_hi, b_lo)
    cum_t = cum.T
    step_t = step_ref[...].T
    rows = lax.broadcasted_iota(jnp.int32, (CHUNK, CHUNK), 0)
    cols = lax.broadcasted_iota(jnp.int32, (CHUNK, CHUNK), 1)
    causal = rows >= cols
    left = cols < HEADDIM
    direct = pad_lanes(direct_ref[...])
    for p in range(width // LANES):
        lanes = slice(p * LANES, (p + 1) * LANES)
        ws, cs = [], []
        for h in (2 * p, 2 * p + 1):
            column = jnp.broadcast_to(cum[:, h : h + 1], (CHUNK, CHUNK))
            differ = jnp.where(causal, column - cum_t[h : h + 1, :], -jnp.inf)
            ws.append((jnp.exp(differ) * (gram * step_t[h : h + 1, :])).astype(BF16))
            cs.append(column)
        x = xc_ref[:, lanes]
        xb = jnp.concatenate([jnp.where(left, x, 0.0), jnp.where(left, 0.0, x)], axis=0)
        both = lambda v: jnp.where(
            left[0:1, :],
            jnp.broadcast_to(v[:, 2 * p : 2 * p + 1], (1, LANES)),
            jnp.broadcast_to(v[:, 2 * p + 1 : 2 * p + 2], (1, LANES)),
        )
        inside = mm(jnp.concatenate(ws, axis=1), xb.astype(BF16))
        fade = jnp.exp(jnp.where(left, cs[0], cs[1]))
        y = inside + fade * mm(c_hi, local_ref[0, :, lanes]) + both(direct) * x
        gate = silu(g_ref[:, lanes])
        a_ref[:, lanes] = y * gate
        b_ref[:, lanes] = fade * jnp.exp(both(before_ref[0, 0:1, :])) * gate


def run_outputs(index, xc, cum, step, before, local_states, gate, direct, local):
    total, wide = xc.shape
    width = gate.shape[1]
    chunks = total // CHUNK
    per = local // CHUNK
    const = lambda c, i: (0, 0)
    row = lambda c, i: (c, 0)
    deep = lambda c, i: (c, 0, 0)
    return pl.pallas_call(
        functools.partial(output_kernel, width),
        out_shape=(
            jax.ShapeDtypeStruct((total, width), F32),
            jax.ShapeDtypeStruct((total, width), F32),
            jax.ShapeDtypeStruct((total, STATE), BF16),
        ),
        grid_spec=pltpu.PrefetchScalarGridSpec(
            num_scalar_prefetch=1,
            grid=(chunks,),
            in_specs=[
                pl.BlockSpec((CHUNK, wide), row),
                pl.BlockSpec((CHUNK, LANES), row),
                pl.BlockSpec((CHUNK, LANES), row),
                pl.BlockSpec((1, 8, LANES), deep),
                pl.BlockSpec((1, STATE, width), deep),
                pl.BlockSpec((CHUNK, width), piece_map(per)),
                pl.BlockSpec(direct.shape, const),
            ],
            out_specs=(
                pl.BlockSpec((CHUNK, width), row),
                pl.BlockSpec((CHUNK, width), row),
                pl.BlockSpec((CHUNK, STATE), row),
            ),
        ),
        cost_estimate=pl.CostEstimate(
            flops=2 * total * width * 1500, transcendentals=total * width * 4, bytes_accessed=16 * total * width
        ),
        compiler_params=pltpu.CompilerParams(
            dimension_semantics=("arbitrary",), vmem_limit_bytes=12 << 20
        ),
        name="run_outputs",
    )(index, xc, cum, step, before, local_states, gate, direct)


def pack_logs(wide):
    hi, mid, lo = split3(wide)
    row = lax.broadcasted_iota(jnp.int32, wide.shape, 0)
    lo = jnp.where(row == 2, lo.astype(F32), 0.0)
    return jnp.where(row == 0, hi.astype(F32), jnp.where(row == 1, mid.astype(F32), lo)).astype(BF16)


def unpack(got_ref):
    other = got_ref[0:STATE, :].astype(F32)
    logs = got_ref[STATE : STATE + 8, :].astype(F32)
    log = logs[0:1, :] + logs[1:2, :] + logs[2:3, :]
    return other, log


def combine_kernel(
    d, index_ref, got_ref, group_ref, glog_ref, prefix_ref, plog_ref,
    send_ref, group_out, glog_out, prefix_out, plog_out,
):
    upper = (index_ref[1] & d) != 0
    other, other_log = unpack(got_ref)
    group, group_log = group_ref[...], glog_ref[0:1, :]
    prefix, prefix_log = prefix_ref[...], plog_ref[0:1, :]
    prefix_out[...] = jnp.where(upper, prefix + jnp.exp(prefix_log) * other, prefix)
    new_plog = jnp.where(upper, prefix_log + other_log, prefix_log)
    plog_out[...] = jnp.broadcast_to(new_plog, plog_out.shape)
    late = jnp.where(upper, group, other)
    early = jnp.where(upper, other, group)
    late_log = jnp.where(upper, group_log, other_log)
    new = late + jnp.exp(late_log) * early
    new_log = jnp.broadcast_to(group_log + other_log, glog_out.shape)
    group_out[...] = new
    glog_out[...] = new_log
    send_ref[0:STATE, :] = new.astype(BF16)
    send_ref[STATE : STATE + 8, :] = pack_logs(new_log)


def combine(index, d, got, group, glog, prefix, plog):
    state = jax.ShapeDtypeStruct(group.shape, F32)
    log = jax.ShapeDtypeStruct(glog.shape, F32)
    full = lambda x: pl.BlockSpec(x.shape, lambda i, s: (0, 0))
    outs = (jax.ShapeDtypeStruct(got.shape, BF16), state, log, state, log)
    return pl.pallas_call(
        functools.partial(combine_kernel, d),
        out_shape=outs,
        grid_spec=pltpu.PrefetchScalarGridSpec(
            num_scalar_prefetch=1,
            grid=(1,),
            in_specs=[full(x) for x in (got, group, glog, prefix, plog)],
            out_specs=tuple(full(x) for x in outs),
        ),
        compiler_params=pltpu.CompilerParams(vmem_limit_bytes=8 << 20),
        name="combine",
    )(index, got, group, glog, prefix, plog)


def join_kernel(d, index_ref, a_ref, b_ref, c_ref, got_ref, prefix_ref, plog_ref, o_ref, ss_ref, s_scr):
    @pl.when(pl.program_id(0) == 0)
    def _():
        other, _ = unpack(got_ref)
        prefix = prefix_ref[...]
        upper = (index_ref[1] & d) != 0
        entering = jnp.where(upper, prefix + jnp.exp(plog_ref[0:1, :]) * other, prefix)
        s_scr[...] = entering.astype(BF16)

    gated = a_ref[...] + b_ref[...] * mm(c_ref[...], s_scr[...])
    o_ref[...] = gated
    hi, lo = split2(gated * gated)
    ones = jnp.ones((8, 2 * hi.shape[1]), BF16)
    ss_ref[...] = mm_nt(ones, jnp.concatenate([hi, lo], axis=1))[0:1]


def join(index, d, a, b, c, got, prefix, plog):
    total, width = a.shape
    rows = 256
    row = lambda i, s: (i, 0)
    full = lambda x: pl.BlockSpec(x.shape, lambda i, s: (0, 0))
    return pl.pallas_call(
        functools.partial(join_kernel, d),
        out_shape=(jax.ShapeDtypeStruct((total, width), F32), jax.ShapeDtypeStruct((1, total), F32)),
        grid_spec=pltpu.PrefetchScalarGridSpec(
            num_scalar_prefetch=1,
            grid=(total // rows,),
            in_specs=[
                pl.BlockSpec((rows, width), row),
                pl.BlockSpec((rows, width), row),
                pl.BlockSpec((rows, STATE), row),
                full(got),
                full(prefix),
                full(plog),
            ],
            out_specs=(
                pl.BlockSpec((rows, width), row),
                pl.BlockSpec((1, rows), lambda i, s: (0, i)),
            ),
            scratch_shapes=[pltpu.VMEM((STATE, width), BF16)],
        ),
        compiler_params=pltpu.CompilerParams(
            dimension_semantics=("arbitrary",), vmem_limit_bytes=10 << 20
        ),
        name="join",
    )(index, a, b, c, got, prefix, plog)


def norm_kernel(inner_width, g_ref, mine_ref, other_ref, gain_ref, o_ref):
    scale = lax.rsqrt((mine_ref[...] + other_ref[...]) / inner_width + 1e-05)
    width = g_ref.shape[1]
    for part in range(g_ref.shape[0] // LANES):
        rows = slice(part * LANES, (part + 1) * LANES)
        column = jnp.broadcast_to(scale[:, rows], (LANES, LANES)).T
        for lane in range(width // LANES):
            lanes = slice(lane * LANES, (lane + 1) * LANES)
            o_ref[rows, lanes] = (g_ref[rows, lanes] * column * gain_ref[:, lanes]).astype(BF16)


def norm(gated, mine, other, gain, inner_width):
    total, width = gated.shape
    rows = 256
    return pl.pallas_call(
        functools.partial(norm_kernel, inner_width),
        out_shape=jax.ShapeDtypeStruct((total, width), BF16),
        grid=(total // rows,),
        in_specs=[
            pl.BlockSpec((rows, width), lambda i: (i, 0)),
            pl.BlockSpec((1, rows), lambda i: (0, i)),
            pl.BlockSpec((1, rows), lambda i: (0, i)),
            pl.BlockSpec(gain.shape, lambda i: (0, 0)),
        ],
        out_specs=pl.BlockSpec((rows, width), lambda i: (i, 0)),
        compiler_params=pltpu.CompilerParams(
            dimension_semantics=("arbitrary",), vmem_limit_bytes=8 << 20
        ),
        name="norm",
    )(gated, mine, other, gain)


def body(
    tokens,
    routes,
    gate_inner_weight,
    state_map_weight,
    step_size_weight,
    adapter_down_weight,
    adapter_up_weight,
    inner_conv_taps,
    state_map_taps,
    inner_conv_bias,
    state_map_conv_bias,
    step_size_bias,
    head_decay_rate,
    direct_head_scale,
    gated_norm_scale,
):
    n = lax.axis_size("exp")
    shards = lax.axis_size("seq")
    local, features = tokens.shape
    total = local * n
    width = gate_inner_weight.shape[2]
    experts = adapter_up_weight.shape[0]
    rank = 8
    e = lax.axis_index("exp")
    index = jnp.stack([e, lax.axis_index("seq")]).astype(jnp.int32)
    per = local // CHUNK

    route_row = jnp.pad(routes.reshape(1, local).astype(BF16), ((0, 0), (0, features - local)))
    down = {0: jnp.concatenate([adapter_down_weight.T, route_row], axis=0)}
    far = {}
    for k in range(2, n, 2):
        down[k] = swap(down[0], "exp", k)
    for k in range(2, n, 2):
        for q in reversed(range(per)):
            far[k, q] = swap(tokens[q * CHUNK : (q + 1) * CHUNK], "exp", k)
    sibling = swap(tokens, "exp", 1)
    for k in range(0, n, 2):
        down[k + 1] = swap(down[k], "exp", 1)
    downs = [down[k] for k in range(n)]
    wz = gate_inner_weight.reshape(features, 2 * width)
    up = adapter_up_weight.reshape(experts, 2 * width)
    call = functools.partial(
        project, index, downs=downs, dt_t=step_size_weight.T, wz=wz, wbc=state_map_weight,
        up=up, rank=rank, total=total,
    )
    *buffers, tail = call(
        [tokens, sibling], route_from=((0, 0, local), (1, 0, local)), row_block=0, buffers=None,
        tail=None, pair=0,
    )
    gate = gate_project(index, [tokens, sibling], buffers[2], wz, up, n, total, 0, None)
    far_rows = {}
    for k in range(2, n, 2):
        for q in reversed(range(per)):
            mine = far[k, q]
            other = swap(mine, "exp", 1)
            block = per + (k // 2 - 1) * per + q
            *buffers, new_tail = call(
                [mine, other],
                route_from=((k, q * CHUNK, CHUNK), (k + 1, q * CHUNK, CHUNK)),
                row_block=block,
                buffers=buffers,
                tail=tail if q == per - 1 else None,
                pair=k // 2,
            )
            if q == per - 1:
                tail = new_tail
            far_rows[k, q] = (mine, other)
        if k == n - 2:
            rim = lax.ppermute(tail, "seq", [(i, (i + 1) % shards) for i in range(shards)])
    z, dt, lift = buffers

    params = [
        inner_conv_taps, state_map_taps, inner_conv_bias[None, :], state_map_conv_bias[None, :],
        step_size_bias[None, :], head_decay_rate[None, :],
    ]
    xc, cum, step, before, states, group, glog, send, prefix, plog = run_states(
        index, z, dt, rim, params, width, local
    )
    d = 1
    while True:
        got = swap(send, "seq", d)
        if 2 * d >= shards:
            break
        send, group, glog, prefix, plog = combine(index, d, got, group, glog, prefix, plog)
        d *= 2
    for k in range(2, n, 2):
        xs = []
        for q in range(per):
            xs.extend(far_rows[k, q])
        gate = gate_project(index, xs, lift, wz, up, n, total, k // 2, gate)
    a, b, c = run_outputs(
        index, xc, cum, step, before, states, gate, direct_head_scale[None, :], local
    )
    gated, mine = join(index, d, a, b, c, got, prefix, plog)
    d = 1
    while 2 * d < n:
        mine = mine + swap(mine, "exp", d)
        d *= 2
    return norm(gated, mine, swap(mine, "exp", d), gated_norm_scale[None, :], width * n)


def solution(mesh):
    in_specs = (
        P(("seq", "exp"), None),
        P(("seq", "exp"), None),
        P(None, None, "exp"),
        P(),
        P(None, "exp"),
        P(None, "exp"),
        P(None, None, "exp"),
        P(None, "exp"),
        P(),
        P("exp"),
        P(),
        P("exp"),
        P("exp"),
        P("exp"),
        P("exp"),
    )
    out_specs = P("seq", "exp")

    return jax.shard_map(body, mesh=mesh, in_specs=in_specs, out_specs=out_specs, check_vma=False)
```

```python
import functools

import jax
import jax.numpy as jnp
from jax import lax
from jax.experimental import pallas as pl
from jax.experimental.pallas import tpu as pltpu
from jax.sharding import PartitionSpec as P


STATE = 128
HEADDIM = 64
CHUNK = 128
LANES = 128
F32 = jnp.float32
BF16 = jnp.bfloat16


def swap(block, axis, mask):
    return lax.ppermute(block, axis, [(i, i ^ mask) for i in range(lax.axis_size(axis))])


def split3(value):
    hi = value.astype(BF16)
    rest = value - hi.astype(F32)
    mid = rest.astype(BF16)
    lo = (rest - mid.astype(F32)).astype(BF16)
    return hi, mid, lo


def split2(value):
    hi = value.astype(BF16)
    return hi, (value - hi.astype(F32)).astype(BF16)


def mm(a, b):
    return jnp.dot(a, b, preferred_element_type=F32)


def mm_nt(a, b):
    return lax.dot_general(a, b, (((1,), (1,)), ((), ())), preferred_element_type=F32)


def silu(v):
    return v / (1.0 + jnp.exp(-v))


def route_mask(e, route_row, experts_dev, rank):
    column = lax.broadcasted_iota(jnp.int32, (LANES, route_row.shape[1]), 0)
    per_dev = experts_dev * rank
    expert = ((column // per_dev) ^ e) * experts_dev + (column % per_dev) // rank
    return jnp.where(expert.astype(F32) == route_row, 1.0, 0.0)


VMEM = pl.BlockSpec(memory_space=pltpu.VMEM)


def up_rows(up_ref, e, devices, lanes):
    cols = up_ref.shape[0] // devices
    return jnp.concatenate(
        [up_ref[pl.ds(pl.multiple_of((e ^ r) * cols, cols), cols), lanes] for r in range(devices)], axis=0
    )


def project_kernel(cfg, index_ref, *refs):
    counts, route_from, devices, cols, rank, aliased = cfg
    x_refs, refs = refs[: len(counts)], refs[len(counts):]
    d_refs, refs = refs[:devices], refs[devices:]
    dt_ref, w_ref, wbc_ref, up_ref = refs[:4]
    if aliased:
        z_ref, dto_ref, lift_ref, x_scr, w_scr = refs[4 + aliased:]
        lift_scr = lift_ref
    else:
        z_ref, dto_ref, lift_ref, tails_ref, rim_ref, x_scr, w_scr, lift_scr = refs[4:]
    e = index_ref[0]
    rows = sum(counts)

    at = 0
    for x_ref, n in zip(x_refs, counts):
        x_scr[at : at + n, :] = x_ref[...]
        at += n
    if not aliased:
        for r in range(devices):
            x_scr[at + 8 * r : at + 8 * r + 8, :] = d_refs[r][cols : cols + 8, :]
    w_scr[LANES:, :] = jnp.zeros((w_scr.shape[0] - LANES, w_scr.shape[1]), BF16)
    w_scr[LANES : LANES + dt_ref.shape[0], :] = dt_ref[...]
    for r in range(devices):
        w_scr[r * cols : (r + 1) * cols, :] = d_refs[r][0:cols, :]
    small = mm_nt(x_scr[...], w_scr[...])

    def mask_of(r, lane):
        row = d_refs[r][cols : cols + 1, lane : lane + LANES].astype(F32)
        return route_mask(e, row, cols // rank, rank).T

    masks = []
    for r, first, n in route_from:
        for lane in range(first, first + n, LANES):
            masks.append(mask_of(r, lane))
    if not aliased:
        last = route_from[0][1] + route_from[0][2] - LANES
        for r in range(devices):
            masks.append(mask_of(r, last)[LANES - 8 :, :])
    lift = jnp.where(jnp.concatenate(masks, axis=0) > 0.5, small[:, :LANES], 0.0).astype(BF16)
    lift_scr[...] = lift
    pad = jnp.zeros((rows, 2 * LANES - small.shape[1]), F32)
    dto_ref[...] = jnp.concatenate([small[:rows, LANES:], pad], axis=1)
    if not aliased:
        lift_ref[...] = lift[:rows]

    def put(lanes, value):
        z_ref[:, lanes] = value[:rows]
        if not aliased:
            tails_ref[:, lanes] = value[rows:]

    width = z_ref.shape[1]
    inner = up_ref.shape[1] // 2
    tn = 256 if inner % 256 == 0 else 128
    for at in range(0, inner, tn):
        lanes = slice(inner + at, inner + at + tn)
        up = up_rows(up_ref, e, devices, lanes)
        put(slice(at, at + tn), mm(x_scr[...], w_ref[:, lanes]) + mm(lift_scr[...], up))
    for at in range(0, width - inner, tn):
        put(slice(inner + at, inner + at + tn), mm(x_scr[...], wbc_ref[:, at : at + tn]))
    if not aliased:
        row = ((devices - 1) ^ e) * 8
        rim_ref[...] = tails_ref[pl.ds(pl.multiple_of(row, 8), 8), :]


def project(index, xs, route_from, downs, dt_t, wz, wbc, up, rank, total, row_block, buffers):
    counts = tuple(x.shape[0] for x in xs)
    rows = sum(counts)
    features = wz.shape[0]
    width = up.shape[1] // 2 + wbc.shape[1]
    devices = len(downs)
    args = list(xs) + list(downs) + [dt_t, wz, wbc, up]
    in_specs = [VMEM] * len(args)
    out_shape = [
        jax.ShapeDtypeStruct((total, width), F32),
        jax.ShapeDtypeStruct((total, LANES), F32),
        jax.ShapeDtypeStruct((total, LANES), BF16),
    ]
    out_specs = [
        pl.BlockSpec((rows, width), lambda t, i: (row_block, 0)),
        pl.BlockSpec((rows, LANES), lambda t, i: (row_block, 0)),
        pl.BlockSpec((rows, LANES), lambda t, i: (row_block, 0)),
    ]
    extra = 8 * devices if buffers is None else 0
    scratch = [
        pltpu.VMEM((rows + extra, features), BF16),
        pltpu.VMEM((LANES + 16, features), BF16),
    ]
    aliases = {}
    if buffers is None:
        out_shape += [jax.ShapeDtypeStruct((extra, width), F32), jax.ShapeDtypeStruct((8, width), F32)]
        out_specs += [
            pl.BlockSpec((extra, width), lambda t, i: (0, 0)),
            pl.BlockSpec((8, width), lambda t, i: (0, 0)),
        ]
        scratch.append(pltpu.VMEM((rows + extra, LANES), BF16))
    else:
        for n, buffer in enumerate(buffers):
            aliases[1 + len(args)] = n
            args.append(buffer)
            in_specs.append(pl.BlockSpec(memory_space=pl.ANY))
    cfg = (counts, route_from, devices, LANES // devices, rank, len(aliases))
    return pl.pallas_call(
        functools.partial(project_kernel, cfg),
        out_shape=tuple(out_shape),
        grid_spec=pltpu.PrefetchScalarGridSpec(
            num_scalar_prefetch=1,
            grid=(1,),
            in_specs=in_specs,
            out_specs=tuple(out_specs),
            scratch_shapes=scratch,
        ),
        input_output_aliases=aliases,
        cost_estimate=pl.CostEstimate(
            flops=2 * rows * features * (width + 256),
            transcendentals=0,
            bytes_accessed=2 * features * (width + rows) + 4 * rows * width,
        ),
        compiler_params=pltpu.CompilerParams(
            dimension_semantics=("arbitrary",), vmem_limit_bytes=16 << 20
        ),
        name="project",
    )(index, *args)


def gate_kernel(counts, devices, index_ref, *refs):
    x_refs, refs = refs[: len(counts)], refs[len(counts):]
    lift_ref, w_ref, up_ref = refs[:3]
    g_ref, x_scr = refs[-2:]
    at = 0
    for x_ref, n in zip(x_refs, counts):
        x_scr[at : at + n, :] = x_ref[...]
        at += n
    width = g_ref.shape[1]
    tn = 256 if width % 256 == 0 else 128
    for at in range(0, width, tn):
        lanes = slice(at, at + tn)
        up = up_rows(up_ref, index_ref[0], devices, lanes)
        g_ref[:, lanes] = mm(x_scr[...], w_ref[:, lanes]) + mm(lift_ref[...], up)


def gate_project(index, xs, lift, wz, up, devices, total, row_block, buffer):
    counts = tuple(x.shape[0] for x in xs)
    rows = sum(counts)
    features = wz.shape[0]
    width = up.shape[1] // 2
    block = lambda t, i: (row_block, 0)
    in_specs = [VMEM] * len(xs) + [pl.BlockSpec((rows, lift.shape[1]), block), VMEM, VMEM]
    args = list(xs) + [lift, wz, up]
    aliases = {}
    if buffer is not None:
        aliases[1 + len(args)] = 0
        args.append(buffer)
        in_specs.append(pl.BlockSpec(memory_space=pl.ANY))
    return pl.pallas_call(
        functools.partial(gate_kernel, counts, devices),
        out_shape=jax.ShapeDtypeStruct((total, width), F32),
        grid_spec=pltpu.PrefetchScalarGridSpec(
            num_scalar_prefetch=1,
            grid=(1,),
            in_specs=in_specs,
            out_specs=pl.BlockSpec((rows, width), block),
            scratch_shapes=[pltpu.VMEM((rows, features), BF16)],
        ),
        input_output_aliases=aliases,
        cost_estimate=pl.CostEstimate(
            flops=2 * rows * features * width,
            transcendentals=0,
            bytes_accessed=2 * features * (width + rows) + 4 * rows * width,
        ),
        compiler_params=pltpu.CompilerParams(
            dimension_semantics=("arbitrary",), vmem_limit_bytes=12 << 20
        ),
        name="gate_project",
    )(index, *args)


def spread(value, width):
    rows = value.shape[0]
    left = lax.broadcasted_iota(jnp.int32, (rows, LANES), 1) < HEADDIM
    parts = []
    for p in range(width // LANES):
        a = jnp.broadcast_to(value[:, 2 * p : 2 * p + 1], (rows, LANES))
        b = jnp.broadcast_to(value[:, 2 * p + 1 : 2 * p + 2], (rows, LANES))
        parts.append(jnp.where(left, a, b))
    return jnp.concatenate(parts, axis=1)


def pad_lanes(row):
    return jnp.concatenate([row, jnp.zeros((1, LANES - row.shape[1]), F32)], axis=1)


def state_kernel(
    cfg, index_ref, z_ref, d_ref, prev_ref, tails_ref, rim_ref,
    taps_ref, mtaps_ref, bias_ref, mbias_ref, dtb_ref, rate_ref, *refs,
):
    width, where_am_i = cfg
    xc_ref, cum_ref, step_ref, update_ref, total_ref, ext = refs[-6:]
    e = index_ref[0]
    r, q = where_am_i(pl.program_id(0))
    block = r ^ e
    before = pl.multiple_of((jnp.maximum(block - 1, 0) ^ e) * 8, 8)
    rim = jnp.where(index_ref[1] == 0, 0.0, rim_ref[...])
    first = jnp.where(block == 0, rim, tails_ref[pl.ds(before, 8), :])
    ext[0:8, :] = jnp.where(q == 0, first, prev_ref[...])
    ext[8 : 8 + CHUNK, :] = z_ref[...]
    taps = taps_ref.shape[0]
    outs = []
    for tr, br, lanes in (
        (taps_ref, bias_ref, slice(0, width)),
        (mtaps_ref, mbias_ref, slice(width, width + 2 * STATE)),
    ):
        acc = br[...] + tr[taps - 1 : taps, :] * ext[8 : 8 + CHUNK, lanes]
        for k in range(taps - 1):
            start = 8 - (taps - 1) + k
            acc = acc + tr[k : k + 1, :] * ext[start : start + CHUNK, lanes]
        out = silu(acc)
        xc_ref[:, lanes] = out
        outs.append(out)
    x, maps = outs

    raw = d_ref[...] + pad_lanes(dtb_ref[...])
    step = jnp.maximum(raw, 0.0) + jnp.log1p(jnp.exp(-jnp.abs(raw)))
    decay = -pad_lanes(rate_ref[...]) * step
    rows = lax.broadcasted_iota(jnp.int32, (CHUNK, CHUNK), 0)
    cols = lax.broadcasted_iota(jnp.int32, (CHUNK, CHUNK), 1)
    lower = jnp.where(rows >= cols, 1.0, 0.0).astype(BF16)
    sums = mm(lower, jnp.concatenate(split3(decay), axis=1))
    cum = sums[:, :LANES] + sums[:, LANES : 2 * LANES] + sums[:, 2 * LANES :]
    total = cum[CHUNK - 1 : CHUNK, :]
    cum_ref[...] = cum
    step_ref[...] = step
    total_ref[0] = jnp.broadcast_to(total, total_ref.shape[1:])

    xs = (spread(jnp.exp(total - cum) * step, width) * x).astype(BF16)
    b_hi, b_lo = split2(maps[:, :STATE].T)
    update_ref[0] = mm(jnp.concatenate([b_hi, b_lo], axis=1), jnp.concatenate([xs, xs], axis=0))


def piece_index(r, q, per):
    if isinstance(r, int):
        return r * per + q if r < 2 else 2 * per + ((r // 2 - 1) * per + q) * 2 + r % 2
    far = 2 * per + ((r // 2 - 1) * per + q) * 2 + r % 2
    return jnp.where(r < 2, r * per + q, far)


def run_states(index, z, dt, tails, rim, params, width, per, far, buffers):
    total, wide = z.shape
    chunks = total // CHUNK
    if far is None:
        steps = 2 * per
        at = lambda c: (c // per, c % per)
    else:
        steps = 2
        at = lambda c: (far[0] + c, far[1])

    def piece(c, i):
        r, q = at(c)
        return (piece_index(r, q, per), 0)

    def previous(c, i):
        r, q = at(c)
        return (piece_index(r, jnp.maximum(q - 1, 0), per) * (CHUNK // 8) + CHUNK // 8 - 1, 0)

    def place(c, i):
        r, q = at(c)
        return (r ^ i[0]) * per + q

    row = lambda c, i: (place(c, i), 0)
    deep = lambda c, i: (place(c, i), 0, 0)
    args = [z, dt, z, tails, rim, *params]
    in_specs = [
        pl.BlockSpec((CHUNK, wide), piece),
        pl.BlockSpec((CHUNK, LANES), piece),
        pl.BlockSpec((8, wide), previous),
    ] + [VMEM] * (2 + len(params))
    aliases = {}
    if buffers is not None:
        for n, buffer in enumerate(buffers):
            aliases[1 + len(args)] = n
            args.append(buffer)
            in_specs.append(pl.BlockSpec(memory_space=pl.ANY))
    return pl.pallas_call(
        functools.partial(state_kernel, (width, at)),
        out_shape=(
            jax.ShapeDtypeStruct((total, wide), F32),
            jax.ShapeDtypeStruct((total, LANES), F32),
            jax.ShapeDtypeStruct((total, LANES), F32),
            jax.ShapeDtypeStruct((chunks, STATE, width), F32),
            jax.ShapeDtypeStruct((chunks, 8, LANES), F32),
        ),
        grid_spec=pltpu.PrefetchScalarGridSpec(
            num_scalar_prefetch=1,
            grid=(steps,),
            in_specs=in_specs,
            out_specs=(
                pl.BlockSpec((CHUNK, wide), row),
                pl.BlockSpec((CHUNK, LANES), row),
                pl.BlockSpec((CHUNK, LANES), row),
                pl.BlockSpec((1, STATE, width), deep),
                pl.BlockSpec((1, 8, LANES), deep),
            ),
            scratch_shapes=[pltpu.VMEM((CHUNK + 8, wide), F32)],
        ),
        input_output_aliases=aliases,
        cost_estimate=pl.CostEstimate(
            flops=2 * steps * CHUNK * width * 1000, transcendentals=steps * CHUNK * wide,
            bytes_accessed=12 * steps * CHUNK * wide,
        ),
        compiler_params=pltpu.CompilerParams(
            dimension_semantics=("arbitrary",), vmem_limit_bytes=12 << 20
        ),
        name="run_states",
    )(index, *args)


def stitch_kernel(
    width, update_ref, total_ref, entry_ref, before_ref, group_ref, glog_ref, send_ref, prefix_ref, plog_ref,
):
    chunks = update_ref.shape[0]
    state = jnp.zeros(group_ref.shape, F32)
    log = jnp.zeros(total_ref.shape[1:], F32)
    for c in range(chunks):
        entry_ref[c] = state.astype(BF16)
        before_ref[c] = log
        total = total_ref[c]
        state = spread(jnp.exp(total), width)[0:1, :] * state + update_ref[c]
        log = log + total
    group_ref[...] = state
    wide = spread(log, width)
    glog_ref[...] = wide
    send_ref[0:STATE, :] = state.astype(BF16)
    send_ref[STATE : STATE + 8, :] = pack_logs(wide)
    prefix_ref[...] = jnp.zeros_like(state)
    plog_ref[...] = jnp.zeros_like(wide)


def stitch(updates, totals):
    _, state, width = updates.shape
    return pl.pallas_call(
        functools.partial(stitch_kernel, width),
        out_shape=(
            jax.ShapeDtypeStruct(updates.shape, BF16),
            jax.ShapeDtypeStruct(totals.shape, F32),
            jax.ShapeDtypeStruct((state, width), F32),
            jax.ShapeDtypeStruct((8, width), F32),
            jax.ShapeDtypeStruct((state + 8, width), BF16),
            jax.ShapeDtypeStruct((state, width), F32),
            jax.ShapeDtypeStruct((8, width), F32),
        ),
        in_specs=[VMEM, VMEM],
        out_specs=(VMEM,) * 7,
        compiler_params=pltpu.CompilerParams(vmem_limit_bytes=8 << 20),
        name="stitch",
    )(updates, totals)


def output_kernel(
    width, index_ref, xc_ref, cum_ref, step_ref, before_ref, local_ref, g_ref, direct_ref,
    a_ref, b_ref, c_ref,
):
    bmap = xc_ref[:, width : width + STATE]
    cmap = xc_ref[:, width + STATE :]
    cum = cum_ref[...]
    b_hi, b_lo = split2(bmap)
    c_hi, c_lo = split2(cmap)
    c_ref[...] = c_hi
    gram = mm_nt(jnp.concatenate([c_hi, c_lo], axis=1), jnp.concatenate([b_hi, b_hi], axis=1))
    gram = gram + mm_nt(c_hi, b_lo)
    cum_t = cum.T
    step_t = step_ref[...].T
    rows = lax.broadcasted_iota(jnp.int32, (CHUNK, CHUNK), 0)
    cols = lax.broadcasted_iota(jnp.int32, (CHUNK, CHUNK), 1)
    causal = rows >= cols
    left = cols < HEADDIM
    direct = pad_lanes(direct_ref[...])
    for p in range(width // LANES):
        lanes = slice(p * LANES, (p + 1) * LANES)
        ws, cs = [], []
        for h in (2 * p, 2 * p + 1):
            column = jnp.broadcast_to(cum[:, h : h + 1], (CHUNK, CHUNK))
            differ = jnp.where(causal, column - cum_t[h : h + 1, :], -jnp.inf)
            ws.append((jnp.exp(differ) * (gram * step_t[h : h + 1, :])).astype(BF16))
            cs.append(column)
        x = xc_ref[:, lanes]
        xb = jnp.concatenate([jnp.where(left, x, 0.0), jnp.where(left, 0.0, x)], axis=0)
        both = lambda v: jnp.where(
            left[0:1, :],
            jnp.broadcast_to(v[:, 2 * p : 2 * p + 1], (1, LANES)),
            jnp.broadcast_to(v[:, 2 * p + 1 : 2 * p + 2], (1, LANES)),
        )
        inside = mm(jnp.concatenate(ws, axis=1), xb.astype(BF16))
        fade = jnp.exp(jnp.where(left, cs[0], cs[1]))
        y = inside + fade * mm(c_hi, local_ref[0, :, lanes]) + both(direct) * x
        gate = silu(g_ref[:, lanes])
        a_ref[:, lanes] = y * gate
        b_ref[:, lanes] = fade * jnp.exp(both(before_ref[0, 0:1, :])) * gate


def run_outputs(index, xc, cum, step, before, local_states, gate, direct, local):
    total, wide = xc.shape
    width = gate.shape[1]
    chunks = total // CHUNK
    per = local // CHUNK
    const = lambda c, i: (0, 0)
    row = lambda c, i: (c, 0)
    deep = lambda c, i: (c, 0, 0)
    return pl.pallas_call(
        functools.partial(output_kernel, width),
        out_shape=(
            jax.ShapeDtypeStruct((total, width), F32),
            jax.ShapeDtypeStruct((total, width), F32),
            jax.ShapeDtypeStruct((total, STATE), BF16),
        ),
        grid_spec=pltpu.PrefetchScalarGridSpec(
            num_scalar_prefetch=1,
            grid=(chunks,),
            in_specs=[
                pl.BlockSpec((CHUNK, wide), row),
                pl.BlockSpec((CHUNK, LANES), row),
                pl.BlockSpec((CHUNK, LANES), row),
                pl.BlockSpec((1, 8, LANES), deep),
                pl.BlockSpec((1, STATE, width), deep),
                pl.BlockSpec((CHUNK, width), lambda c, i: (piece_index((c // per) ^ i[0], c % per, per), 0)),
                pl.BlockSpec(direct.shape, const),
            ],
            out_specs=(
                pl.BlockSpec((CHUNK, width), row),
                pl.BlockSpec((CHUNK, width), row),
                pl.BlockSpec((CHUNK, STATE), row),
            ),
        ),
        cost_estimate=pl.CostEstimate(
            flops=2 * total * width * 1500, transcendentals=total * width * 4, bytes_accessed=16 * total * width
        ),
        compiler_params=pltpu.CompilerParams(
            dimension_semantics=("arbitrary",), vmem_limit_bytes=12 << 20
        ),
        name="run_outputs",
    )(index, xc, cum, step, before, local_states, gate, direct)


def pack_logs(wide):
    hi, mid, lo = split3(wide)
    row = lax.broadcasted_iota(jnp.int32, wide.shape, 0)
    lo = jnp.where(row == 2, lo.astype(F32), 0.0)
    return jnp.where(row == 0, hi.astype(F32), jnp.where(row == 1, mid.astype(F32), lo)).astype(BF16)


def unpack(got_ref):
    other = got_ref[0:STATE, :].astype(F32)
    logs = got_ref[STATE : STATE + 8, :].astype(F32)
    log = logs[0:1, :] + logs[1:2, :] + logs[2:3, :]
    return other, log


def combine_kernel(
    d, index_ref, got_ref, group_ref, glog_ref, prefix_ref, plog_ref,
    send_ref, group_out, glog_out, prefix_out, plog_out,
):
    upper = (index_ref[1] & d) != 0
    other, other_log = unpack(got_ref)
    group, group_log = group_ref[...], glog_ref[0:1, :]
    prefix, prefix_log = prefix_ref[...], plog_ref[0:1, :]
    prefix_out[...] = jnp.where(upper, prefix + jnp.exp(prefix_log) * other, prefix)
    new_plog = jnp.where(upper, prefix_log + other_log, prefix_log)
    plog_out[...] = jnp.broadcast_to(new_plog, plog_out.shape)
    late = jnp.where(upper, group, other)
    early = jnp.where(upper, other, group)
    late_log = jnp.where(upper, group_log, other_log)
    new = late + jnp.exp(late_log) * early
    new_log = jnp.broadcast_to(group_log + other_log, glog_out.shape)
    group_out[...] = new
    glog_out[...] = new_log
    send_ref[0:STATE, :] = new.astype(BF16)
    send_ref[STATE : STATE + 8, :] = pack_logs(new_log)


def combine(index, d, got, group, glog, prefix, plog):
    state = jax.ShapeDtypeStruct(group.shape, F32)
    log = jax.ShapeDtypeStruct(glog.shape, F32)
    full = lambda x: pl.BlockSpec(x.shape, lambda i, s: (0, 0))
    outs = (jax.ShapeDtypeStruct(got.shape, BF16), state, log, state, log)
    return pl.pallas_call(
        functools.partial(combine_kernel, d),
        out_shape=outs,
        grid_spec=pltpu.PrefetchScalarGridSpec(
            num_scalar_prefetch=1,
            grid=(1,),
            in_specs=[full(x) for x in (got, group, glog, prefix, plog)],
            out_specs=tuple(full(x) for x in outs),
        ),
        compiler_params=pltpu.CompilerParams(vmem_limit_bytes=8 << 20),
        name="combine",
    )(index, got, group, glog, prefix, plog)


def join_kernel(d, index_ref, a_ref, b_ref, c_ref, got_ref, prefix_ref, plog_ref, o_ref, ss_ref, s_scr):
    @pl.when(pl.program_id(0) == 0)
    def _():
        other, _ = unpack(got_ref)
        prefix = prefix_ref[...]
        upper = (index_ref[1] & d) != 0
        entering = jnp.where(upper, prefix + jnp.exp(plog_ref[0:1, :]) * other, prefix)
        s_scr[...] = entering.astype(BF16)

    gated = a_ref[...] + b_ref[...] * mm(c_ref[...], s_scr[...])
    o_ref[...] = gated
    hi, lo = split2(gated * gated)
    ones = jnp.ones((8, 2 * hi.shape[1]), BF16)
    ss_ref[...] = mm_nt(ones, jnp.concatenate([hi, lo], axis=1))[0:1]


def join(index, d, a, b, c, got, prefix, plog):
    total, width = a.shape
    rows = 256
    row = lambda i, s: (i, 0)
    full = lambda x: pl.BlockSpec(x.shape, lambda i, s: (0, 0))
    return pl.pallas_call(
        functools.partial(join_kernel, d),
        out_shape=(jax.ShapeDtypeStruct((total, width), F32), jax.ShapeDtypeStruct((1, total), F32)),
        grid_spec=pltpu.PrefetchScalarGridSpec(
            num_scalar_prefetch=1,
            grid=(total // rows,),
            in_specs=[
                pl.BlockSpec((rows, width), row),
                pl.BlockSpec((rows, width), row),
                pl.BlockSpec((rows, STATE), row),
                full(got),
                full(prefix),
                full(plog),
            ],
            out_specs=(
                pl.BlockSpec((rows, width), row),
                pl.BlockSpec((1, rows), lambda i, s: (0, i)),
            ),
            scratch_shapes=[pltpu.VMEM((STATE, width), BF16)],
        ),
        compiler_params=pltpu.CompilerParams(
            dimension_semantics=("arbitrary",), vmem_limit_bytes=10 << 20
        ),
        name="join",
    )(index, a, b, c, got, prefix, plog)


def norm_kernel(inner_width, g_ref, mine_ref, other_ref, gain_ref, o_ref):
    scale = lax.rsqrt((mine_ref[...] + other_ref[...]) / inner_width + 1e-05)
    width = g_ref.shape[1]
    for part in range(g_ref.shape[0] // LANES):
        rows = slice(part * LANES, (part + 1) * LANES)
        column = jnp.broadcast_to(scale[:, rows], (LANES, LANES)).T
        for lane in range(width // LANES):
            lanes = slice(lane * LANES, (lane + 1) * LANES)
            o_ref[rows, lanes] = (g_ref[rows, lanes] * column * gain_ref[:, lanes]).astype(BF16)


def norm(gated, mine, other, gain, inner_width):
    total, width = gated.shape
    rows = 256
    return pl.pallas_call(
        functools.partial(norm_kernel, inner_width),
        out_shape=jax.ShapeDtypeStruct((total, width), BF16),
        grid=(total // rows,),
        in_specs=[
            pl.BlockSpec((rows, width), lambda i: (i, 0)),
            pl.BlockSpec((1, rows), lambda i: (0, i)),
            pl.BlockSpec((1, rows), lambda i: (0, i)),
            pl.BlockSpec(gain.shape, lambda i: (0, 0)),
        ],
        out_specs=pl.BlockSpec((rows, width), lambda i: (i, 0)),
        compiler_params=pltpu.CompilerParams(
            dimension_semantics=("arbitrary",), vmem_limit_bytes=8 << 20
        ),
        name="norm",
    )(gated, mine, other, gain)


def body(
    tokens,
    routes,
    gate_inner_weight,
    state_map_weight,
    step_size_weight,
    adapter_down_weight,
    adapter_up_weight,
    inner_conv_taps,
    state_map_taps,
    inner_conv_bias,
    state_map_conv_bias,
    step_size_bias,
    head_decay_rate,
    direct_head_scale,
    gated_norm_scale,
):
    n = lax.axis_size("exp")
    shards = lax.axis_size("seq")
    local, features = tokens.shape
    total = local * n
    width = gate_inner_weight.shape[2]
    experts = adapter_up_weight.shape[0]
    rank = 8
    e = lax.axis_index("exp")
    index = jnp.stack([e, lax.axis_index("seq")]).astype(jnp.int32)
    per = local // CHUNK

    route_row = jnp.pad(routes.reshape(1, local).astype(BF16), ((0, 0), (0, features - local)))
    down = {0: jnp.concatenate([adapter_down_weight.T, route_row, tokens[local - 7 :]], axis=0)}
    far = {}
    for k in range(2, n, 2):
        down[k] = swap(down[0], "exp", k)
    for q in range(per):
        for k in range(2, n, 2):
            far[k, q] = swap(tokens[q * CHUNK : (q + 1) * CHUNK], "exp", k)
    sibling = swap(tokens, "exp", 1)
    for k in range(0, n, 2):
        down[k + 1] = swap(down[k], "exp", 1)
    downs = [down[k] for k in range(n)]
    wz = gate_inner_weight.reshape(features, 2 * width)
    up = adapter_up_weight.reshape(experts, 2 * width)
    call = functools.partial(
        project, index, downs=downs, dt_t=step_size_weight.T, wz=wz, wbc=state_map_weight,
        up=up, rank=rank, total=total,
    )
    *buffers, tails, rim = call(
        [tokens, sibling], route_from=((0, 0, local), (1, 0, local)), row_block=0, buffers=None
    )
    rim = lax.ppermute(rim, "seq", [(i, (i + 1) % shards) for i in range(shards)])
    params = [
        inner_conv_taps, state_map_taps, inner_conv_bias[None, :], state_map_conv_bias[None, :],
        step_size_bias[None, :], head_decay_rate[None, :],
    ]
    kept = run_states(index, buffers[0], buffers[1], tails, rim, params, width, per, None, None)
    far_rows = {}
    for q in range(per):
        for k in range(2, n, 2):
            mine = far[k, q]
            other = swap(mine, "exp", 1)
            far_rows[k, q] = (mine, other)
            buffers = call(
                [mine, other],
                route_from=((k, q * CHUNK, CHUNK), (k + 1, q * CHUNK, CHUNK)),
                row_block=per + (k // 2 - 1) * per + q,
                buffers=buffers,
            )
            kept = run_states(
                index, buffers[0], buffers[1], tails, rim, params, width, per, (k, q), kept
            )
    xc, cum, step, updates, totals = kept
    lift = buffers[2]
    states, before, group, glog, send, prefix, plog = stitch(updates, totals)
    d = 1
    while True:
        got = swap(send, "seq", d)
        if 2 * d >= shards:
            break
        send, group, glog, prefix, plog = combine(index, d, got, group, glog, prefix, plog)
        d *= 2
    gate = gate_project(index, [tokens, sibling], lift, wz, up, n, total, 0, None)
    for k in range(2, n, 2):
        xs = []
        for q in range(per):
            xs.extend(far_rows[k, q])
        gate = gate_project(index, xs, lift, wz, up, n, total, k // 2, gate)
    a, b, c = run_outputs(
        index, xc, cum, step, before, states, gate, direct_head_scale[None, :], local
    )
    gated, mine = join(index, d, a, b, c, got, prefix, plog)
    d = 1
    while 2 * d < n:
        mine = mine + swap(mine, "exp", d)
        d *= 2
    return norm(gated, mine, swap(mine, "exp", d), gated_norm_scale[None, :], width * n)


def solution(mesh):
    in_specs = (
        P(("seq", "exp"), None),
        P(("seq", "exp"), None),
        P(None, None, "exp"),
        P(),
        P(None, "exp"),
        P(None, "exp"),
        P(None, None, "exp"),
        P(None, "exp"),
        P(),
        P("exp"),
        P(),
        P("exp"),
        P("exp"),
        P("exp"),
        P("exp"),
    )
    out_specs = P("seq", "exp")

    return jax.shard_map(body, mesh=mesh, in_specs=in_specs, out_specs=out_specs, check_vma=False)
```

```python
import functools

import jax
import jax.numpy as jnp
from jax import lax
from jax.experimental import pallas as pl
from jax.experimental.pallas import tpu as pltpu
from jax.sharding import PartitionSpec as P


STATE = 128
HEADDIM = 64
CHUNK = 128
LANES = 128
F32 = jnp.float32
BF16 = jnp.bfloat16


def swap(block, axis, mask):
    return lax.ppermute(block, axis, [(i, i ^ mask) for i in range(lax.axis_size(axis))])


def split3(value):
    hi = value.astype(BF16)
    rest = value - hi.astype(F32)
    mid = rest.astype(BF16)
    lo = (rest - mid.astype(F32)).astype(BF16)
    return hi, mid, lo


def split2(value):
    hi = value.astype(BF16)
    return hi, (value - hi.astype(F32)).astype(BF16)


def mm(a, b):
    return jnp.dot(a, b, preferred_element_type=F32)


def mm_nt(a, b):
    return lax.dot_general(a, b, (((1,), (1,)), ((), ())), preferred_element_type=F32)


def silu(v):
    half = 0.5 * v
    return half + half * jnp.tanh(half)


def route_mask(e, route_row, experts_dev, rank):
    column = lax.broadcasted_iota(jnp.int32, (LANES, route_row.shape[1]), 0)
    per_dev = experts_dev * rank
    expert = ((column // per_dev) ^ e) * experts_dev + (column % per_dev) // rank
    return jnp.where(expert.astype(F32) == route_row, 1.0, 0.0)


VMEM = pl.BlockSpec(memory_space=pltpu.VMEM)


def up_rows(up_ref, e, devices, lanes):
    cols = up_ref.shape[0] // devices
    return jnp.concatenate(
        [up_ref[pl.ds(pl.multiple_of((e ^ r) * cols, cols), cols), lanes] for r in range(devices)], axis=0
    )


def pack_kernel(tokens_ref, route_ref, *refs):
    halves, (note_ref, tail, sems) = refs[:-3], refs[-3:]
    rows = halves[0].shape[0]
    copies = [
        pltpu.make_async_copy(tokens_ref.at[q * rows : (q + 1) * rows], half, sems.at[q])
        for q, half in enumerate(halves)
    ]
    last = tokens_ref.shape[0] - 8
    copies.append(pltpu.make_async_copy(tokens_ref.at[last:], tail, sems.at[len(halves)]))
    for copy in copies[::-1]:
        copy.start()
    copies[-1].wait()
    route = route_ref[...].astype(F32)
    route = jnp.concatenate([route, jnp.zeros((1, tail.shape[1] - route.shape[1]), F32)], axis=1)
    row = lax.broadcasted_iota(jnp.int32, tail.shape, 0)
    note_ref[...] = jnp.where(row == 0, route, tail[...].astype(F32)).astype(BF16)
    for copy in copies[:-1]:
        copy.wait()


def pack(tokens, route_row, per):
    features = tokens.shape[1]
    anywhere = pl.BlockSpec(memory_space=pl.ANY)
    piece = jax.ShapeDtypeStruct((CHUNK, features), BF16)
    return pl.pallas_call(
        pack_kernel,
        out_shape=(piece,) * per + (jax.ShapeDtypeStruct((8, features), BF16),),
        in_specs=[anywhere, VMEM],
        out_specs=(VMEM,) * (per + 1),
        scratch_shapes=[pltpu.VMEM((8, features), BF16), pltpu.SemaphoreType.DMA((per + 1,))],
        compiler_params=pltpu.CompilerParams(vmem_limit_bytes=4 << 20),
        name="pack",
    )(tokens, route_row)


def project_kernel(cfg, index_ref, *refs):
    counts, route_from, devices, cols, rank, near = cfg
    x_refs, refs = refs[: len(counts)], refs[len(counts):]
    n_refs, refs = refs[:devices], refs[devices:]
    w_ref, wbc_ref, up_ref = refs[:3]
    refs = refs[3:]
    if near:
        dt_ref, d_refs, refs = refs[0], refs[1 : 1 + devices], refs[1 + devices:]
        z_ref, dto_ref, lift_ref, tails_ref, rim_ref, wsm_ref, x_scr, lift_scr = refs
    else:
        wsm_ref, z_ref, dto_ref, lift_ref, x_scr = refs
        lift_scr = lift_ref
    e = index_ref[0]
    rows = sum(counts)

    at = 0
    for x_ref, n in zip(x_refs, counts):
        x_scr[at : at + n, :] = x_ref[...]
        at += n
    if near:
        for r in range(devices):
            x_scr[at + 8 * r : at + 8 * r + 8, :] = n_refs[r][...]
        wsm_ref[LANES:, :] = jnp.zeros((wsm_ref.shape[0] - LANES, wsm_ref.shape[1]), BF16)
        wsm_ref[LANES : LANES + dt_ref.shape[0], :] = dt_ref[...]
        for r in range(devices):
            wsm_ref[r * cols : (r + 1) * cols, :] = d_refs[r][...]
    small = mm_nt(x_scr[...], wsm_ref[...])

    def mask_of(r, lane):
        row = n_refs[r][0:1, lane : lane + LANES].astype(F32)
        return route_mask(e, row, cols // rank, rank).T

    masks = []
    for r, first, n in route_from:
        for lane in range(first, first + n, LANES):
            masks.append(mask_of(r, lane))
    if near:
        last = route_from[0][1] + route_from[0][2] - LANES
        for r in range(devices):
            masks.append(mask_of(r, last)[LANES - 8 :, :])
    lift = jnp.where(jnp.concatenate(masks, axis=0) > 0.5, small[:, :LANES], 0.0).astype(BF16)
    lift_scr[...] = lift
    pad = jnp.zeros((rows, 2 * LANES - small.shape[1]), F32)
    dto_ref[...] = jnp.concatenate([small[:rows, LANES:], pad], axis=1)
    if near:
        lift_ref[...] = lift[:rows]

    def put(lanes, value):
        z_ref[:, lanes] = value[:rows]
        if near:
            tails_ref[:, lanes] = value[rows:]

    width = z_ref.shape[1]
    inner = up_ref.shape[1] // 2
    tn = 256 if inner % 256 == 0 else 128
    for at in range(0, inner, tn):
        lanes = slice(inner + at, inner + at + tn)
        up = up_rows(up_ref, e, devices, lanes)
        put(slice(at, at + tn), mm(x_scr[...], w_ref[:, lanes]) + mm(lift_scr[...], up))
    for at in range(0, width - inner, tn):
        put(slice(inner + at, inner + at + tn), mm(x_scr[...], wbc_ref[:, at : at + tn]))
    if near:
        row = ((devices - 1) ^ e) * 8
        rim_ref[...] = tails_ref[pl.ds(pl.multiple_of(row, 8), 8), :]


def project(index, xs, route_from, notes, wz, wbc, up, rank, dt_t=None, downs=None, wsm=None):
    counts = tuple(x.shape[0] for x in xs)
    rows = sum(counts)
    features = wz.shape[0]
    width = up.shape[1] // 2 + wbc.shape[1]
    devices = len(notes)
    near = wsm is None
    args = list(xs) + list(notes) + [wz, wbc, up]
    args += [dt_t, *downs] if near else [wsm]
    out_shape = [
        jax.ShapeDtypeStruct((rows, width), F32),
        jax.ShapeDtypeStruct((rows, LANES), F32),
        jax.ShapeDtypeStruct((rows, LANES), BF16),
    ]
    extra = 8 * devices if near else 0
    scratch = [pltpu.VMEM((rows + extra, features), BF16)]
    if near:
        out_shape += [jax.ShapeDtypeStruct((extra, width), F32), jax.ShapeDtypeStruct((8, width), F32)]
        out_shape.append(jax.ShapeDtypeStruct((LANES + 16, features), BF16))
        scratch.append(pltpu.VMEM((rows + extra, LANES), BF16))
    cfg = (counts, route_from, devices, LANES // devices, rank, near)
    return pl.pallas_call(
        functools.partial(project_kernel, cfg),
        out_shape=tuple(out_shape),
        grid_spec=pltpu.PrefetchScalarGridSpec(
            num_scalar_prefetch=1,
            grid=(1,),
            in_specs=[VMEM] * len(args),
            out_specs=(VMEM,) * len(out_shape),
            scratch_shapes=scratch,
        ),
        cost_estimate=pl.CostEstimate(
            flops=2 * rows * features * (width + 256),
            transcendentals=0,
            bytes_accessed=2 * features * (width + rows) + 4 * rows * width,
        ),
        compiler_params=pltpu.CompilerParams(
            dimension_semantics=("arbitrary",), vmem_limit_bytes=16 << 20
        ),
        name="project",
    )(index, *args)


def gate_kernel(counts, devices, lifts, index_ref, *refs):
    x_refs, refs = refs[: len(counts)], refs[len(counts):]
    lift = jnp.concatenate([r[...] for r in refs[:lifts]], axis=0)
    w_ref, up_ref = refs[lifts : lifts + 2]
    g_ref, x_scr = refs[-2:]
    at = 0
    for x_ref, n in zip(x_refs, counts):
        x_scr[at : at + n, :] = x_ref[...]
        at += n
    width = g_ref.shape[1]
    tn = 256 if width % 256 == 0 else 128
    for at in range(0, width, tn):
        lanes = slice(at, at + tn)
        up = up_rows(up_ref, index_ref[0], devices, lanes)
        g_ref[:, lanes] = mm(x_scr[...], w_ref[:, lanes]) + mm(lift, up)


def gate_project(index, xs, lifts, wz, up, devices, total, row_block, buffer):
    counts = tuple(x.shape[0] for x in xs)
    rows = sum(counts)
    features = wz.shape[0]
    width = up.shape[1] // 2
    block = lambda t, i: (row_block, 0)
    args = list(xs) + list(lifts) + [wz, up]
    in_specs = [VMEM] * len(args)
    aliases = {}
    if buffer is not None:
        aliases[1 + len(args)] = 0
        args.append(buffer)
        in_specs.append(pl.BlockSpec(memory_space=pl.ANY))
    return pl.pallas_call(
        functools.partial(gate_kernel, counts, devices, len(lifts)),
        out_shape=jax.ShapeDtypeStruct((total, width), F32),
        grid_spec=pltpu.PrefetchScalarGridSpec(
            num_scalar_prefetch=1,
            grid=(1,),
            in_specs=in_specs,
            out_specs=pl.BlockSpec((rows, width), block),
            scratch_shapes=[pltpu.VMEM((rows, features), BF16)],
        ),
        input_output_aliases=aliases,
        cost_estimate=pl.CostEstimate(
            flops=2 * rows * features * width,
            transcendentals=0,
            bytes_accessed=2 * features * (width + rows) + 4 * rows * width,
        ),
        compiler_params=pltpu.CompilerParams(
            dimension_semantics=("arbitrary",), vmem_limit_bytes=12 << 20
        ),
        name="gate_project",
    )(index, *args)


def spread(value, width):
    rows = value.shape[0]
    left = lax.broadcasted_iota(jnp.int32, (rows, LANES), 1) < HEADDIM
    parts = []
    for p in range(width // LANES):
        a = jnp.broadcast_to(value[:, 2 * p : 2 * p + 1], (rows, LANES))
        b = jnp.broadcast_to(value[:, 2 * p + 1 : 2 * p + 2], (rows, LANES))
        parts.append(jnp.where(left, a, b))
    return jnp.concatenate(parts, axis=1)


def pad_lanes(row):
    return jnp.concatenate([row, jnp.zeros((1, LANES - row.shape[1]), F32)], axis=1)


def state_kernel(
    cfg, index_ref, z_all, d_all, older_all, tails_ref, rim_ref,
    taps_ref, mtaps_ref, bias_ref, mbias_ref, dtb_ref, rate_ref, *refs,
):
    width, per, far, where_am_i = cfg
    xc_all, cum_all, step_all, update_all, total_all, ext = refs[-6:]
    e = index_ref[0]
    r, q = where_am_i(pl.program_id(0))
    block = r ^ e
    at = pl.program_id(0) * CHUNK
    there = pl.ds(pl.multiple_of(at, CHUNK), CHUNK)
    z_ref, d_ref = z_all.at[there], d_all.at[there]
    older = at + CHUNK - 8 if far else jnp.maximum(at - 8, 0)
    prev_ref = older_all.at[pl.ds(pl.multiple_of(older, 8), 8)]
    chunk = block * per + q
    here = pl.ds(pl.multiple_of(chunk * CHUNK, CHUNK), CHUNK)
    xc_ref, cum_ref, step_ref = xc_all.at[here], cum_all.at[here], step_all.at[here]
    update_ref, total_ref = update_all.at[pl.ds(chunk, 1)], total_all.at[pl.ds(chunk, 1)]
    before = pl.multiple_of((jnp.maximum(block - 1, 0) ^ e) * 8, 8)
    rim = jnp.where(index_ref[1] == 0, 0.0, rim_ref[...])
    first = jnp.where(block == 0, rim, tails_ref[pl.ds(before, 8), :])
    ext[0:8, :] = jnp.where(q == 0, first, prev_ref[...])
    ext[8 : 8 + CHUNK, :] = z_ref[...]
    taps = taps_ref.shape[0]
    outs = []
    for tr, br, lanes in (
        (taps_ref, bias_ref, slice(0, width)),
        (mtaps_ref, mbias_ref, slice(width, width + 2 * STATE)),
    ):
        acc = br[...] + tr[taps - 1 : taps, :] * ext[8 : 8 + CHUNK, lanes]
        for k in range(taps - 1):
            start = 8 - (taps - 1) + k
            acc = acc + tr[k : k + 1, :] * ext[start : start + CHUNK, lanes]
        out = silu(acc)
        xc_ref[:, lanes] = out
        outs.append(out)
    x, maps = outs

    raw = d_ref[...] + pad_lanes(dtb_ref[...])
    step = jnp.maximum(raw, 0.0) + jnp.log1p(jnp.exp(-jnp.abs(raw)))
    decay = -pad_lanes(rate_ref[...]) * step
    rows = lax.broadcasted_iota(jnp.int32, (CHUNK, CHUNK), 0)
    cols = lax.broadcasted_iota(jnp.int32, (CHUNK, CHUNK), 1)
    lower = jnp.where(rows >= cols, 1.0, 0.0).astype(BF16)
    sums = mm(lower, jnp.concatenate(split3(decay), axis=1))
    cum = sums[:, :LANES] + sums[:, LANES : 2 * LANES] + sums[:, 2 * LANES :]
    total = cum[CHUNK - 1 : CHUNK, :]
    cum_ref[...] = cum
    step_ref[...] = step
    total_ref[0] = jnp.broadcast_to(total, total_ref.shape[1:])

    xs = (spread(jnp.exp(total - cum) * step, width) * x).astype(BF16)
    b_hi, b_lo = split2(maps[:, :STATE].T)
    update_ref[0] = mm(jnp.concatenate([b_hi, b_lo], axis=1), jnp.concatenate([xs, xs], axis=0))


def piece_index(r, q, per):
    if isinstance(r, int):
        return r * per + q if r < 2 else 2 * per + ((r // 2 - 1) * per + q) * 2 + r % 2
    far = 2 * per + ((r // 2 - 1) * per + q) * 2 + r % 2
    return jnp.where(r < 2, r * per + q, far)


def run_states(index, total, z, dt, older, tails, rim, params, width, per, far, buffers):
    wide = z.shape[1]
    chunks = total // CHUNK
    if far is None:
        steps = 2 * per
        at = lambda c: (c // per, c % per)
    else:
        steps = 2
        at = lambda c: (far[0] + c, far[1])

    args = [z, dt, older, tails, rim, *params]
    in_specs = [VMEM] * len(args)
    aliases = {}
    if buffers is not None:
        for n, buffer in enumerate(buffers):
            aliases[1 + len(args)] = n
            args.append(buffer)
            in_specs.append(VMEM)
    return pl.pallas_call(
        functools.partial(state_kernel, (width, per, far is not None, at)),
        out_shape=(
            jax.ShapeDtypeStruct((total, wide), F32),
            jax.ShapeDtypeStruct((total, LANES), F32),
            jax.ShapeDtypeStruct((total, LANES), F32),
            jax.ShapeDtypeStruct((chunks, STATE, width), F32),
            jax.ShapeDtypeStruct((chunks, 8, LANES), F32),
        ),
        grid_spec=pltpu.PrefetchScalarGridSpec(
            num_scalar_prefetch=1,
            grid=(steps,),
            in_specs=in_specs,
            out_specs=(VMEM,) * 5,
            scratch_shapes=[pltpu.VMEM((CHUNK + 8, wide), F32)],
        ),
        input_output_aliases=aliases,
        cost_estimate=pl.CostEstimate(
            flops=2 * steps * CHUNK * width * 1000, transcendentals=steps * CHUNK * wide,
            bytes_accessed=12 * steps * CHUNK * wide,
        ),
        compiler_params=pltpu.CompilerParams(
            dimension_semantics=("arbitrary",), vmem_limit_bytes=12 << 20
        ),
        name="run_states",
    )(index, *args)


def stitch_kernel(
    width, update_ref, total_ref, entry_ref, before_ref, group_ref, glog_ref, send_ref, prefix_ref, plog_ref,
):
    chunks = update_ref.shape[0]
    state = jnp.zeros(group_ref.shape, F32)
    log = jnp.zeros(total_ref.shape[1:], F32)
    for c in range(chunks):
        entry_ref[c] = state.astype(BF16)
        before_ref[c] = log
        total = total_ref[c]
        state = spread(jnp.exp(total), width)[0:1, :] * state + update_ref[c]
        log = log + total
    group_ref[...] = state
    wide = spread(log, width)
    glog_ref[...] = wide
    send_ref[0:STATE, :] = state.astype(BF16)
    send_ref[STATE : STATE + 8, :] = pack_logs(wide)
    prefix_ref[...] = jnp.zeros_like(state)
    plog_ref[...] = jnp.zeros_like(wide)


def stitch(updates, totals):
    _, state, width = updates.shape
    return pl.pallas_call(
        functools.partial(stitch_kernel, width),
        out_shape=(
            jax.ShapeDtypeStruct(updates.shape, BF16),
            jax.ShapeDtypeStruct(totals.shape, F32),
            jax.ShapeDtypeStruct((state, width), F32),
            jax.ShapeDtypeStruct((8, width), F32),
            jax.ShapeDtypeStruct((state + 8, width), BF16),
            jax.ShapeDtypeStruct((state, width), F32),
            jax.ShapeDtypeStruct((8, width), F32),
        ),
        in_specs=[VMEM, VMEM],
        out_specs=(VMEM,) * 7,
        compiler_params=pltpu.CompilerParams(vmem_limit_bytes=8 << 20),
        name="stitch",
    )(updates, totals)


def output_kernel(
    width, per, index_ref, xc_all, cum_all, step_all, before_all, local_all, g_all, direct_ref,
    a_all, b_all, c_all,
):
    c = pl.program_id(0)
    here = pl.ds(pl.multiple_of(c * CHUNK, CHUNK), CHUNK)
    piece = piece_index((c // per) ^ index_ref[0], c % per, per)
    there = pl.ds(pl.multiple_of(piece * CHUNK, CHUNK), CHUNK)
    xc_ref, cum_ref, step_ref, g_ref = xc_all.at[here], cum_all.at[here], step_all.at[here], g_all.at[there]
    before_ref, local_ref = before_all.at[pl.ds(c, 1)], local_all.at[pl.ds(c, 1)]
    a_ref, b_ref, c_ref = a_all.at[here], b_all.at[here], c_all.at[here]
    bmap = xc_ref[:, width : width + STATE]
    cmap = xc_ref[:, width + STATE :]
    cum = cum_ref[...]
    b_hi, b_lo = split2(bmap)
    c_hi, c_lo = split2(cmap)
    c_ref[...] = c_hi
    gram = mm_nt(jnp.concatenate([c_hi, c_lo], axis=1), jnp.concatenate([b_hi, b_hi], axis=1))
    gram = gram + mm_nt(c_hi, b_lo)
    cum_t = cum.T
    step_t = step_ref[...].T
    rows = lax.broadcasted_iota(jnp.int32, (CHUNK, CHUNK), 0)
    cols = lax.broadcasted_iota(jnp.int32, (CHUNK, CHUNK), 1)
    causal = rows >= cols
    left = cols < HEADDIM
    direct = pad_lanes(direct_ref[...])
    for p in range(width // LANES):
        lanes = slice(p * LANES, (p + 1) * LANES)
        ws, cs = [], []
        for h in (2 * p, 2 * p + 1):
            column = jnp.broadcast_to(cum[:, h : h + 1], (CHUNK, CHUNK))
            differ = jnp.where(causal, column - cum_t[h : h + 1, :], -jnp.inf)
            ws.append((jnp.exp(differ) * (gram * step_t[h : h + 1, :])).astype(BF16))
            cs.append(column)
        x = xc_ref[:, lanes]
        xb = jnp.concatenate([jnp.where(left, x, 0.0), jnp.where(left, 0.0, x)], axis=0)
        both = lambda v: jnp.where(
            left[0:1, :],
            jnp.broadcast_to(v[:, 2 * p : 2 * p + 1], (1, LANES)),
            jnp.broadcast_to(v[:, 2 * p + 1 : 2 * p + 2], (1, LANES)),
        )
        inside = mm(jnp.concatenate(ws, axis=1), xb.astype(BF16))
        fade = jnp.exp(jnp.where(left, cs[0], cs[1]))
        y = inside + fade * mm(c_hi, local_ref[0, :, lanes]) + both(direct) * x
        gate = silu(g_ref[:, lanes])
        a_ref[:, lanes] = y * gate
        b_ref[:, lanes] = fade * jnp.exp(both(before_ref[0, 0:1, :])) * gate


def run_outputs(index, xc, cum, step, before, local_states, gate, direct, local):
    total, _ = xc.shape
    width = gate.shape[1]
    chunks = total // CHUNK
    per = local // CHUNK
    return pl.pallas_call(
        functools.partial(output_kernel, width, per),
        out_shape=(
            jax.ShapeDtypeStruct((total, width), F32),
            jax.ShapeDtypeStruct((total, width), F32),
            jax.ShapeDtypeStruct((total, STATE), BF16),
        ),
        grid_spec=pltpu.PrefetchScalarGridSpec(
            num_scalar_prefetch=1,
            grid=(chunks,),
            in_specs=[VMEM] * 7,
            out_specs=(VMEM,) * 3,
        ),
        cost_estimate=pl.CostEstimate(
            flops=2 * total * width * 1500, transcendentals=total * width * 4, bytes_accessed=16 * total * width
        ),
        compiler_params=pltpu.CompilerParams(
            dimension_semantics=("arbitrary",), vmem_limit_bytes=12 << 20
        ),
        name="run_outputs",
    )(index, xc, cum, step, before, local_states, gate, direct)


def pack_logs(wide):
    hi, mid, lo = split3(wide)
    row = lax.broadcasted_iota(jnp.int32, wide.shape, 0)
    lo = jnp.where(row == 2, lo.astype(F32), 0.0)
    return jnp.where(row == 0, hi.astype(F32), jnp.where(row == 1, mid.astype(F32), lo)).astype(BF16)


def unpack(got_ref):
    other = got_ref[0:STATE, :].astype(F32)
    logs = got_ref[STATE : STATE + 8, :].astype(F32)
    log = logs[0:1, :] + logs[1:2, :] + logs[2:3, :]
    return other, log


def combine_kernel(
    d, index_ref, got_ref, group_ref, glog_ref, prefix_ref, plog_ref,
    send_ref, group_out, glog_out, prefix_out, plog_out,
):
    upper = (index_ref[1] & d) != 0
    other, other_log = unpack(got_ref)
    group, group_log = group_ref[...], glog_ref[0:1, :]
    prefix, prefix_log = prefix_ref[...], plog_ref[0:1, :]
    prefix_out[...] = jnp.where(upper, prefix + jnp.exp(prefix_log) * other, prefix)
    new_plog = jnp.where(upper, prefix_log + other_log, prefix_log)
    plog_out[...] = jnp.broadcast_to(new_plog, plog_out.shape)
    late = jnp.where(upper, group, other)
    early = jnp.where(upper, other, group)
    late_log = jnp.where(upper, group_log, other_log)
    new = late + jnp.exp(late_log) * early
    new_log = jnp.broadcast_to(group_log + other_log, glog_out.shape)
    group_out[...] = new
    glog_out[...] = new_log
    send_ref[0:STATE, :] = new.astype(BF16)
    send_ref[STATE : STATE + 8, :] = pack_logs(new_log)


def combine(index, d, got, group, glog, prefix, plog):
    state = jax.ShapeDtypeStruct(group.shape, F32)
    log = jax.ShapeDtypeStruct(glog.shape, F32)
    full = lambda x: pl.BlockSpec(x.shape, lambda i, s: (0, 0))
    outs = (jax.ShapeDtypeStruct(got.shape, BF16), state, log, state, log)
    return pl.pallas_call(
        functools.partial(combine_kernel, d),
        out_shape=outs,
        grid_spec=pltpu.PrefetchScalarGridSpec(
            num_scalar_prefetch=1,
            grid=(1,),
            in_specs=[full(x) for x in (got, group, glog, prefix, plog)],
            out_specs=tuple(full(x) for x in outs),
        ),
        compiler_params=pltpu.CompilerParams(vmem_limit_bytes=8 << 20),
        name="combine",
    )(index, got, group, glog, prefix, plog)


def join_kernel(d, index_ref, a_ref, b_ref, c_ref, got_ref, prefix_ref, plog_ref, o_ref, ss_ref, s_scr):
    other, _ = unpack(got_ref)
    prefix = prefix_ref[...]
    upper = (index_ref[1] & d) != 0
    entering = jnp.where(upper, prefix + jnp.exp(plog_ref[0:1, :]) * other, prefix)
    s_scr[...] = entering.astype(BF16)

    part = 256
    ones = jnp.ones((8, 2 * o_ref.shape[1]), BF16)
    for at in range(0, o_ref.shape[0], part):
        rows = slice(at, at + part)
        gated = a_ref[rows, :] + b_ref[rows, :] * mm(c_ref[rows, :], s_scr[...])
        o_ref[rows, :] = gated
        hi, lo = split2(gated * gated)
        ss_ref[:, rows] = mm_nt(ones, jnp.concatenate([hi, lo], axis=1))[0:1]


def join(index, d, a, b, c, got, prefix, plog):
    total, width = a.shape
    return pl.pallas_call(
        functools.partial(join_kernel, d),
        out_shape=(jax.ShapeDtypeStruct((total, width), F32), jax.ShapeDtypeStruct((1, total), F32)),
        grid_spec=pltpu.PrefetchScalarGridSpec(
            num_scalar_prefetch=1,
            grid=(1,),
            in_specs=[VMEM] * 6,
            out_specs=(VMEM, VMEM),
            scratch_shapes=[pltpu.VMEM((STATE, width), BF16)],
        ),
        compiler_params=pltpu.CompilerParams(
            dimension_semantics=("arbitrary",), vmem_limit_bytes=10 << 20
        ),
        name="join",
    )(index, a, b, c, got, prefix, plog)


def norm_kernel(inner_width, g_ref, gain_ref, *refs):
    *squares_refs, o_ref = refs
    rows, width = o_ref.shape
    base = pl.program_id(0) * rows
    for part in range(rows // LANES):
        at = pl.multiple_of(base + part * LANES, LANES)
        squares = sum(r[:, pl.ds(at, LANES)] for r in squares_refs)
        scale = lax.rsqrt(squares / inner_width + 1e-05)
        column = jnp.broadcast_to(scale, (LANES, LANES)).T
        for lane in range(width // LANES):
            lanes = slice(lane * LANES, (lane + 1) * LANES)
            value = g_ref[pl.ds(at, LANES), lanes] * column * gain_ref[:, lanes]
            o_ref[part * LANES : (part + 1) * LANES, lanes] = value.astype(BF16)


def norm(gated, squares, gain, inner_width):
    total, width = gated.shape
    rows = 256
    return pl.pallas_call(
        functools.partial(norm_kernel, inner_width),
        out_shape=jax.ShapeDtypeStruct((total, width), BF16),
        grid=(total // rows,),
        in_specs=[VMEM] * (2 + len(squares)),
        out_specs=pl.BlockSpec((rows, width), lambda i: (i, 0)),
        compiler_params=pltpu.CompilerParams(
            dimension_semantics=("arbitrary",), vmem_limit_bytes=8 << 20
        ),
        name="norm",
    )(gated, gain, *squares)


def body(
    tokens,
    routes,
    gate_inner_weight,
    state_map_weight,
    step_size_weight,
    adapter_down_weight,
    adapter_up_weight,
    inner_conv_taps,
    state_map_taps,
    inner_conv_bias,
    state_map_conv_bias,
    step_size_bias,
    head_decay_rate,
    direct_head_scale,
    gated_norm_scale,
):
    n = lax.axis_size("exp")
    shards = lax.axis_size("seq")
    local, features = tokens.shape
    total = local * n
    width = gate_inner_weight.shape[2]
    experts = adapter_up_weight.shape[0]
    rank = 8
    e = lax.axis_index("exp")
    index = jnp.stack([e, lax.axis_index("seq")]).astype(jnp.int32)
    per = local // CHUNK

    down = {0: adapter_down_weight.T}
    for k in range(2, n, 2):
        down[k] = swap(down[0], "exp", k)
    *pieces, note = pack(tokens, routes.reshape(1, local), per)
    notes = {0: note}
    far = {}
    for k in range(2, n, 2):
        notes[k] = swap(note, "exp", k)
    for q in range(per):
        for k in range(2, n, 2):
            far[k, q] = swap(pieces[q], "exp", k)
    sibling = swap(tokens, "exp", 1)
    for k in range(0, n, 2):
        down[k + 1] = swap(down[k], "exp", 1)
        notes[k + 1] = swap(notes[k], "exp", 1)
    downs = [down[k] for k in range(n)]
    notes = [notes[k] for k in range(n)]
    wz = gate_inner_weight.reshape(features, 2 * width)
    up = adapter_up_weight.reshape(experts, 2 * width)
    call = functools.partial(
        project, index, notes=notes, wz=wz, wbc=state_map_weight, up=up, rank=rank
    )
    z, dt, lift, tails, rim, wsm = call(
        [tokens, sibling], route_from=((0, 0, local), (1, 0, local)),
        dt_t=step_size_weight.T, downs=downs,
    )
    gate = gate_project(index, [tokens, sibling], [lift], wz, up, n, total, 0, None)
    rim = lax.ppermute(rim, "seq", [(i, (i + 1) % shards) for i in range(shards)])
    params = [
        inner_conv_taps, state_map_taps, inner_conv_bias[None, :], state_map_conv_bias[None, :],
        step_size_bias[None, :], head_decay_rate[None, :],
    ]
    kept = run_states(index, total, z, dt, z, tails, rim, params, width, per, None, None)
    far_rows = {}
    for q in range(per):
        for k in range(2, n, 2):
            mine = far[k, q]
            other = swap(mine, "exp", 1)
            z, dt, lift = call(
                [mine, other],
                route_from=((k, q * CHUNK, CHUNK), (k + 1, q * CHUNK, CHUNK)),
                wsm=wsm,
            )
            far_rows[k, q] = (mine, other, z, lift)
            older = far_rows[k, max(q - 1, 0)][2]
            kept = run_states(
                index, total, z, dt, older, tails, rim, params, width, per, (k, q), kept
            )
    xc, cum, step, updates, totals = kept
    states, before, group, glog, send, prefix, plog = stitch(updates, totals)
    d = 1
    while True:
        got = swap(send, "seq", d)
        if 2 * d >= shards:
            break
        send, group, glog, prefix, plog = combine(index, d, got, group, glog, prefix, plog)
        d *= 2
    for k in range(2, n, 2):
        xs = [row for q in range(per) for row in far_rows[k, q][:2]]
        lifts = [far_rows[k, q][3] for q in range(per)]
        gate = gate_project(index, xs, lifts, wz, up, n, total, k // 2, gate)
    a, b, c = run_outputs(
        index, xc, cum, step, before, states, gate, direct_head_scale[None, :], local
    )
    gated, mine = join(index, d, a, b, c, got, prefix, plog)
    others = [swap(mine, "exp", k) for k in range(1, n)]
    return norm(gated, [mine, *others], gated_norm_scale[None, :], width * n)


def solution(mesh):
    in_specs = (
        P(("seq", "exp"), None),
        P(("seq", "exp"), None),
        P(None, None, "exp"),
        P(),
        P(None, "exp"),
        P(None, "exp"),
        P(None, None, "exp"),
        P(None, "exp"),
        P(),
        P("exp"),
        P(),
        P("exp"),
        P("exp"),
        P("exp"),
        P("exp"),
    )
    out_specs = P("seq", "exp")

    return jax.shard_map(body, mesh=mesh, in_specs=in_specs, out_specs=out_specs, check_vma=False)
```

```python
import functools

import jax
import jax.numpy as jnp
from jax import lax
from jax.experimental import pallas as pl
from jax.experimental.pallas import tpu as pltpu
from jax.sharding import PartitionSpec as P


STATE = 128
HEADDIM = 64
CHUNK = 128
LANES = 128
F32 = jnp.float32
BF16 = jnp.bfloat16


def swap(block, axis, mask):
    return lax.ppermute(block, axis, [(i, i ^ mask) for i in range(lax.axis_size(axis))])


def split3(value):
    hi = value.astype(BF16)
    rest = value - hi.astype(F32)
    mid = rest.astype(BF16)
    lo = (rest - mid.astype(F32)).astype(BF16)
    return hi, mid, lo


def split2(value):
    hi = value.astype(BF16)
    return hi, (value - hi.astype(F32)).astype(BF16)


def mm(a, b):
    return jnp.dot(a, b, preferred_element_type=F32)


def mm_nt(a, b):
    return lax.dot_general(a, b, (((1,), (1,)), ((), ())), preferred_element_type=F32)


def silu_of_double(half):
    return half + half * jnp.tanh(half)


def silu(v):
    return silu_of_double(0.5 * v)


def route_mask(e, route_row, experts_dev, rank):
    column = lax.broadcasted_iota(jnp.int32, (LANES, route_row.shape[1]), 0)
    per_dev = experts_dev * rank
    expert = ((column // per_dev) ^ e) * experts_dev + (column % per_dev) // rank
    return jnp.where(expert.astype(F32) == route_row, 1.0, 0.0)


VMEM = pl.BlockSpec(memory_space=pltpu.VMEM)


def up_rows(up_ref, e, devices, lanes):
    cols = up_ref.shape[0] // devices
    return jnp.concatenate(
        [up_ref[pl.ds(pl.multiple_of((e ^ r) * cols, cols), cols), lanes] for r in range(devices)], axis=0
    )


def pack_kernel(tokens_ref, route_ref, *refs):
    halves, (note_ref, tail, route, sems) = refs[:-4], refs[-4:]
    rows = halves[0].shape[0]
    copies = [
        pltpu.make_async_copy(tokens_ref.at[q * rows : (q + 1) * rows], half, sems.at[q])
        for q, half in enumerate(halves)
    ]
    last = tokens_ref.shape[0] - 8
    copies.append(pltpu.make_async_copy(tokens_ref.at[last:], tail, sems.at[len(halves)]))
    copies.append(pltpu.make_async_copy(route_ref, route, sems.at[len(halves) + 1]))
    for copy in copies[::-1]:
        copy.start()
    copies[-1].wait()
    copies[-2].wait()
    route = route[...].astype(F32)
    route = jnp.concatenate([route, jnp.zeros((1, tail.shape[1] - route.shape[1]), F32)], axis=1)
    row = lax.broadcasted_iota(jnp.int32, tail.shape, 0)
    note_ref[...] = jnp.where(row == 0, route, tail[...].astype(F32)).astype(BF16)
    for copy in copies[:-2]:
        copy.wait()


def pack(tokens, route_row, per):
    features = tokens.shape[1]
    anywhere = pl.BlockSpec(memory_space=pl.ANY)
    piece = jax.ShapeDtypeStruct((CHUNK, features), BF16)
    return pl.pallas_call(
        pack_kernel,
        out_shape=(piece,) * per + (jax.ShapeDtypeStruct((8, features), BF16),),
        in_specs=[anywhere, anywhere],
        out_specs=(VMEM,) * (per + 1),
        scratch_shapes=[
            pltpu.VMEM((8, features), BF16),
            pltpu.VMEM(route_row.shape, route_row.dtype),
            pltpu.SemaphoreType.DMA((per + 2,)),
        ],
        compiler_params=pltpu.CompilerParams(vmem_limit_bytes=4 << 20),
        name="pack",
    )(tokens, route_row)


def project_kernel(cfg, *refs):
    counts, route_from, devices, cols, rank, near = cfg
    x_refs, refs = refs[: len(counts)], refs[len(counts):]
    n_refs, refs = refs[:devices], refs[devices:]
    w_ref, wbc_ref, up_ref = refs[:3]
    refs = refs[3:]
    if near:
        dt_ref, d_refs, refs = refs[0], refs[1 : 1 + devices], refs[1 + devices:]
        z_ref, dto_ref, lift_ref, x_scr, tails_ref, rim_ref, wsm_ref, lift_scr = refs
    else:
        wsm_ref, z_ref, dto_ref, lift_ref, x_scr = refs
        lift_scr = lift_ref
    e = lax.axis_index("exp")
    rows = sum(counts)

    at = 0
    for x_ref, n in zip(x_refs, counts):
        x_scr[at : at + n, :] = x_ref[...]
        at += n
    if near:
        for r in range(devices):
            x_scr[at + 8 * r : at + 8 * r + 8, :] = n_refs[r][...]
        wsm_ref[LANES:, :] = jnp.zeros((wsm_ref.shape[0] - LANES, wsm_ref.shape[1]), BF16)
        wsm_ref[LANES : LANES + dt_ref.shape[0], :] = dt_ref[...]
        for r in range(devices):
            wsm_ref[r * cols : (r + 1) * cols, :] = d_refs[r][...]
    small = mm_nt(x_scr[...], wsm_ref[...])

    def mask_of(r, lane):
        row = n_refs[r][0:1, lane : lane + LANES].astype(F32)
        return route_mask(e, row, cols // rank, rank).T

    masks = []
    for r, first, n in route_from:
        for lane in range(first, first + n, LANES):
            masks.append(mask_of(r, lane))
    if near:
        last = route_from[0][1] + route_from[0][2] - LANES
        for r in range(devices):
            masks.append(mask_of(r, last)[LANES - 8 :, :])
    lift = jnp.where(jnp.concatenate(masks, axis=0) > 0.5, small[:, :LANES], 0.0).astype(BF16)
    lift_scr[...] = lift
    pad = jnp.zeros((rows, 2 * LANES - small.shape[1]), F32)
    dto_ref[...] = jnp.concatenate([small[:rows, LANES:], pad], axis=1)
    if near:
        lift_ref[...] = lift[:rows]

    def put(lanes, value):
        z_ref[:, lanes] = value[:rows]
        if near:
            tails_ref[:, lanes] = value[rows:]

    width = z_ref.shape[1]
    inner = up_ref.shape[1] // 2
    tn = 256 if inner % 256 == 0 else 128
    for at in range(0, inner, tn):
        lanes = slice(inner + at, inner + at + tn)
        up = up_rows(up_ref, e, devices, lanes)
        put(slice(at, at + tn), mm(x_scr[...], w_ref[:, lanes]) + mm(lift_scr[...], up))
    for at in range(0, width - inner, tn):
        put(slice(inner + at, inner + at + tn), mm(x_scr[...], wbc_ref[:, at : at + tn]))
    if near:
        row = ((devices - 1) ^ e) * 8
        rim_ref[...] = tails_ref[pl.ds(pl.multiple_of(row, 8), 8), :]


def project(xs, route_from, notes, wz, wbc, up, rank, dt_t=None, downs=None, wsm=None):
    counts = tuple(x.shape[0] for x in xs)
    rows = sum(counts)
    features = wz.shape[0]
    width = up.shape[1] // 2 + wbc.shape[1]
    devices = len(notes)
    near = wsm is None
    args = list(xs) + list(notes) + [wz, wbc, up]
    args += [dt_t, *downs] if near else [wsm]
    out_shape = [
        jax.ShapeDtypeStruct((rows, width), F32),
        jax.ShapeDtypeStruct((rows, LANES), F32),
        jax.ShapeDtypeStruct((rows, LANES), BF16),
    ]
    extra = 8 * devices if near else 0
    out_shape.append(jax.ShapeDtypeStruct((rows + extra, features), BF16))
    scratch = []
    if near:
        out_shape += [jax.ShapeDtypeStruct((extra, width), F32), jax.ShapeDtypeStruct((8, width), F32)]
        out_shape.append(jax.ShapeDtypeStruct((LANES + 16, features), BF16))
        scratch.append(pltpu.VMEM((rows + extra, LANES), BF16))
    cfg = (counts, route_from, devices, LANES // devices, rank, near)
    return pl.pallas_call(
        functools.partial(project_kernel, cfg),
        out_shape=tuple(out_shape),
        grid_spec=pltpu.PrefetchScalarGridSpec(
            num_scalar_prefetch=0,
            grid=(1,),
            in_specs=[VMEM] * len(args),
            out_specs=(VMEM,) * len(out_shape),
            scratch_shapes=scratch,
        ),
        cost_estimate=pl.CostEstimate(
            flops=2 * rows * features * (width + 256),
            transcendentals=0,
            bytes_accessed=2 * features * (width + rows) + 4 * rows * width,
        ),
        compiler_params=pltpu.CompilerParams(
            dimension_semantics=("arbitrary",), vmem_limit_bytes=16 << 20
        ),
        name="project",
    )(*args)


def gate_kernel(rows, devices, *refs):
    x_refs, lift_refs = refs[: len(rows)], refs[len(rows) : 2 * len(rows)]
    w_ref, up_ref, g_ref = refs[-3:]
    width = g_ref.shape[1]
    tn = 256 if width % 256 == 0 else 128
    for lane in range(0, width, tn):
        lanes = slice(lane, lane + tn)
        up = up_rows(up_ref, lax.axis_index("exp"), devices, lanes)
        at = 0
        for x_ref, lift_ref, n in zip(x_refs, lift_refs, rows):
            g_ref[at : at + n, lanes] = mm(x_ref[0:n, :], w_ref[:, lanes]) + mm(lift_ref[...], up)
            at += n


def gate_project(xs, lifts, wz, up, devices):
    counts = tuple(lift.shape[0] for lift in lifts)
    rows = sum(counts)
    features = wz.shape[0]
    width = up.shape[1] // 2
    args = list(xs) + list(lifts) + [wz, up]
    return pl.pallas_call(
        functools.partial(gate_kernel, counts, devices),
        out_shape=jax.ShapeDtypeStruct((rows, width), F32),
        in_specs=[VMEM] * len(args),
        out_specs=VMEM,
        cost_estimate=pl.CostEstimate(
            flops=2 * rows * features * width,
            transcendentals=0,
            bytes_accessed=2 * features * (width + rows) + 4 * rows * width,
        ),
        compiler_params=pltpu.CompilerParams(vmem_limit_bytes=12 << 20),
        name="gate_project",
    )(*args)


def spread(value, width):
    rows = value.shape[0]
    left = lax.broadcasted_iota(jnp.int32, (rows, LANES), 1) < HEADDIM
    parts = []
    for p in range(width // LANES):
        a = jnp.broadcast_to(value[:, 2 * p : 2 * p + 1], (rows, LANES))
        b = jnp.broadcast_to(value[:, 2 * p + 1 : 2 * p + 2], (rows, LANES))
        parts.append(jnp.where(left, a, b))
    return jnp.concatenate(parts, axis=1)


def pad_lanes(row):
    return jnp.concatenate([row, jnp.zeros((1, LANES - row.shape[1]), F32)], axis=1)


def state_kernel(
    cfg, z_all, d_all, older_all, tails_ref, rim_ref,
    taps_ref, mtaps_ref, bias_ref, mbias_ref, dtb_ref, rate_ref, *refs,
):
    width, per, far, where_am_i = cfg
    xc_all, cum_all, step_all, update_all, total_all, ext = refs[-6:]
    e = lax.axis_index("exp")
    r, q = where_am_i(pl.program_id(0))
    block = r ^ e
    at = pl.program_id(0) * CHUNK
    there = pl.ds(pl.multiple_of(at, CHUNK), CHUNK)
    z_ref, d_ref = z_all.at[there], d_all.at[there]
    older = at + CHUNK - 8 if far else jnp.maximum(at - 8, 0)
    prev_ref = older_all.at[pl.ds(pl.multiple_of(older, 8), 8)]
    chunk = block * per + q
    here = pl.ds(pl.multiple_of(chunk * CHUNK, CHUNK), CHUNK)
    xc_ref, cum_ref, step_ref = xc_all.at[here], cum_all.at[here], step_all.at[here]
    update_ref, total_ref = update_all.at[pl.ds(chunk, 1)], total_all.at[pl.ds(chunk, 1)]
    before = pl.multiple_of((jnp.maximum(block - 1, 0) ^ e) * 8, 8)
    rim = jnp.where(lax.axis_index("seq") == 0, 0.0, rim_ref[...])
    first = jnp.where(block == 0, rim, tails_ref[pl.ds(before, 8), :])
    ext[0:8, :] = jnp.where(q == 0, first, prev_ref[...])
    ext[8 : 8 + CHUNK, :] = z_ref[...]
    taps = taps_ref.shape[0]
    outs = []
    for tr, br, lanes in (
        (taps_ref, bias_ref, slice(0, width)),
        (mtaps_ref, mbias_ref, slice(width, width + 2 * STATE)),
    ):
        halved = 0.5 * tr[...]
        acc = 0.5 * br[...] + halved[taps - 1 : taps, :] * ext[8 : 8 + CHUNK, lanes]
        for k in range(taps - 1):
            start = 8 - (taps - 1) + k
            acc = acc + halved[k : k + 1, :] * ext[start : start + CHUNK, lanes]
        out = silu_of_double(acc)
        xc_ref[:, lanes] = out
        outs.append(out)
    x, maps = outs

    raw = d_ref[...] + pad_lanes(dtb_ref[...])
    step = jnp.maximum(raw, 0.0) + jnp.log1p(jnp.exp(-jnp.abs(raw)))
    decay = -pad_lanes(rate_ref[...]) * step
    rows = lax.broadcasted_iota(jnp.int32, (CHUNK, CHUNK), 0)
    cols = lax.broadcasted_iota(jnp.int32, (CHUNK, CHUNK), 1)
    lower = jnp.where(rows >= cols, 1.0, 0.0).astype(BF16)
    sums = mm(lower, jnp.concatenate(split3(decay), axis=1))
    cum = sums[:, :LANES] + sums[:, LANES : 2 * LANES] + sums[:, 2 * LANES :]
    total = cum[CHUNK - 1 : CHUNK, :]
    cum_ref[...] = cum
    step_ref[...] = step
    total_ref[0] = jnp.broadcast_to(total, total_ref.shape[1:])

    xs = (spread(jnp.exp(total - cum) * step, width) * x).astype(BF16)
    b_hi, b_lo = split2(maps[:, :STATE].T)
    update_ref[0] = mm(jnp.concatenate([b_hi, b_lo], axis=1), jnp.concatenate([xs, xs], axis=0))


def run_states(total, z, dt, older, tails, rim, params, width, per, far, buffers):
    wide = z.shape[1]
    chunks = total // CHUNK
    if far is None:
        steps = 2 * per
        at = lambda c: (c // per, c % per)
    else:
        steps = 2
        at = lambda c: (far[0] + c, far[1])

    args = [z, dt, older, tails, rim, *params]
    in_specs = [VMEM] * len(args)
    aliases = {}
    if buffers is not None:
        for n, buffer in enumerate(buffers):
            aliases[len(args)] = n
            args.append(buffer)
            in_specs.append(VMEM)
    return pl.pallas_call(
        functools.partial(state_kernel, (width, per, far is not None, at)),
        out_shape=(
            jax.ShapeDtypeStruct((total, wide), F32),
            jax.ShapeDtypeStruct((total, LANES), F32),
            jax.ShapeDtypeStruct((total, LANES), F32),
            jax.ShapeDtypeStruct((chunks, STATE, width), F32),
            jax.ShapeDtypeStruct((chunks, 8, LANES), F32),
        ),
        grid_spec=pltpu.PrefetchScalarGridSpec(
            num_scalar_prefetch=0,
            grid=(steps,),
            in_specs=in_specs,
            out_specs=(VMEM,) * 5,
            scratch_shapes=[pltpu.VMEM((CHUNK + 8, wide), F32)],
        ),
        input_output_aliases=aliases,
        cost_estimate=pl.CostEstimate(
            flops=2 * steps * CHUNK * width * 1000, transcendentals=steps * CHUNK * wide,
            bytes_accessed=12 * steps * CHUNK * wide,
        ),
        compiler_params=pltpu.CompilerParams(
            dimension_semantics=("arbitrary",), vmem_limit_bytes=12 << 20
        ),
        name="run_states",
    )(*args)


def part_lanes(width):
    middle = (width // LANES + 1) // 2 * LANES
    return [slice(0, middle), slice(middle, width)]


def stitch_kernel(width, update_ref, total_ref, entry_ref, before_ref, *refs):
    chunks = update_ref.shape[0]
    state = jnp.zeros(update_ref.shape[1:], F32)
    log = jnp.zeros(total_ref.shape[1:], F32)
    for c in range(chunks):
        entry_ref[c] = state.astype(BF16)
        before_ref[c] = log
        total = total_ref[c]
        state = spread(jnp.exp(total), width)[0:1, :] * state + update_ref[c]
        log = log + total
    wide = spread(log, width)
    for p, lanes in enumerate(part_lanes(width)):
        send_ref, group_ref, glog_ref, prefix_ref, plog_ref = refs[5 * p : 5 * p + 5]
        group_ref[...] = state[:, lanes]
        glog_ref[...] = wide[:, lanes]
        send_ref[0:STATE, :] = state[:, lanes].astype(BF16)
        send_ref[STATE : STATE + 8, :] = pack_logs(wide[:, lanes])
        prefix_ref[...] = jnp.zeros(prefix_ref.shape, F32)
        plog_ref[...] = jnp.zeros(plog_ref.shape, F32)


def stitch(updates, totals):
    _, state, width = updates.shape
    outs = [jax.ShapeDtypeStruct(updates.shape, BF16), jax.ShapeDtypeStruct(totals.shape, F32)]
    for lanes in part_lanes(width):
        wide = lanes.stop - lanes.start
        outs += [
            jax.ShapeDtypeStruct((state + 8, wide), BF16),
            jax.ShapeDtypeStruct((state, wide), F32),
            jax.ShapeDtypeStruct((8, wide), F32),
            jax.ShapeDtypeStruct((state, wide), F32),
            jax.ShapeDtypeStruct((8, wide), F32),
        ]
    entry, before, *rest = pl.pallas_call(
        functools.partial(stitch_kernel, width),
        out_shape=tuple(outs),
        in_specs=[VMEM, VMEM],
        out_specs=(VMEM,) * len(outs),
        compiler_params=pltpu.CompilerParams(vmem_limit_bytes=8 << 20),
        name="stitch",
    )(updates, totals)
    return entry, before, [rest[:5], rest[5:]]


def output_kernel(
    width, per, xc_all, cum_all, step_all, before_all, local_all, direct_ref, *refs,
):
    g_refs, (a_all, b_all, c_all) = refs[:-3], refs[-3:]
    c = pl.program_id(0)
    here = pl.ds(pl.multiple_of(c * CHUNK, CHUNK), CHUNK)
    r, q = (c // per) ^ lax.axis_index("exp"), c % per
    piece = jnp.where(r < 2, r * per + q, q * 2 + r % 2)
    there = pl.ds(pl.multiple_of(piece * CHUNK, CHUNK), CHUNK)
    xc_ref, cum_ref, step_ref = xc_all.at[here], cum_all.at[here], step_all.at[here]
    before_ref, local_ref = before_all.at[pl.ds(c, 1)], local_all.at[pl.ds(c, 1)]
    a_ref, b_ref, c_ref = a_all.at[here], b_all.at[here], c_all.at[here]
    bmap = xc_ref[:, width : width + STATE]
    cmap = xc_ref[:, width + STATE :]
    cum = cum_ref[...]
    b_hi, b_lo = split2(bmap)
    c_hi, c_lo = split2(cmap)
    c_ref[...] = c_hi
    gram = mm_nt(jnp.concatenate([c_hi, c_lo], axis=1), jnp.concatenate([b_hi, b_hi], axis=1))
    gram = gram + mm_nt(c_hi, b_lo)
    cum_t = cum.T
    step_t = step_ref[...].T
    rows = lax.broadcasted_iota(jnp.int32, (CHUNK, CHUNK), 0)
    cols = lax.broadcasted_iota(jnp.int32, (CHUNK, CHUNK), 1)
    causal = rows >= cols
    left = cols < HEADDIM
    direct = pad_lanes(direct_ref[...])
    for p in range(width // LANES):
        lanes = slice(p * LANES, (p + 1) * LANES)
        ws, cs = [], []
        for h in (2 * p, 2 * p + 1):
            column = jnp.broadcast_to(cum[:, h : h + 1], (CHUNK, CHUNK))
            differ = jnp.where(causal, column - cum_t[h : h + 1, :], -jnp.inf)
            ws.append((jnp.exp(differ) * (gram * step_t[h : h + 1, :])).astype(BF16))
            cs.append(column)
        x = xc_ref[:, lanes]
        xb = jnp.concatenate([jnp.where(left, x, 0.0), jnp.where(left, 0.0, x)], axis=0)
        both = lambda v: jnp.where(
            left[0:1, :],
            jnp.broadcast_to(v[:, 2 * p : 2 * p + 1], (1, LANES)),
            jnp.broadcast_to(v[:, 2 * p + 1 : 2 * p + 2], (1, LANES)),
        )
        inside = mm(jnp.concatenate(ws, axis=1), xb.astype(BF16))
        fade = jnp.exp(jnp.where(left, cs[0], cs[1]))
        y = inside + fade * mm(c_hi, local_ref[0, :, lanes]) + both(direct) * x
        gate = g_refs[0][there, lanes]
        for k, g_ref in enumerate(g_refs[1:]):
            gate = jnp.where(r // 2 == k + 1, g_ref[there, lanes], gate)
        gate = silu(gate)
        a_ref[:, lanes] = y * gate
        b_ref[:, lanes] = fade * jnp.exp(both(before_ref[0, 0:1, :])) * gate


def run_outputs(xc, cum, step, before, local_states, gates, direct, local):
    total, _ = xc.shape
    width = gates[0].shape[1]
    chunks = total // CHUNK
    per = local // CHUNK
    return pl.pallas_call(
        functools.partial(output_kernel, width, per),
        out_shape=(
            jax.ShapeDtypeStruct((total, width), F32),
            jax.ShapeDtypeStruct((total, width), F32),
            jax.ShapeDtypeStruct((total, STATE), BF16),
        ),
        grid_spec=pltpu.PrefetchScalarGridSpec(
            num_scalar_prefetch=0,
            grid=(chunks,),
            in_specs=[VMEM] * (6 + len(gates)),
            out_specs=(VMEM,) * 3,
        ),
        cost_estimate=pl.CostEstimate(
            flops=2 * total * width * 1500, transcendentals=total * width * 4, bytes_accessed=16 * total * width
        ),
        compiler_params=pltpu.CompilerParams(
            dimension_semantics=("arbitrary",), vmem_limit_bytes=12 << 20
        ),
        name="run_outputs",
    )(xc, cum, step, before, local_states, direct, *gates)


def pack_logs(wide):
    hi, mid, lo = split3(wide)
    row = lax.broadcasted_iota(jnp.int32, wide.shape, 0)
    lo = jnp.where(row == 2, lo.astype(F32), 0.0)
    return jnp.where(row == 0, hi.astype(F32), jnp.where(row == 1, mid.astype(F32), lo)).astype(BF16)


def unpack(got_ref):
    other = got_ref[0:STATE, :].astype(F32)
    logs = got_ref[STATE : STATE + 8, :].astype(F32)
    log = logs[0:1, :] + logs[1:2, :] + logs[2:3, :]
    return other, log


def combine_kernel(
    d, radix, *refs,
):
    got_refs, refs = refs[: radix - 1], refs[radix - 1 :]
    group_ref, glog_ref, prefix_ref, plog_ref = refs[:4]
    send_ref, group_out, glog_out, prefix_out, plog_out, states, logs = refs[4:]
    mine = (lax.axis_index("seq") // d) % radix
    states[0] = group_ref[...]
    logs[0] = glog_ref[...]
    for k, got_ref in enumerate(got_refs):
        other, other_log = unpack(got_ref)
        states[k + 1] = other
        logs[k + 1] = jnp.broadcast_to(other_log, logs.shape[1:])
    total = jnp.zeros(group_ref.shape, F32)
    total_log = jnp.zeros((1, total.shape[1]), F32)
    early, early_log = total, total_log
    for m in range(radix):
        state = states[pl.ds(m ^ mine, 1)][0]
        log = logs[pl.ds(m ^ mine, 1)][0, 0:1]
        if m:
            early = jnp.where(mine == m, total, early)
            early_log = jnp.where(mine == m, total_log, early_log)
            state = jnp.exp(log) * total + state
        total = state
        total_log = total_log + log
    prefix_log = plog_ref[0:1, :]
    prefix_out[...] = prefix_ref[...] + jnp.exp(prefix_log) * early
    plog_out[...] = jnp.broadcast_to(prefix_log + early_log, plog_out.shape)
    new_log = jnp.broadcast_to(total_log, glog_out.shape)
    group_out[...] = total
    glog_out[...] = new_log
    send_ref[0:STATE, :] = total.astype(BF16)
    send_ref[STATE : STATE + 8, :] = pack_logs(new_log)


def combine(d, got, group, glog, prefix, plog):
    radix = len(got) + 1
    state = jax.ShapeDtypeStruct(group.shape, F32)
    log = jax.ShapeDtypeStruct(glog.shape, F32)
    return pl.pallas_call(
        functools.partial(combine_kernel, d, radix),
        out_shape=(jax.ShapeDtypeStruct(got[0].shape, BF16), state, log, state, log),
        grid_spec=pltpu.PrefetchScalarGridSpec(
            num_scalar_prefetch=0,
            grid=(1,),
            in_specs=[VMEM] * (radix + 3),
            out_specs=(VMEM,) * 5,
            scratch_shapes=[
                pltpu.VMEM((radix, *group.shape), F32),
                pltpu.VMEM((radix, *glog.shape), F32),
            ],
        ),
        compiler_params=pltpu.CompilerParams(vmem_limit_bytes=8 << 20),
        name="combine",
    )(*got, group, glog, prefix, plog)


def join_kernel(d, a_ref, b_ref, c_ref, *refs):
    o_ref, ss_ref, s_scr = refs[-3:]
    upper = (lax.axis_index("seq") & d) != 0
    for p, lanes in enumerate(part_lanes(o_ref.shape[1])):
        got_ref, prefix_ref, plog_ref = refs[3 * p : 3 * p + 3]
        other, _ = unpack(got_ref)
        prefix = prefix_ref[...]
        entering = jnp.where(upper, prefix + jnp.exp(plog_ref[0:1, :]) * other, prefix)
        s_scr[:, lanes] = entering.astype(BF16)

    part = 256
    ones = jnp.ones((8, 2 * o_ref.shape[1]), BF16)
    for at in range(0, o_ref.shape[0], part):
        rows = slice(at, at + part)
        gated = a_ref[rows, :] + b_ref[rows, :] * mm(c_ref[rows, :], s_scr[...])
        o_ref[rows, :] = gated
        hi, lo = split2(gated * gated)
        ss_ref[:, rows] = mm_nt(ones, jnp.concatenate([hi, lo], axis=1))[0:1]


def join(d, a, b, c, entering):
    total, width = a.shape
    return pl.pallas_call(
        functools.partial(join_kernel, d),
        out_shape=(jax.ShapeDtypeStruct((total, width), F32), jax.ShapeDtypeStruct((1, total), F32)),
        grid_spec=pltpu.PrefetchScalarGridSpec(
            num_scalar_prefetch=0,
            grid=(1,),
            in_specs=[VMEM] * (3 + len(entering)),
            out_specs=(VMEM, VMEM),
            scratch_shapes=[pltpu.VMEM((STATE, width), BF16)],
        ),
        compiler_params=pltpu.CompilerParams(
            dimension_semantics=("arbitrary",), vmem_limit_bytes=10 << 20
        ),
        name="join",
    )(a, b, c, *entering)


def norm_kernel(inner_width, g_ref, gain_ref, *refs):
    *squares_refs, o_ref = refs
    rows, width = o_ref.shape
    base = pl.program_id(0) * rows
    for part in range(rows // LANES):
        at = pl.multiple_of(base + part * LANES, LANES)
        squares = sum(r[:, pl.ds(at, LANES)] for r in squares_refs)
        scale = lax.rsqrt(squares / inner_width + 1e-05)
        column = jnp.broadcast_to(scale, (LANES, LANES)).T
        for lane in range(width // LANES):
            lanes = slice(lane * LANES, (lane + 1) * LANES)
            value = g_ref[pl.ds(at, LANES), lanes] * column * gain_ref[:, lanes]
            o_ref[part * LANES : (part + 1) * LANES, lanes] = value.astype(BF16)


def norm(gated, squares, gain, inner_width):
    total, width = gated.shape
    rows = 256
    return pl.pallas_call(
        functools.partial(norm_kernel, inner_width),
        out_shape=jax.ShapeDtypeStruct((total, width), BF16),
        grid=(total // rows,),
        in_specs=[VMEM] * (2 + len(squares)),
        out_specs=pl.BlockSpec((rows, width), lambda i: (i, 0)),
        compiler_params=pltpu.CompilerParams(
            dimension_semantics=("arbitrary",), vmem_limit_bytes=8 << 20
        ),
        name="norm",
    )(gated, gain, *squares)


def stages(shards):
    out, d = [], 1
    while d < shards:
        radix = 4 if 8 * d <= shards else 2
        out.append((d, radix))
        d *= radix
    return out


def body(
    tokens,
    routes,
    gate_inner_weight,
    state_map_weight,
    step_size_weight,
    adapter_down_weight,
    adapter_up_weight,
    inner_conv_taps,
    state_map_taps,
    inner_conv_bias,
    state_map_conv_bias,
    step_size_bias,
    head_decay_rate,
    direct_head_scale,
    gated_norm_scale,
):
    n = lax.axis_size("exp")
    shards = lax.axis_size("seq")
    local, features = tokens.shape
    total = local * n
    width = gate_inner_weight.shape[2]
    experts = adapter_up_weight.shape[0]
    rank = 8
    per = local // CHUNK

    down = {0: adapter_down_weight.T}
    for k in range(2, n, 2):
        down[k] = swap(down[0], "exp", k)
    *pieces, note = pack(tokens, routes.reshape(1, local), per)
    notes = {0: note}
    far = {}
    for k in range(2, n, 2):
        notes[k] = swap(note, "exp", k)
    for q in range(per):
        for k in range(2, n, 2):
            far[k, q] = swap(pieces[q], "exp", k)
    sibling = swap(tokens, "exp", 1)
    for k in range(0, n, 2):
        down[k + 1] = swap(down[k], "exp", 1)
        notes[k + 1] = swap(notes[k], "exp", 1)
    downs = [down[k] for k in range(n)]
    notes = [notes[k] for k in range(n)]
    wz = gate_inner_weight.reshape(features, 2 * width)
    up = adapter_up_weight.reshape(experts, 2 * width)
    call = functools.partial(
        project, notes=notes, wz=wz, wbc=state_map_weight, up=up, rank=rank
    )
    z, dt, lift, rows, tails, rim, wsm = call(
        [tokens, sibling], route_from=((0, 0, local), (1, 0, local)),
        dt_t=step_size_weight.T, downs=downs,
    )
    gates = [gate_project([rows], [lift], wz, up, n)]
    rim = lax.ppermute(rim, "seq", [(i, (i + 1) % shards) for i in range(shards)])
    params = [
        inner_conv_taps, state_map_taps, inner_conv_bias[None, :], state_map_conv_bias[None, :],
        step_size_bias[None, :], head_decay_rate[None, :],
    ]
    kept = run_states(total, z, dt, z, tails, rim, params, width, per, None, None)
    far_rows = {}
    for q in range(per):
        for k in range(2, n, 2):
            mine = far[k, q]
            other = swap(mine, "exp", 1)
            z, dt, lift, rows = call(
                [mine, other],
                route_from=((k, q * CHUNK, CHUNK), (k + 1, q * CHUNK, CHUNK)),
                wsm=wsm,
            )
            far_rows[k, q] = (rows, lift, z)
            older = far_rows[k, max(q - 1, 0)][2]
            kept = run_states(
                total, z, dt, older, tails, rim, params, width, per, (k, q), kept
            )
    xc, cum, step, updates, totals = kept
    states, before, parts = stitch(updates, totals)
    for d, radix in stages(shards):
        last = 2 * d == shards
        got = {}
        for p, part in enumerate(parts):
            for k in range(1, radix):
                got[p, k] = swap(part[0], "seq", d * k)
        for p, part in enumerate(parts):
            arrived = [got[p, k] for k in range(1, radix)]
            if last:
                parts[p] = [arrived[0], *part[3:]]
            else:
                parts[p] = combine(d, arrived, *part[1:])
    entering = [x for part in parts for x in part]
    for k in range(2, n, 2):
        xs = [far_rows[k, q][0] for q in range(per)]
        lifts = [far_rows[k, q][1] for q in range(per)]
        gates.append(gate_project(xs, lifts, wz, up, n))
    a, b, c = run_outputs(xc, cum, step, before, states, gates, direct_head_scale[None, :], local)
    gated, mine = join(shards // 2, a, b, c, entering)
    others = [swap(mine, "exp", k) for k in range(1, n)]
    return norm(gated, [mine, *others], gated_norm_scale[None, :], width * n)


def solution(mesh):
    in_specs = (
        P(("seq", "exp"), None),
        P(("seq", "exp"), None),
        P(None, None, "exp"),
        P(),
        P(None, "exp"),
        P(None, "exp"),
        P(None, None, "exp"),
        P(None, "exp"),
        P(),
        P("exp"),
        P(),
        P("exp"),
        P("exp"),
        P("exp"),
        P("exp"),
    )
    out_specs = P("seq", "exp")

    return jax.shard_map(body, mesh=mesh, in_specs=in_specs, out_specs=out_specs, check_vma=False)
```

```python
import functools

import jax
import jax.numpy as jnp
from jax import lax
from jax.experimental import pallas as pl
from jax.experimental.pallas import tpu as pltpu
from jax.sharding import PartitionSpec as P


STATE = 128
HEADDIM = 64
CHUNK = 128
HEADS_PAD = 16
LANES = 128
F32 = jnp.float32
BF16 = jnp.bfloat16


def swap(block, axis, mask):
    return lax.ppermute(block, axis, [(i, i ^ mask) for i in range(lax.axis_size(axis))])


def split3(value):
    hi = value.astype(BF16)
    rest = value - hi.astype(F32)
    mid = rest.astype(BF16)
    lo = (rest - mid.astype(F32)).astype(BF16)
    return hi, mid, lo


def split2(value):
    hi = value.astype(BF16)
    return hi, (value - hi.astype(F32)).astype(BF16)


def mm(a, b):
    return jnp.dot(a, b, preferred_element_type=F32)


def mm_nt(a, b):
    return lax.dot_general(a, b, (((1,), (1,)), ((), ())), preferred_element_type=F32)


def silu_of_double(half):
    return half + half * jnp.tanh(half)


def silu(v):
    return silu_of_double(0.5 * v)


def route_mask(e, route_row, experts_dev, rank):
    column = lax.broadcasted_iota(jnp.int32, (LANES, route_row.shape[1]), 0)
    per_dev = experts_dev * rank
    expert = ((column // per_dev) ^ e) * experts_dev + (column % per_dev) // rank
    return jnp.where(expert.astype(F32) == route_row, 1.0, 0.0)


VMEM = pl.BlockSpec(memory_space=pltpu.VMEM)


def up_rows(up_ref, e, devices, lanes):
    cols = up_ref.shape[0] // devices
    return jnp.concatenate(
        [up_ref[pl.ds(pl.multiple_of((e ^ r) * cols, cols), cols), lanes] for r in range(devices)], axis=0
    )


def pack_kernel(tokens_ref, route_ref, *refs):
    halves, (note_ref, tail, route, sems) = refs[:-4], refs[-4:]
    rows = halves[0].shape[0]
    copies = [
        pltpu.make_async_copy(tokens_ref.at[q * rows : (q + 1) * rows], half, sems.at[q])
        for q, half in enumerate(halves)
    ]
    last = tokens_ref.shape[0] - 8
    copies.append(pltpu.make_async_copy(tokens_ref.at[last:], tail, sems.at[len(halves)]))
    copies.append(pltpu.make_async_copy(route_ref, route, sems.at[len(halves) + 1]))
    for copy in copies[::-1]:
        copy.start()
    copies[-1].wait()
    copies[-2].wait()
    route = route[...].astype(F32)
    route = jnp.concatenate([route, jnp.zeros((1, tail.shape[1] - route.shape[1]), F32)], axis=1)
    row = lax.broadcasted_iota(jnp.int32, tail.shape, 0)
    note_ref[...] = jnp.where(row == 0, route, tail[...].astype(F32)).astype(BF16)
    for copy in copies[:-2]:
        copy.wait()


def pack(tokens, route_row, per):
    features = tokens.shape[1]
    anywhere = pl.BlockSpec(memory_space=pl.ANY)
    piece = jax.ShapeDtypeStruct((CHUNK, features), BF16)
    return pl.pallas_call(
        pack_kernel,
        out_shape=(piece,) * per + (jax.ShapeDtypeStruct((8, features), BF16),),
        in_specs=[anywhere, anywhere],
        out_specs=(VMEM,) * (per + 1),
        scratch_shapes=[
            pltpu.VMEM((8, features), BF16),
            pltpu.VMEM(route_row.shape, route_row.dtype),
            pltpu.SemaphoreType.DMA((per + 2,)),
        ],
        compiler_params=pltpu.CompilerParams(vmem_limit_bytes=4 << 20),
        name="pack",
    )(tokens, route_row)


def pad_lanes(row):
    pad = LANES - row.shape[1]
    return jnp.concatenate([row, jnp.zeros((row.shape[0], pad), F32)], axis=1)


def step_chain(raw, bias, rate):
    column = lambda row: jnp.broadcast_to(pad_lanes(row), (LANES, LANES)).T[:HEADS_PAD]
    raw = pad_lanes(raw).T[:HEADS_PAD] + column(bias)
    step = jnp.maximum(raw, 0.0) + jnp.log1p(jnp.exp(-jnp.abs(raw)))
    decay = -column(rate) * step
    rows = lax.broadcasted_iota(jnp.int32, (CHUNK, CHUNK), 0)
    cols = lax.broadcasted_iota(jnp.int32, (CHUNK, CHUNK), 1)
    upper = jnp.where(rows <= cols, 1.0, 0.0).astype(BF16)
    sums = mm(jnp.concatenate(split3(decay), axis=0), upper)
    cum_t = sums[:HEADS_PAD] + sums[HEADS_PAD : 2 * HEADS_PAD] + sums[2 * HEADS_PAD :]
    carried = jnp.exp(jnp.broadcast_to(cum_t[:, CHUNK - 1 :], cum_t.shape) - cum_t) * step
    blank = jnp.zeros((LANES - 2 * HEADS_PAD, CHUNK), F32)
    return jnp.concatenate([cum_t, carried, blank], axis=0).T, cum_t, step


def project_kernel(cfg, *refs):
    counts, route_from, devices, cols, rank, near = cfg
    x_refs, refs = refs[: len(counts)], refs[len(counts):]
    if near:
        n_refs, refs = refs[:devices], refs[devices:]
    else:
        route_ref, refs = refs[0], refs[1:]
    w_ref, wbc_ref, up_ref, dtb_ref, rate_ref = refs[:5]
    refs = refs[5:]
    if near:
        dt_ref, d_refs, refs = refs[0], refs[1 : 1 + devices], refs[1 + devices:]
        z_ref, cum_ref, cum_t_ref, step_t_ref, lift_ref, x_scr, tails_ref, rim_ref, wsm_ref, route_ref, lift_scr = refs
    else:
        wsm_ref, z_ref, cum_ref, cum_t_ref, step_t_ref, lift_ref, x_scr = refs
        lift_scr = lift_ref
    e = lax.axis_index("exp")
    rows = sum(counts)

    at = 0
    for x_ref, n in zip(x_refs, counts):
        x_scr[at : at + n, :] = x_ref[...]
        at += n
    if near:
        for r in range(devices):
            x_scr[at + 8 * r : at + 8 * r + 8, :] = n_refs[r][...]
        wsm_ref[LANES:, :] = jnp.zeros((wsm_ref.shape[0] - LANES, wsm_ref.shape[1]), BF16)
        wsm_ref[LANES : LANES + dt_ref.shape[0], :] = dt_ref[...]
        for r in range(devices):
            wsm_ref[r * cols : (r + 1) * cols, :] = d_refs[r][...]
    small = mm_nt(x_scr[...], wsm_ref[...])

    def mask_of(r, lane):
        row = n_refs[r][0:1, lane : lane + LANES].astype(F32)
        return route_mask(e, row, cols // rank, rank).T

    masks = []
    if near:
        whole = route_ref.shape[0] // devices
        for r in range(devices):
            for lane in range(0, whole, LANES):
                mask = mask_of(r, lane)
                route_ref[r * whole + lane : r * whole + lane + LANES, :] = mask.astype(BF16)
                if r < 2:
                    masks.append(mask)
        for r in range(devices):
            masks.append(route_ref[(r + 1) * whole - 16 : (r + 1) * whole, :].astype(F32)[8:])
    else:
        masks = [route_ref[first : first + n, :].astype(F32) for first, n in route_from]
    lift = jnp.where(jnp.concatenate(masks, axis=0) > 0.5, small[:, :LANES], 0.0).astype(BF16)
    lift_scr[...] = lift
    for c in range(rows // CHUNK):
        here = slice(c * CHUNK, (c + 1) * CHUNK)
        both, cum_t, step_t = step_chain(small[here, LANES:], dtb_ref[...], rate_ref[...])
        cum_ref[here, :] = both
        cum_t_ref[c] = cum_t
        step_t_ref[c] = step_t
    if near:
        lift_ref[...] = lift[:rows]

    def put(lanes, value):
        z_ref[:, lanes] = value[:rows]
        if near:
            tails_ref[:, lanes] = value[rows:]

    width = z_ref.shape[1]
    inner = up_ref.shape[1] // 2
    tn = 256 if inner % 256 == 0 else 128
    for at in range(0, inner, tn):
        lanes = slice(inner + at, inner + at + tn)
        up = up_rows(up_ref, e, devices, lanes)
        put(slice(at, at + tn), mm(x_scr[...], w_ref[:, lanes]) + mm(lift_scr[...], up))
    for at in range(0, width - inner, tn):
        put(slice(inner + at, inner + at + tn), mm(x_scr[...], wbc_ref[:, at : at + tn]))
    if near:
        row = ((devices - 1) ^ e) * 8
        rim_ref[...] = tails_ref[pl.ds(pl.multiple_of(row, 8), 8), :]


def project(xs, wz, wbc, up, dtb, rate, rank, devices, notes=None, dt_t=None, downs=None, route_from=None, routes=None, wsm=None):
    counts = tuple(x.shape[0] for x in xs)
    rows = sum(counts)
    features = wz.shape[0]
    width = up.shape[1] // 2 + wbc.shape[1]
    near = wsm is None
    args = list(xs) + (list(notes) if near else [routes]) + [wz, wbc, up, dtb, rate]
    args += [dt_t, *downs] if near else [wsm]
    out_shape = [
        jax.ShapeDtypeStruct((rows, width), F32),
        jax.ShapeDtypeStruct((rows, LANES), F32),
        jax.ShapeDtypeStruct((rows // CHUNK, HEADS_PAD, CHUNK), F32),
        jax.ShapeDtypeStruct((rows // CHUNK, HEADS_PAD, CHUNK), F32),
        jax.ShapeDtypeStruct((rows, LANES), BF16),
    ]
    extra = 8 * devices if near else 0
    out_shape.append(jax.ShapeDtypeStruct((rows + extra, features), BF16))
    scratch = []
    if near:
        out_shape += [jax.ShapeDtypeStruct((extra, width), F32), jax.ShapeDtypeStruct((8, width), F32)]
        out_shape.append(jax.ShapeDtypeStruct((LANES + 16, features), BF16))
        out_shape.append(jax.ShapeDtypeStruct((devices * counts[0], LANES), BF16))
        scratch.append(pltpu.VMEM((rows + extra, LANES), BF16))
    cfg = (counts, route_from, devices, LANES // devices, rank, near)
    return pl.pallas_call(
        functools.partial(project_kernel, cfg),
        out_shape=tuple(out_shape),
        grid_spec=pltpu.PrefetchScalarGridSpec(
            num_scalar_prefetch=0,
            grid=(1,),
            in_specs=[VMEM] * len(args),
            out_specs=(VMEM,) * len(out_shape),
            scratch_shapes=scratch,
        ),
        cost_estimate=pl.CostEstimate(
            flops=2 * rows * features * (width + 256),
            transcendentals=0,
            bytes_accessed=2 * features * (width + rows) + 4 * rows * width,
        ),
        compiler_params=pltpu.CompilerParams(
            dimension_semantics=("arbitrary",), vmem_limit_bytes=16 << 20
        ),
        name="project",
    )(*args)


def gate_kernel(rows, devices, *refs):
    x_refs, lift_refs = refs[: len(rows)], refs[len(rows) : 2 * len(rows)]
    w_ref, up_ref, g_ref = refs[-3:]
    width = g_ref.shape[1]
    tn = 256 if width % 256 == 0 else 128
    for lane in range(0, width, tn):
        lanes = slice(lane, lane + tn)
        up = up_rows(up_ref, lax.axis_index("exp"), devices, lanes)
        at = 0
        for x_ref, lift_ref, n in zip(x_refs, lift_refs, rows):
            g_ref[at : at + n, lanes] = mm(x_ref[0:n, :], w_ref[:, lanes]) + mm(lift_ref[...], up)
            at += n


def gate_project(xs, lifts, wz, up, devices):
    counts = tuple(lift.shape[0] for lift in lifts)
    rows = sum(counts)
    features = wz.shape[0]
    width = up.shape[1] // 2
    args = list(xs) + list(lifts) + [wz, up]
    return pl.pallas_call(
        functools.partial(gate_kernel, counts, devices),
        out_shape=jax.ShapeDtypeStruct((rows, width), F32),
        in_specs=[VMEM] * len(args),
        out_specs=VMEM,
        cost_estimate=pl.CostEstimate(
            flops=2 * rows * features * width,
            transcendentals=0,
            bytes_accessed=2 * features * (width + rows) + 4 * rows * width,
        ),
        compiler_params=pltpu.CompilerParams(vmem_limit_bytes=12 << 20),
        name="gate_project",
    )(*args)


def spread(value, width):
    rows = value.shape[0]
    left = lax.broadcasted_iota(jnp.int32, (rows, LANES), 1) < HEADDIM
    parts = []
    for p in range(width // LANES):
        a = jnp.broadcast_to(value[:, 2 * p : 2 * p + 1], (rows, LANES))
        b = jnp.broadcast_to(value[:, 2 * p + 1 : 2 * p + 2], (rows, LANES))
        parts.append(jnp.where(left, a, b))
    return jnp.concatenate(parts, axis=1)


def state_kernel(
    cfg, z_all, sums_all, sums_t_all, steps_t_all, older_all, tails_ref, rim_ref,
    taps_ref, mtaps_ref, bias_ref, mbias_ref, *refs,
):
    width, per, far, where_am_i = cfg
    xc_all, cum_all, cum_t_all, step_t_all, update_all, total_all, ext = refs[-7:]
    e = lax.axis_index("exp")
    r, q = where_am_i(pl.program_id(0))
    block = r ^ e
    at = pl.program_id(0) * CHUNK
    there = pl.ds(pl.multiple_of(at, CHUNK), CHUNK)
    z_ref = z_all.at[there]
    older = r % 2 * CHUNK + CHUNK - 8 if far else jnp.maximum(at - 8, 0)
    prev_ref = older_all.at[pl.ds(pl.multiple_of(older, 8), 8)]
    chunk = block * per + q
    here = pl.ds(pl.multiple_of(chunk * CHUNK, CHUNK), CHUNK)
    xc_ref, cum_ref = xc_all.at[here], cum_all.at[here]
    cum_t_ref, step_t_ref = cum_t_all.at[pl.ds(chunk, 1)], step_t_all.at[pl.ds(chunk, 1)]
    update_ref, total_ref = update_all.at[pl.ds(chunk, 1)], total_all.at[pl.ds(chunk, 1)]
    before = pl.multiple_of((jnp.maximum(block - 1, 0) ^ e) * 8, 8)
    rim = jnp.where(lax.axis_index("seq") == 0, 0.0, rim_ref[...])
    first = jnp.where(block == 0, rim, tails_ref[pl.ds(before, 8), :])
    ext[0:8, :] = jnp.where(q == 0, first, prev_ref[...])
    ext[8 : 8 + CHUNK, :] = z_ref[...]
    taps = taps_ref.shape[0]
    outs = []
    for tr, br, lanes in (
        (taps_ref, bias_ref, slice(0, width)),
        (mtaps_ref, mbias_ref, slice(width, width + 2 * STATE)),
    ):
        halved = 0.5 * tr[...]
        acc = 0.5 * br[...] + halved[taps - 1 : taps, :] * ext[8 : 8 + CHUNK, lanes]
        for k in range(taps - 1):
            start = 8 - (taps - 1) + k
            acc = acc + halved[k : k + 1, :] * ext[start : start + CHUNK, lanes]
        out = silu_of_double(acc)
        xc_ref[:, lanes] = out
        outs.append(out)
    x, maps = outs

    both = sums_all[there, :]
    cum_ref[...] = both
    cum_t_ref[0] = sums_t_all[pl.ds(pl.program_id(0), 1)][0]
    step_t_ref[0] = steps_t_all[pl.ds(pl.program_id(0), 1)][0]
    total_ref[0] = jnp.broadcast_to(both[CHUNK - 1 : CHUNK, :], total_ref.shape[1:])

    xs = (spread(both[:, HEADS_PAD:], width) * x).astype(BF16)
    b_hi, b_lo = split2(maps[:, :STATE].T)
    update_ref[0] = mm(jnp.concatenate([b_hi, b_lo], axis=1), jnp.concatenate([xs, xs], axis=0))


def run_states(total, z, sums, older, tails, rim, params, width, per, far, buffers):
    wide = z.shape[1]
    chunks = total // CHUNK
    if far is None:
        steps = 2 * per
        at = lambda c: (c // per, c % per)
    else:
        steps = z.shape[0] // CHUNK
        at = lambda c: (far[0] + c, far[1])

    args = [z, *sums, older, tails, rim, *params]
    in_specs = [VMEM] * len(args)
    aliases = {}
    if buffers is not None:
        for n, buffer in enumerate(buffers):
            aliases[len(args)] = n
            args.append(buffer)
            in_specs.append(VMEM)
    return pl.pallas_call(
        functools.partial(state_kernel, (width, per, far is not None, at)),
        out_shape=(
            jax.ShapeDtypeStruct((total, wide), F32),
            jax.ShapeDtypeStruct((total, LANES), F32),
            jax.ShapeDtypeStruct((chunks, HEADS_PAD, CHUNK), F32),
            jax.ShapeDtypeStruct((chunks, HEADS_PAD, CHUNK), F32),
            jax.ShapeDtypeStruct((chunks, STATE, width), F32),
            jax.ShapeDtypeStruct((chunks, 8, LANES), F32),
        ),
        grid_spec=pltpu.PrefetchScalarGridSpec(
            num_scalar_prefetch=0,
            grid=(steps,),
            in_specs=in_specs,
            out_specs=(VMEM,) * 6,
            scratch_shapes=[pltpu.VMEM((CHUNK + 8, wide), F32)],
        ),
        input_output_aliases=aliases,
        cost_estimate=pl.CostEstimate(
            flops=2 * steps * CHUNK * width * 1000, transcendentals=steps * CHUNK * wide,
            bytes_accessed=12 * steps * CHUNK * wide,
        ),
        compiler_params=pltpu.CompilerParams(
            dimension_semantics=("arbitrary",), vmem_limit_bytes=12 << 20
        ),
        name="run_states",
    )(*args)


def part_lanes(width):
    middle = (width // LANES + 1) // 2 * LANES
    return [slice(0, middle), slice(middle, width)]


def stitch_kernel(width, update_ref, total_ref, entry_ref, before_ref, *refs):
    chunks = update_ref.shape[0]
    state = jnp.zeros(update_ref.shape[1:], F32)
    log = jnp.zeros(total_ref.shape[1:], F32)
    for c in range(chunks):
        entry_ref[c] = state.astype(BF16)
        before_ref[c] = log
        total = total_ref[c]
        state = spread(jnp.exp(total), width)[0:1, :] * state + update_ref[c]
        log = log + total
    wide = spread(log, width)
    for p, lanes in enumerate(part_lanes(width)):
        send_ref, group_ref, glog_ref, prefix_ref, plog_ref = refs[5 * p : 5 * p + 5]
        group_ref[...] = state[:, lanes]
        glog_ref[...] = wide[:, lanes]
        send_ref[0:STATE, :] = state[:, lanes].astype(BF16)
        send_ref[STATE : STATE + 8, :] = pack_logs(wide[:, lanes])
        prefix_ref[...] = jnp.zeros(prefix_ref.shape, F32)
        plog_ref[...] = jnp.zeros(plog_ref.shape, F32)


def stitch(updates, totals):
    _, state, width = updates.shape
    outs = [jax.ShapeDtypeStruct(updates.shape, BF16), jax.ShapeDtypeStruct(totals.shape, F32)]
    for lanes in part_lanes(width):
        wide = lanes.stop - lanes.start
        outs += [
            jax.ShapeDtypeStruct((state + 8, wide), BF16),
            jax.ShapeDtypeStruct((state, wide), F32),
            jax.ShapeDtypeStruct((8, wide), F32),
            jax.ShapeDtypeStruct((state, wide), F32),
            jax.ShapeDtypeStruct((8, wide), F32),
        ]
    entry, before, *rest = pl.pallas_call(
        functools.partial(stitch_kernel, width),
        out_shape=tuple(outs),
        in_specs=[VMEM, VMEM],
        out_specs=(VMEM,) * len(outs),
        compiler_params=pltpu.CompilerParams(vmem_limit_bytes=8 << 20),
        name="stitch",
    )(updates, totals)
    return entry, before, [rest[:5], rest[5:]]


def output_kernel(
    width, per, xc_all, cum_all, cum_t_all, step_t_all, before_all, local_all, direct_ref, *refs,
):
    g_refs, (a_all, b_all, c_all) = refs[:-3], refs[-3:]
    c = pl.program_id(0)
    here = pl.ds(pl.multiple_of(c * CHUNK, CHUNK), CHUNK)
    r, q = (c // per) ^ lax.axis_index("exp"), c % per
    piece = jnp.where(r < 2, r * per + q, q * 2 + r % 2)
    there = pl.ds(pl.multiple_of(piece * CHUNK, CHUNK), CHUNK)
    xc_ref, cum_ref = xc_all.at[here], cum_all.at[here]
    before_ref, local_ref = before_all.at[pl.ds(c, 1)], local_all.at[pl.ds(c, 1)]
    a_ref, b_ref, c_ref = a_all.at[here], b_all.at[here], c_all.at[here]
    bmap = xc_ref[:, width : width + STATE]
    cmap = xc_ref[:, width + STATE :]
    cum = cum_ref[...]
    b_hi, b_lo = split2(bmap)
    c_hi, c_lo = split2(cmap)
    c_ref[...] = c_hi
    gram = mm_nt(jnp.concatenate([c_hi, c_lo], axis=1), jnp.concatenate([b_hi, b_hi], axis=1))
    gram = gram + mm_nt(c_hi, b_lo)
    cum_t = cum_t_all[pl.ds(c, 1)][0]
    step_t = step_t_all[pl.ds(c, 1)][0]
    rows = lax.broadcasted_iota(jnp.int32, (CHUNK, CHUNK), 0)
    cols = lax.broadcasted_iota(jnp.int32, (CHUNK, CHUNK), 1)
    causal = rows >= cols
    left = cols < HEADDIM
    direct = pad_lanes(direct_ref[...])
    for p in range(width // LANES):
        lanes = slice(p * LANES, (p + 1) * LANES)
        ws, cs = [], []
        for h in (2 * p, 2 * p + 1):
            column = jnp.broadcast_to(cum[:, h : h + 1], (CHUNK, CHUNK))
            differ = jnp.where(causal, column - cum_t[h : h + 1, :], -jnp.inf)
            ws.append((jnp.exp(differ) * (gram * step_t[h : h + 1, :])).astype(BF16))
            cs.append(column)
        x = xc_ref[:, lanes]
        xb = jnp.concatenate([jnp.where(left, x, 0.0), jnp.where(left, 0.0, x)], axis=0)
        both = lambda v: jnp.where(
            left[0:1, :],
            jnp.broadcast_to(v[:, 2 * p : 2 * p + 1], (1, LANES)),
            jnp.broadcast_to(v[:, 2 * p + 1 : 2 * p + 2], (1, LANES)),
        )
        inside = mm(jnp.concatenate(ws, axis=1), xb.astype(BF16))
        fade = jnp.exp(jnp.where(left, cs[0], cs[1]))
        y = inside + fade * mm(c_hi, local_ref[0, :, lanes]) + both(direct) * x
        gate = g_refs[0][there, lanes]
        for k, g_ref in enumerate(g_refs[1:]):
            gate = jnp.where(r // 2 == k + 1, g_ref[there, lanes], gate)
        gate = silu(gate)
        a_ref[:, lanes] = y * gate
        b_ref[:, lanes] = fade * jnp.exp(both(before_ref[0, 0:1, :])) * gate


def run_outputs(xc, cum, cum_t, step_t, before, local_states, gates, direct, local):
    total, _ = xc.shape
    width = gates[0].shape[1]
    chunks = total // CHUNK
    per = local // CHUNK
    return pl.pallas_call(
        functools.partial(output_kernel, width, per),
        out_shape=(
            jax.ShapeDtypeStruct((total, width), F32),
            jax.ShapeDtypeStruct((total, width), F32),
            jax.ShapeDtypeStruct((total, STATE), BF16),
        ),
        grid_spec=pltpu.PrefetchScalarGridSpec(
            num_scalar_prefetch=0,
            grid=(chunks,),
            in_specs=[VMEM] * (7 + len(gates)),
            out_specs=(VMEM,) * 3,
        ),
        cost_estimate=pl.CostEstimate(
            flops=2 * total * width * 1500, transcendentals=total * width * 4, bytes_accessed=16 * total * width
        ),
        compiler_params=pltpu.CompilerParams(
            dimension_semantics=("arbitrary",), vmem_limit_bytes=12 << 20
        ),
        name="run_outputs",
    )(xc, cum, cum_t, step_t, before, local_states, direct, *gates)


def pack_logs(wide):
    hi, mid, lo = split3(wide)
    row = lax.broadcasted_iota(jnp.int32, wide.shape, 0)
    lo = jnp.where(row == 2, lo.astype(F32), 0.0)
    return jnp.where(row == 0, hi.astype(F32), jnp.where(row == 1, mid.astype(F32), lo)).astype(BF16)


def unpack(got_ref):
    other = got_ref[0:STATE, :].astype(F32)
    logs = got_ref[STATE : STATE + 8, :].astype(F32)
    log = logs[0:1, :] + logs[1:2, :] + logs[2:3, :]
    return other, log


def combine_kernel(
    d, radix, *refs,
):
    got_refs, refs = refs[: radix - 1], refs[radix - 1 :]
    group_ref, glog_ref, prefix_ref, plog_ref = refs[:4]
    send_ref, group_out, glog_out, prefix_out, plog_out, states, logs = refs[4:]
    mine = (lax.axis_index("seq") // d) % radix
    states[0] = group_ref[...]
    logs[0] = glog_ref[...]
    for k, got_ref in enumerate(got_refs):
        other, other_log = unpack(got_ref)
        states[k + 1] = other
        logs[k + 1] = jnp.broadcast_to(other_log, logs.shape[1:])
    total = jnp.zeros(group_ref.shape, F32)
    total_log = jnp.zeros((1, total.shape[1]), F32)
    early, early_log = total, total_log
    for m in range(radix):
        state = states[pl.ds(m ^ mine, 1)][0]
        log = logs[pl.ds(m ^ mine, 1)][0, 0:1]
        if m:
            early = jnp.where(mine == m, total, early)
            early_log = jnp.where(mine == m, total_log, early_log)
            state = jnp.exp(log) * total + state
        total = state
        total_log = total_log + log
    prefix_log = plog_ref[0:1, :]
    prefix_out[...] = prefix_ref[...] + jnp.exp(prefix_log) * early
    plog_out[...] = jnp.broadcast_to(prefix_log + early_log, plog_out.shape)
    new_log = jnp.broadcast_to(total_log, glog_out.shape)
    group_out[...] = total
    glog_out[...] = new_log
    send_ref[0:STATE, :] = total.astype(BF16)
    send_ref[STATE : STATE + 8, :] = pack_logs(new_log)


def combine(d, got, group, glog, prefix, plog):
    radix = len(got) + 1
    state = jax.ShapeDtypeStruct(group.shape, F32)
    log = jax.ShapeDtypeStruct(glog.shape, F32)
    return pl.pallas_call(
        functools.partial(combine_kernel, d, radix),
        out_shape=(jax.ShapeDtypeStruct(got[0].shape, BF16), state, log, state, log),
        grid_spec=pltpu.PrefetchScalarGridSpec(
            num_scalar_prefetch=0,
            grid=(1,),
            in_specs=[VMEM] * (radix + 3),
            out_specs=(VMEM,) * 5,
            scratch_shapes=[
                pltpu.VMEM((radix, *group.shape), F32),
                pltpu.VMEM((radix, *glog.shape), F32),
            ],
        ),
        compiler_params=pltpu.CompilerParams(vmem_limit_bytes=8 << 20),
        name="combine",
    )(*got, group, glog, prefix, plog)


def join_kernel(d, a_ref, b_ref, c_ref, *refs):
    o_ref, ss_ref, s_scr = refs[-3:]
    upper = (lax.axis_index("seq") & d) != 0
    for p, lanes in enumerate(part_lanes(o_ref.shape[1])):
        got_ref, prefix_ref, plog_ref = refs[3 * p : 3 * p + 3]
        other, _ = unpack(got_ref)
        prefix = prefix_ref[...]
        entering = jnp.where(upper, prefix + jnp.exp(plog_ref[0:1, :]) * other, prefix)
        s_scr[:, lanes] = entering.astype(BF16)

    part = 256
    ones = jnp.ones((8, 2 * LANES), BF16)
    for at in range(0, o_ref.shape[0], part):
        rows = slice(at, at + part)
        gated = a_ref[rows, :] + b_ref[rows, :] * mm(c_ref[rows, :], s_scr[...])
        o_ref[rows, :] = gated
        squared = gated * gated
        folded = sum(squared[:, k : k + LANES] for k in range(0, squared.shape[1], LANES))
        hi, lo = split2(folded)
        ss_ref[:, rows] = mm_nt(ones, jnp.concatenate([hi, lo], axis=1))[0:1]


def join(d, a, b, c, entering):
    total, width = a.shape
    return pl.pallas_call(
        functools.partial(join_kernel, d),
        out_shape=(jax.ShapeDtypeStruct((total, width), F32), jax.ShapeDtypeStruct((1, total), F32)),
        grid_spec=pltpu.PrefetchScalarGridSpec(
            num_scalar_prefetch=0,
            grid=(1,),
            in_specs=[VMEM] * (3 + len(entering)),
            out_specs=(VMEM, VMEM),
            scratch_shapes=[pltpu.VMEM((STATE, width), BF16)],
        ),
        compiler_params=pltpu.CompilerParams(
            dimension_semantics=("arbitrary",), vmem_limit_bytes=10 << 20
        ),
        name="join",
    )(a, b, c, *entering)


def norm_kernel(inner_width, g_ref, gain_ref, *refs):
    *squares_refs, o_hbm, o_ref, sems = refs
    rows, width = o_ref.shape
    copies = []
    for part in range(rows // LANES):
        here = slice(part * LANES, (part + 1) * LANES)
        squares = sum(r[:, here] for r in squares_refs)
        scale = lax.rsqrt(squares / inner_width + 1e-05)
        column = jnp.broadcast_to(scale, (LANES, LANES)).T
        for lane in range(width // LANES):
            lanes = slice(lane * LANES, (lane + 1) * LANES)
            o_ref[here, lanes] = (g_ref[here, lanes] * column * gain_ref[:, lanes]).astype(BF16)
        copies.append(pltpu.make_async_copy(o_ref.at[here], o_hbm.at[here], sems.at[part]))
        copies[-1].start()
    for copy in copies:
        copy.wait()


def norm(gated, squares, gain, inner_width):
    total, width = gated.shape
    return pl.pallas_call(
        functools.partial(norm_kernel, inner_width),
        out_shape=jax.ShapeDtypeStruct((total, width), BF16),
        in_specs=[VMEM] * (2 + len(squares)),
        out_specs=pl.BlockSpec(memory_space=pl.ANY),
        scratch_shapes=[
            pltpu.VMEM((total, width), BF16),
            pltpu.SemaphoreType.DMA((total // LANES,)),
        ],
        compiler_params=pltpu.CompilerParams(vmem_limit_bytes=8 << 20),
        name="norm",
    )(gated, gain, *squares)


def stages(shards):
    out, d = [], 1
    while d < shards:
        radix = 4 if 8 * d <= shards else 2
        out.append((d, radix))
        d *= radix
    return out


def body(
    tokens,
    routes,
    gate_inner_weight,
    state_map_weight,
    step_size_weight,
    adapter_down_weight,
    adapter_up_weight,
    inner_conv_taps,
    state_map_taps,
    inner_conv_bias,
    state_map_conv_bias,
    step_size_bias,
    head_decay_rate,
    direct_head_scale,
    gated_norm_scale,
):
    n = lax.axis_size("exp")
    shards = lax.axis_size("seq")
    local, features = tokens.shape
    total = local * n
    width = gate_inner_weight.shape[2]
    experts = adapter_up_weight.shape[0]
    rank = 8
    per = local // CHUNK

    down = {0: adapter_down_weight.T}
    for k in range(2, n, 2):
        down[k] = swap(down[0], "exp", k)
    *pieces, note = pack(tokens, routes.reshape(1, local), max(per - 1, 1))
    notes = {0: note}
    far = {}
    for k in range(2, n, 2):
        notes[k] = swap(note, "exp", k)
    wz = gate_inner_weight.reshape(features, 2 * width)
    for q in range(per):
        if q and q == per - 1:
            late, wz = lax.optimization_barrier((tokens, wz))
            pieces.append(late[q * CHUNK :])
        for k in range(2, n, 2):
            far[k, q] = swap(pieces[q], "exp", k)
    sibling = swap(tokens, "exp", 1)
    for k in range(0, n, 2):
        down[k + 1] = swap(down[k], "exp", 1)
        notes[k + 1] = swap(notes[k], "exp", 1)
    downs = [down[k] for k in range(n)]
    notes = [notes[k] for k in range(n)]
    up = adapter_up_weight.reshape(experts, 2 * width)
    call = functools.partial(
        project, devices=n, wz=wz, wbc=state_map_weight, up=up, rank=rank,
        dtb=step_size_bias[None, :], rate=head_decay_rate[None, :],
    )
    z, *sums, lift, rows, tails, rim, wsm, masks = call(
        [tokens, sibling], notes=notes, dt_t=step_size_weight.T, downs=downs
    )
    gates = [gate_project([rows], [lift], wz, up, n)]
    rim = lax.ppermute(rim, "seq", [(i, (i + 1) % shards) for i in range(shards)])
    params = [
        inner_conv_taps, state_map_taps, inner_conv_bias[None, :], state_map_conv_bias[None, :],
    ]
    kept = run_states(total, z, sums, z, tails, rim, params, width, per, None, None)
    far_rows = {}
    for q in range(per):
        for k in range(2, n, 2):
            mine = far[k, q]
            other = swap(mine, "exp", 1)
            older = far_rows[k, q - 1][2] if q else z
            pieces = [[mine, other]] if (k, q) != (n - 2, per - 1) else [[mine], [other]]
            found = []
            for p, piece in enumerate(pieces):
                new_z, *sums, lift, rows = call(
                    piece,
                    route_from=tuple(
                        ((k + p + m) * local + q * CHUNK, CHUNK) for m in range(len(piece))
                    ),
                    routes=masks,
                    wsm=wsm,
                )
                kept = run_states(
                    total, new_z, sums, older, tails, rim, params, width, per, (k + p, q), kept
                )
                found.append((rows, lift))
            far_rows[k, q] = ([f[0] for f in found], [f[1] for f in found], new_z)
    xc, cum, cum_t, step_t, updates, totals = kept
    states, before, parts = stitch(updates, totals)
    for d, radix in stages(shards):
        last = 2 * d == shards
        got = {}
        for p, part in enumerate(parts):
            for k in range(1, radix):
                got[p, k] = swap(part[0], "seq", d * k)
        for p, part in enumerate(parts):
            arrived = [got[p, k] for k in range(1, radix)]
            if last:
                parts[p] = [arrived[0], *part[3:]]
            else:
                parts[p] = combine(d, arrived, *part[1:])
    entering = [x for part in parts for x in part]
    for k in range(2, n, 2):
        xs = [x for q in range(per) for x in far_rows[k, q][0]]
        lifts = [x for q in range(per) for x in far_rows[k, q][1]]
        gates.append(gate_project(xs, lifts, wz, up, n))
    a, b, c = run_outputs(
        xc, cum, cum_t, step_t, before, states, gates, direct_head_scale[None, :], local
    )
    gated, mine = join(shards // 2, a, b, c, entering)
    others = [swap(mine, "exp", k) for k in range(1, n)]
    return norm(gated, [mine, *others], gated_norm_scale[None, :], width * n)


def solution(mesh):
    in_specs = (
        P(("seq", "exp"), None),
        P(("seq", "exp"), None),
        P(None, None, "exp"),
        P(),
        P(None, "exp"),
        P(None, "exp"),
        P(None, None, "exp"),
        P(None, "exp"),
        P(),
        P("exp"),
        P(),
        P("exp"),
        P("exp"),
        P("exp"),
        P("exp"),
    )
    out_specs = P("seq", "exp")

    return jax.shard_map(body, mesh=mesh, in_specs=in_specs, out_specs=out_specs, check_vma=False)
```

```python
import functools

import jax
import jax.numpy as jnp
from jax import lax
from jax.experimental import pallas as pl
from jax.experimental.pallas import tpu as pltpu
from jax.sharding import PartitionSpec as P


STATE = 128
HEADDIM = 64
CHUNK = 128
HEADS_PAD = 16
LANES = 128
F32 = jnp.float32
BF16 = jnp.bfloat16


def swap(block, axis, mask):
    return lax.ppermute(block, axis, [(i, i ^ mask) for i in range(lax.axis_size(axis))])


def split3(value):
    hi = value.astype(BF16)
    rest = value - hi.astype(F32)
    mid = rest.astype(BF16)
    lo = (rest - mid.astype(F32)).astype(BF16)
    return hi, mid, lo


def split2(value):
    hi = value.astype(BF16)
    return hi, (value - hi.astype(F32)).astype(BF16)


def mm(a, b):
    return jnp.dot(a, b, preferred_element_type=F32)


def mm_nt(a, b):
    return lax.dot_general(a, b, (((1,), (1,)), ((), ())), preferred_element_type=F32)


def silu_of_double(half):
    return half + half * jnp.tanh(half)


def silu(v):
    return silu_of_double(0.5 * v)


def route_mask(e, route_row, experts_dev, rank):
    column = lax.broadcasted_iota(jnp.int32, (LANES, route_row.shape[1]), 0)
    per_dev = experts_dev * rank
    expert = ((column // per_dev) ^ e) * experts_dev + (column % per_dev) // rank
    return jnp.where(expert.astype(F32) == route_row, 1.0, 0.0)


VMEM = pl.BlockSpec(memory_space=pltpu.VMEM)


def up_rows(up_ref, e, devices, lanes):
    cols = up_ref.shape[0] // devices
    return jnp.concatenate(
        [up_ref[pl.ds(pl.multiple_of((e ^ r) * cols, cols), cols), lanes] for r in range(devices)], axis=0
    )


def pack_kernel(tokens_ref, route_ref, *refs):
    halves, (note_ref, tail, route, sems) = refs[:-4], refs[-4:]
    rows = halves[0].shape[0]
    copies = [
        pltpu.make_async_copy(tokens_ref.at[q * rows : (q + 1) * rows], half, sems.at[q])
        for q, half in enumerate(halves)
    ]
    last = tokens_ref.shape[0] - 8
    copies.append(pltpu.make_async_copy(tokens_ref.at[last:], tail, sems.at[len(halves)]))
    copies.append(pltpu.make_async_copy(route_ref, route, sems.at[len(halves) + 1]))
    for copy in copies[::-1]:
        copy.start()
    copies[-1].wait()
    copies[-2].wait()
    route = route[...].astype(F32)
    route = jnp.concatenate([route, jnp.zeros((1, tail.shape[1] - route.shape[1]), F32)], axis=1)
    row = lax.broadcasted_iota(jnp.int32, tail.shape, 0)
    note_ref[...] = jnp.where(row == 0, route, tail[...].astype(F32)).astype(BF16)
    for copy in copies[:-2]:
        copy.wait()


def pack(tokens, route_row, per):
    features = tokens.shape[1]
    anywhere = pl.BlockSpec(memory_space=pltpu.HBM)
    piece = jax.ShapeDtypeStruct((CHUNK, features), BF16)
    return pl.pallas_call(
        pack_kernel,
        out_shape=(piece,) * per + (jax.ShapeDtypeStruct((8, features), BF16),),
        in_specs=[anywhere, anywhere],
        out_specs=(VMEM,) * (per + 1),
        scratch_shapes=[
            pltpu.VMEM((8, features), BF16),
            pltpu.VMEM(route_row.shape, route_row.dtype),
            pltpu.SemaphoreType.DMA((per + 2,)),
        ],
        compiler_params=pltpu.CompilerParams(vmem_limit_bytes=4 << 20),
        name="pack",
    )(tokens, route_row)


def pad_lanes(row):
    pad = LANES - row.shape[1]
    return jnp.concatenate([row, jnp.zeros((row.shape[0], pad), F32)], axis=1)


def step_chain(raw, bias, rate):
    column = lambda row: jnp.broadcast_to(pad_lanes(row), (LANES, LANES)).T[:HEADS_PAD]
    raw = pad_lanes(raw).T[:HEADS_PAD] + column(bias)
    step = jnp.maximum(raw, 0.0) + jnp.log1p(jnp.exp(-jnp.abs(raw)))
    decay = -column(rate) * step
    rows = lax.broadcasted_iota(jnp.int32, (CHUNK, CHUNK), 0)
    cols = lax.broadcasted_iota(jnp.int32, (CHUNK, CHUNK), 1)
    upper = jnp.where(rows <= cols, 1.0, 0.0).astype(BF16)
    sums = mm(jnp.concatenate(split3(decay), axis=0), upper)
    cum_t = sums[:HEADS_PAD] + sums[HEADS_PAD : 2 * HEADS_PAD] + sums[2 * HEADS_PAD :]
    carried = jnp.exp(jnp.broadcast_to(cum_t[:, CHUNK - 1 :], cum_t.shape) - cum_t) * step
    blank = jnp.zeros((LANES - 2 * HEADS_PAD, CHUNK), F32)
    return jnp.concatenate([cum_t, carried, blank], axis=0).T, cum_t, step


def project_kernel(cfg, *refs):
    counts, route_from, devices, cols, rank, near = cfg
    x_refs, refs = refs[: len(counts)], refs[len(counts):]
    if near:
        n_refs, refs = refs[:devices], refs[devices:]
    else:
        route_ref, refs = refs[0], refs[1:]
    w_ref, wbc_ref, up_ref, dtb_ref, rate_ref = refs[:5]
    refs = refs[5:]
    if near:
        dt_ref, d_refs, refs = refs[0], refs[1 : 1 + devices], refs[1 + devices:]
        z_ref, cum_ref, cum_t_ref, step_t_ref, lift_ref, x_scr, tails_ref, rim_ref, wsm_t_ref, route_ref, lift_scr, wsm_ref = refs
    else:
        wsm_ref, z_ref, cum_ref, cum_t_ref, step_t_ref, lift_ref, x_scr = refs
        lift_scr = lift_ref
    e = lax.axis_index("exp")
    rows = sum(counts)

    at = 0
    for x_ref, n in zip(x_refs, counts):
        x_scr[at : at + n, :] = x_ref[...]
        at += n
    if near:
        for r in range(devices):
            x_scr[at + 8 * r : at + 8 * r + 8, :] = n_refs[r][...]
        wsm_ref[LANES:, :] = jnp.zeros((wsm_ref.shape[0] - LANES, wsm_ref.shape[1]), BF16)
        wsm_ref[LANES : LANES + dt_ref.shape[0], :] = dt_ref[...]
        for r in range(devices):
            wsm_ref[r * cols : (r + 1) * cols, :] = d_refs[r][...]
    if near:
        weights = jnp.concatenate([d[...] for d in d_refs], axis=0).astype(F32)
        wide = 512
        for at in range(0, weights.shape[1], wide):
            wsm_t_ref[at : at + wide, :LANES] = weights[:, at : at + wide].T.astype(BF16)
        small = mm_nt(x_scr[...], wsm_ref[...])
        steps = wsm_ref[LANES:, :].astype(F32)
        steps = jnp.concatenate([steps, jnp.zeros((LANES - 16, steps.shape[1]), F32)], axis=0)
        for at in range(0, weights.shape[1], wide):
            wsm_t_ref[at : at + wide, LANES:] = steps[:, at : at + wide].T.astype(BF16)
    else:
        small = mm(x_scr[...], wsm_ref[...])[:, : LANES + 16]

    def mask_of(r, lane):
        row = n_refs[r][0:1, lane : lane + LANES].astype(F32)
        return route_mask(e, row, cols // rank, rank).T

    masks = []
    if near:
        whole = route_ref.shape[0] // devices
        for r in range(devices):
            for lane in range(0, whole, LANES):
                mask = mask_of(r, lane)
                route_ref[r * whole + lane : r * whole + lane + LANES, :] = mask.astype(BF16)
                if r < 2:
                    masks.append(mask)
        for r in range(devices):
            masks.append(route_ref[(r + 1) * whole - 16 : (r + 1) * whole, :].astype(F32)[8:])
    else:
        masks = [route_ref[first : first + n, :].astype(F32) for first, n in route_from]
    lift = jnp.where(jnp.concatenate(masks, axis=0) > 0.5, small[:, :LANES], 0.0).astype(BF16)
    lift_scr[...] = lift
    for c in range(rows // CHUNK):
        here = slice(c * CHUNK, (c + 1) * CHUNK)
        both, cum_t, step_t = step_chain(small[here, LANES:], dtb_ref[...], rate_ref[...])
        cum_ref[here, :] = both
        cum_t_ref[c] = cum_t
        step_t_ref[c] = step_t
    if near:
        lift_ref[...] = lift[:rows]

    def put(lanes, value):
        z_ref[:, lanes] = value[:rows]
        if near:
            tails_ref[:, lanes] = value[rows:]

    width = z_ref.shape[1]
    inner = up_ref.shape[1] // 2
    tn = 256 if inner % 256 == 0 else 128
    for at in range(0, inner, tn):
        lanes = slice(inner + at, inner + at + tn)
        up = up_rows(up_ref, e, devices, lanes)
        put(slice(at, at + tn), mm(x_scr[...], w_ref[:, lanes]) + mm(lift_scr[...], up))
    for at in range(0, width - inner, tn):
        put(slice(inner + at, inner + at + tn), mm(x_scr[...], wbc_ref[:, at : at + tn]))
    if near:
        row = ((devices - 1) ^ e) * 8
        rim_ref[...] = tails_ref[pl.ds(pl.multiple_of(row, 8), 8), :]


def project(xs, wz, wbc, up, dtb, rate, rank, devices, notes=None, dt_t=None, downs=None, route_from=None, routes=None, wsm=None):
    counts = tuple(x.shape[0] for x in xs)
    rows = sum(counts)
    features = wz.shape[0]
    width = up.shape[1] // 2 + wbc.shape[1]
    near = wsm is None
    args = list(xs) + (list(notes) if near else [routes]) + [wz, wbc, up, dtb, rate]
    args += [dt_t, *downs] if near else [wsm]
    out_shape = [
        jax.ShapeDtypeStruct((rows, width), F32),
        jax.ShapeDtypeStruct((rows, LANES), F32),
        jax.ShapeDtypeStruct((rows // CHUNK, HEADS_PAD, CHUNK), F32),
        jax.ShapeDtypeStruct((rows // CHUNK, HEADS_PAD, CHUNK), F32),
        jax.ShapeDtypeStruct((rows, LANES), BF16),
    ]
    extra = 8 * devices if near else 0
    out_shape.append(jax.ShapeDtypeStruct((rows + extra, features), BF16))
    scratch = []
    if near:
        out_shape += [jax.ShapeDtypeStruct((extra, width), F32), jax.ShapeDtypeStruct((8, width), F32)]
        out_shape.append(jax.ShapeDtypeStruct((features, 2 * LANES), BF16))
        out_shape.append(jax.ShapeDtypeStruct((devices * counts[0], LANES), BF16))
        scratch.append(pltpu.VMEM((rows + extra, LANES), BF16))
        scratch.append(pltpu.VMEM((LANES + 16, features), BF16))
    cfg = (counts, route_from, devices, LANES // devices, rank, near)
    return pl.pallas_call(
        functools.partial(project_kernel, cfg),
        out_shape=tuple(out_shape),
        grid_spec=pltpu.PrefetchScalarGridSpec(
            num_scalar_prefetch=0,
            grid=(1,),
            in_specs=[VMEM] * len(args),
            out_specs=(VMEM,) * len(out_shape),
            scratch_shapes=scratch,
        ),
        cost_estimate=pl.CostEstimate(
            flops=2 * rows * features * (width + 256),
            transcendentals=0,
            bytes_accessed=2 * features * (width + rows) + 4 * rows * width,
        ),
        compiler_params=pltpu.CompilerParams(
            dimension_semantics=("arbitrary",), vmem_limit_bytes=16 << 20
        ),
        name="project",
    )(*args)


def gate_kernel(rows, devices, *refs):
    x_refs, lift_refs = refs[: len(rows)], refs[len(rows) : 2 * len(rows)]
    w_ref, up_ref, g_ref = refs[-3:]
    width = g_ref.shape[1]
    tn = 256 if width % 256 == 0 else 128
    for lane in range(0, width, tn):
        lanes = slice(lane, lane + tn)
        up = up_rows(up_ref, lax.axis_index("exp"), devices, lanes)
        at = 0
        for x_ref, lift_ref, n in zip(x_refs, lift_refs, rows):
            g_ref[at : at + n, lanes] = mm(x_ref[0:n, :], w_ref[:, lanes]) + mm(lift_ref[...], up)
            at += n


def gate_project(xs, lifts, wz, up, devices):
    counts = tuple(lift.shape[0] for lift in lifts)
    rows = sum(counts)
    features = wz.shape[0]
    width = up.shape[1] // 2
    args = list(xs) + list(lifts) + [wz, up]
    return pl.pallas_call(
        functools.partial(gate_kernel, counts, devices),
        out_shape=jax.ShapeDtypeStruct((rows, width), F32),
        in_specs=[VMEM] * len(args),
        out_specs=VMEM,
        cost_estimate=pl.CostEstimate(
            flops=2 * rows * features * width,
            transcendentals=0,
            bytes_accessed=2 * features * (width + rows) + 4 * rows * width,
        ),
        compiler_params=pltpu.CompilerParams(vmem_limit_bytes=12 << 20),
        name="gate_project",
    )(*args)


def spread(value, width):
    rows = value.shape[0]
    left = lax.broadcasted_iota(jnp.int32, (rows, LANES), 1) < HEADDIM
    parts = []
    for p in range(width // LANES):
        a = jnp.broadcast_to(value[:, 2 * p : 2 * p + 1], (rows, LANES))
        b = jnp.broadcast_to(value[:, 2 * p + 1 : 2 * p + 2], (rows, LANES))
        parts.append(jnp.where(left, a, b))
    return jnp.concatenate(parts, axis=1)


def state_kernel(
    cfg, z_all, sums_all, sums_t_all, steps_t_all, older_all, tails_ref, rim_ref,
    taps_ref, mtaps_ref, bias_ref, mbias_ref, *refs,
):
    width, per, far, where_am_i = cfg
    xc_all, cum_all, cum_t_all, step_t_all, update_all, total_all, ext = refs[-7:]
    e = lax.axis_index("exp")
    r, q = where_am_i(pl.program_id(0))
    block = r ^ e
    at = pl.program_id(0) * CHUNK
    there = pl.ds(pl.multiple_of(at, CHUNK), CHUNK)
    z_ref = z_all.at[there]
    older = r % 2 * CHUNK + CHUNK - 8 if far else jnp.maximum(at - 8, 0)
    prev_ref = older_all.at[pl.ds(pl.multiple_of(older, 8), 8)]
    chunk = block * per + q
    here = pl.ds(pl.multiple_of(chunk * CHUNK, CHUNK), CHUNK)
    xc_ref, cum_ref = xc_all.at[here], cum_all.at[here]
    cum_t_ref, step_t_ref = cum_t_all.at[pl.ds(chunk, 1)], step_t_all.at[pl.ds(chunk, 1)]
    update_ref, total_ref = update_all.at[pl.ds(chunk, 1)], total_all.at[pl.ds(chunk, 1)]
    before = pl.multiple_of((jnp.maximum(block - 1, 0) ^ e) * 8, 8)
    rim = jnp.where(lax.axis_index("seq") == 0, 0.0, rim_ref[...])
    first = jnp.where(block == 0, rim, tails_ref[pl.ds(before, 8), :])
    ext[0:8, :] = jnp.where(q == 0, first, prev_ref[...])
    ext[8 : 8 + CHUNK, :] = z_ref[...]
    taps = taps_ref.shape[0]
    outs = []
    for tr, br, lanes in (
        (taps_ref, bias_ref, slice(0, width)),
        (mtaps_ref, mbias_ref, slice(width, width + 2 * STATE)),
    ):
        halved = 0.5 * tr[...]
        acc = 0.5 * br[...] + halved[taps - 1 : taps, :] * ext[8 : 8 + CHUNK, lanes]
        for k in range(taps - 1):
            start = 8 - (taps - 1) + k
            acc = acc + halved[k : k + 1, :] * ext[start : start + CHUNK, lanes]
        out = silu_of_double(acc)
        xc_ref[:, lanes] = out
        outs.append(out)
    x, maps = outs

    both = sums_all[there, :]
    cum_ref[...] = both
    cum_t_ref[0] = sums_t_all[pl.ds(pl.program_id(0), 1)][0]
    step_t_ref[0] = steps_t_all[pl.ds(pl.program_id(0), 1)][0]
    total_ref[0] = jnp.broadcast_to(both[CHUNK - 1 : CHUNK, :], total_ref.shape[1:])

    xs = (spread(both[:, HEADS_PAD:], width) * x).astype(BF16)
    b_hi, b_lo = split2(maps[:, :STATE].T)
    update_ref[0] = mm(jnp.concatenate([b_hi, b_lo], axis=1), jnp.concatenate([xs, xs], axis=0))


def run_states(total, z, sums, older, tails, rim, params, width, per, far, buffers):
    wide = z.shape[1]
    chunks = total // CHUNK
    if far is None:
        steps = 2 * per
        at = lambda c: (c // per, c % per)
    else:
        steps = z.shape[0] // CHUNK
        at = lambda c: (far[0] + c, far[1])

    args = [z, *sums, older, tails, rim, *params]
    in_specs = [VMEM] * len(args)
    aliases = {}
    if buffers is not None:
        for n, buffer in enumerate(buffers):
            aliases[len(args)] = n
            args.append(buffer)
            in_specs.append(VMEM)
    return pl.pallas_call(
        functools.partial(state_kernel, (width, per, far is not None, at)),
        out_shape=(
            jax.ShapeDtypeStruct((total, wide), F32),
            jax.ShapeDtypeStruct((total, LANES), F32),
            jax.ShapeDtypeStruct((chunks, HEADS_PAD, CHUNK), F32),
            jax.ShapeDtypeStruct((chunks, HEADS_PAD, CHUNK), F32),
            jax.ShapeDtypeStruct((chunks, STATE, width), F32),
            jax.ShapeDtypeStruct((chunks, 8, LANES), F32),
        ),
        grid_spec=pltpu.PrefetchScalarGridSpec(
            num_scalar_prefetch=0,
            grid=(steps,),
            in_specs=in_specs,
            out_specs=(VMEM,) * 6,
            scratch_shapes=[pltpu.VMEM((CHUNK + 8, wide), F32)],
        ),
        input_output_aliases=aliases,
        cost_estimate=pl.CostEstimate(
            flops=2 * steps * CHUNK * width * 1000, transcendentals=steps * CHUNK * wide,
            bytes_accessed=12 * steps * CHUNK * wide,
        ),
        compiler_params=pltpu.CompilerParams(
            dimension_semantics=("arbitrary",), vmem_limit_bytes=12 << 20
        ),
        name="run_states",
    )(*args)


def part_lanes(width):
    middle = (width // LANES + 1) // 2 * LANES
    return [slice(0, middle), slice(middle, width)]


def stitch_kernel(width, update_ref, total_ref, entry_ref, before_ref, *refs):
    chunks = update_ref.shape[0]
    state = jnp.zeros(update_ref.shape[1:], F32)
    log = jnp.zeros(total_ref.shape[1:], F32)
    for c in range(chunks):
        entry_ref[c] = state.astype(BF16)
        before_ref[c] = log
        total = total_ref[c]
        state = spread(jnp.exp(total), width)[0:1, :] * state + update_ref[c]
        log = log + total
    wide = spread(log, width)
    for p, lanes in enumerate(part_lanes(width)):
        send_ref, group_ref, glog_ref, prefix_ref, plog_ref = refs[5 * p : 5 * p + 5]
        group_ref[...] = state[:, lanes]
        glog_ref[...] = wide[:, lanes]
        send_ref[0:STATE, :] = state[:, lanes].astype(BF16)
        send_ref[STATE : STATE + 8, :] = pack_logs(wide[:, lanes])
        prefix_ref[...] = jnp.zeros(prefix_ref.shape, F32)
        plog_ref[...] = jnp.zeros(plog_ref.shape, F32)


def stitch(updates, totals):
    _, state, width = updates.shape
    outs = [jax.ShapeDtypeStruct(updates.shape, BF16), jax.ShapeDtypeStruct(totals.shape, F32)]
    for lanes in part_lanes(width):
        wide = lanes.stop - lanes.start
        outs += [
            jax.ShapeDtypeStruct((state + 8, wide), BF16),
            jax.ShapeDtypeStruct((state, wide), F32),
            jax.ShapeDtypeStruct((8, wide), F32),
            jax.ShapeDtypeStruct((state, wide), F32),
            jax.ShapeDtypeStruct((8, wide), F32),
        ]
    entry, before, *rest = pl.pallas_call(
        functools.partial(stitch_kernel, width),
        out_shape=tuple(outs),
        in_specs=[VMEM, VMEM],
        out_specs=(VMEM,) * len(outs),
        compiler_params=pltpu.CompilerParams(vmem_limit_bytes=8 << 20),
        name="stitch",
    )(updates, totals)
    return entry, before, [rest[:5], rest[5:]]


def output_kernel(
    width, per, xc_all, cum_all, cum_t_all, step_t_all, before_all, local_all, direct_ref, *refs,
):
    g_refs, (a_all, b_all, c_all) = refs[:-3], refs[-3:]
    c = pl.program_id(0)
    here = pl.ds(pl.multiple_of(c * CHUNK, CHUNK), CHUNK)
    r, q = (c // per) ^ lax.axis_index("exp"), c % per
    near = pl.ds(pl.multiple_of(jnp.where(r < 2, r * per + q, 0) * CHUNK, CHUNK), CHUNK)
    far = pl.ds(pl.multiple_of(r % 2 * CHUNK, CHUNK), CHUNK)
    xc_ref, cum_ref = xc_all.at[here], cum_all.at[here]
    before_ref, local_ref = before_all.at[pl.ds(c, 1)], local_all.at[pl.ds(c, 1)]
    a_ref, b_ref, c_ref = a_all.at[here], b_all.at[here], c_all.at[here]
    bmap = xc_ref[:, width : width + STATE]
    cmap = xc_ref[:, width + STATE :]
    cum = cum_ref[...]
    b_hi, b_lo = split2(bmap)
    c_hi, c_lo = split2(cmap)
    c_ref[...] = c_hi
    gram = mm_nt(jnp.concatenate([c_hi, c_lo], axis=1), jnp.concatenate([b_hi, b_hi], axis=1))
    gram = gram + mm_nt(c_hi, b_lo)
    cum_t = cum_t_all[pl.ds(c, 1)][0]
    step_t = step_t_all[pl.ds(c, 1)][0]
    rows = lax.broadcasted_iota(jnp.int32, (CHUNK, CHUNK), 0)
    cols = lax.broadcasted_iota(jnp.int32, (CHUNK, CHUNK), 1)
    causal = rows >= cols
    left = cols < HEADDIM
    direct = pad_lanes(direct_ref[...])
    for p in range(width // LANES):
        lanes = slice(p * LANES, (p + 1) * LANES)
        ws, cs = [], []
        for h in (2 * p, 2 * p + 1):
            column = jnp.broadcast_to(cum[:, h : h + 1], (CHUNK, CHUNK))
            differ = jnp.where(causal, column - cum_t[h : h + 1, :], -jnp.inf)
            ws.append((jnp.exp(differ) * (gram * step_t[h : h + 1, :])).astype(BF16))
            cs.append(column)
        x = xc_ref[:, lanes]
        xb = jnp.concatenate([jnp.where(left, x, 0.0), jnp.where(left, 0.0, x)], axis=0)
        both = lambda v: jnp.where(
            left[0:1, :],
            jnp.broadcast_to(v[:, 2 * p : 2 * p + 1], (1, LANES)),
            jnp.broadcast_to(v[:, 2 * p + 1 : 2 * p + 2], (1, LANES)),
        )
        inside = mm(jnp.concatenate(ws, axis=1), xb.astype(BF16))
        fade = jnp.exp(jnp.where(left, cs[0], cs[1]))
        y = inside + fade * mm(c_hi, local_ref[0, :, lanes]) + both(direct) * x
        gate = g_refs[0][near, lanes]
        for k, g_ref in enumerate(g_refs[1:]):
            found = (r // 2 == k // per + 1) & (q == k % per)
            gate = jnp.where(found, g_ref[far, lanes], gate)
        gate = silu(gate)
        a_ref[:, lanes] = y * gate
        b_ref[:, lanes] = fade * jnp.exp(both(before_ref[0, 0:1, :])) * gate


def run_outputs(xc, cum, cum_t, step_t, before, local_states, gates, direct, local):
    total, _ = xc.shape
    width = gates[0].shape[1]
    chunks = total // CHUNK
    per = local // CHUNK
    return pl.pallas_call(
        functools.partial(output_kernel, width, per),
        out_shape=(
            jax.ShapeDtypeStruct((total, width), F32),
            jax.ShapeDtypeStruct((total, width), F32),
            jax.ShapeDtypeStruct((total, STATE), BF16),
        ),
        grid_spec=pltpu.PrefetchScalarGridSpec(
            num_scalar_prefetch=0,
            grid=(chunks,),
            in_specs=[VMEM] * (7 + len(gates)),
            out_specs=(VMEM,) * 3,
        ),
        cost_estimate=pl.CostEstimate(
            flops=2 * total * width * 1500, transcendentals=total * width * 4, bytes_accessed=16 * total * width
        ),
        compiler_params=pltpu.CompilerParams(
            dimension_semantics=("arbitrary",), vmem_limit_bytes=12 << 20
        ),
        name="run_outputs",
    )(xc, cum, cum_t, step_t, before, local_states, direct, *gates)


def pack_logs(wide):
    hi, mid, lo = split3(wide)
    row = lax.broadcasted_iota(jnp.int32, wide.shape, 0)
    lo = jnp.where(row == 2, lo.astype(F32), 0.0)
    return jnp.where(row == 0, hi.astype(F32), jnp.where(row == 1, mid.astype(F32), lo)).astype(BF16)


def unpack(got_ref):
    other = got_ref[0:STATE, :].astype(F32)
    logs = got_ref[STATE : STATE + 8, :].astype(F32)
    log = logs[0:1, :] + logs[1:2, :] + logs[2:3, :]
    return other, log


def combine_kernel(
    d, radix, *refs,
):
    got_refs, refs = refs[: radix - 1], refs[radix - 1 :]
    group_ref, glog_ref, prefix_ref, plog_ref = refs[:4]
    send_ref, group_out, glog_out, prefix_out, plog_out, states, logs = refs[4:]
    mine = (lax.axis_index("seq") // d) % radix
    states[0] = group_ref[...]
    logs[0] = glog_ref[...]
    for k, got_ref in enumerate(got_refs):
        other, other_log = unpack(got_ref)
        states[k + 1] = other
        logs[k + 1] = jnp.broadcast_to(other_log, logs.shape[1:])
    total = jnp.zeros(group_ref.shape, F32)
    total_log = jnp.zeros((1, total.shape[1]), F32)
    early, early_log = total, total_log
    for m in range(radix):
        state = states[pl.ds(m ^ mine, 1)][0]
        log = logs[pl.ds(m ^ mine, 1)][0, 0:1]
        if m:
            early = jnp.where(mine == m, total, early)
            early_log = jnp.where(mine == m, total_log, early_log)
            state = jnp.exp(log) * total + state
        total = state
        total_log = total_log + log
    prefix_log = plog_ref[0:1, :]
    prefix_out[...] = prefix_ref[...] + jnp.exp(prefix_log) * early
    plog_out[...] = jnp.broadcast_to(prefix_log + early_log, plog_out.shape)
    new_log = jnp.broadcast_to(total_log, glog_out.shape)
    group_out[...] = total
    glog_out[...] = new_log
    send_ref[0:STATE, :] = total.astype(BF16)
    send_ref[STATE : STATE + 8, :] = pack_logs(new_log)


def combine(d, got, group, glog, prefix, plog):
    radix = len(got) + 1
    state = jax.ShapeDtypeStruct(group.shape, F32)
    log = jax.ShapeDtypeStruct(glog.shape, F32)
    return pl.pallas_call(
        functools.partial(combine_kernel, d, radix),
        out_shape=(jax.ShapeDtypeStruct(got[0].shape, BF16), state, log, state, log),
        grid_spec=pltpu.PrefetchScalarGridSpec(
            num_scalar_prefetch=0,
            grid=(1,),
            in_specs=[VMEM] * (radix + 3),
            out_specs=(VMEM,) * 5,
            scratch_shapes=[
                pltpu.VMEM((radix, *group.shape), F32),
                pltpu.VMEM((radix, *glog.shape), F32),
            ],
        ),
        compiler_params=pltpu.CompilerParams(vmem_limit_bytes=8 << 20),
        name="combine",
    )(*got, group, glog, prefix, plog)


def join_kernel(d, a_ref, b_ref, c_ref, *refs):
    o_ref, ss_ref, s_scr = refs[-3:]
    upper = (lax.axis_index("seq") & d) != 0
    for p, lanes in enumerate(part_lanes(o_ref.shape[1])):
        got_ref, prefix_ref, plog_ref = refs[3 * p : 3 * p + 3]
        other, _ = unpack(got_ref)
        prefix = prefix_ref[...]
        entering = jnp.where(upper, prefix + jnp.exp(plog_ref[0:1, :]) * other, prefix)
        s_scr[:, lanes] = entering.astype(BF16)

    part = 256
    ones = jnp.ones((8, 2 * LANES), BF16)
    for at in range(0, o_ref.shape[0], part):
        rows = slice(at, at + part)
        gated = a_ref[rows, :] + b_ref[rows, :] * mm(c_ref[rows, :], s_scr[...])
        o_ref[rows, :] = gated
        squared = gated * gated
        folded = sum(squared[:, k : k + LANES] for k in range(0, squared.shape[1], LANES))
        hi, lo = split2(folded)
        ss_ref[:, rows] = mm_nt(ones, jnp.concatenate([hi, lo], axis=1))[0:1]


def join(d, a, b, c, entering):
    total, width = a.shape
    return pl.pallas_call(
        functools.partial(join_kernel, d),
        out_shape=(jax.ShapeDtypeStruct((total, width), F32), jax.ShapeDtypeStruct((1, total), F32)),
        grid_spec=pltpu.PrefetchScalarGridSpec(
            num_scalar_prefetch=0,
            grid=(1,),
            in_specs=[VMEM] * (3 + len(entering)),
            out_specs=(VMEM, VMEM),
            scratch_shapes=[pltpu.VMEM((STATE, width), BF16)],
        ),
        compiler_params=pltpu.CompilerParams(
            dimension_semantics=("arbitrary",), vmem_limit_bytes=10 << 20
        ),
        name="join",
    )(a, b, c, *entering)


def norm_kernel(inner_width, g_ref, gain_ref, *refs):
    *squares_refs, o_hbm, o_ref, sems = refs
    rows, width = o_ref.shape
    copies = []
    for part in range(rows // LANES):
        here = slice(part * LANES, (part + 1) * LANES)
        squares = sum(r[:, here] for r in squares_refs)
        scale = lax.rsqrt(squares / inner_width + 1e-05)
        column = jnp.broadcast_to(scale, (LANES, LANES)).T
        for lane in range(width // LANES):
            lanes = slice(lane * LANES, (lane + 1) * LANES)
            o_ref[here, lanes] = (g_ref[here, lanes] * column * gain_ref[:, lanes]).astype(BF16)
        copies.append(pltpu.make_async_copy(o_ref.at[here], o_hbm.at[here], sems.at[part]))
        copies[-1].start()
    for copy in copies:
        copy.wait()


def norm(gated, squares, gain, inner_width):
    total, width = gated.shape
    return pl.pallas_call(
        functools.partial(norm_kernel, inner_width),
        out_shape=jax.ShapeDtypeStruct((total, width), BF16),
        in_specs=[VMEM] * (2 + len(squares)),
        out_specs=pl.BlockSpec(memory_space=pl.ANY),
        scratch_shapes=[
            pltpu.VMEM((total, width), BF16),
            pltpu.SemaphoreType.DMA((total // LANES,)),
        ],
        compiler_params=pltpu.CompilerParams(vmem_limit_bytes=8 << 20),
        name="norm",
    )(gated, gain, *squares)


def stages(shards):
    out, d = [], 1
    while d < shards:
        radix = 4 if 8 * d <= shards else 2
        out.append((d, radix))
        d *= radix
    return out


def body(
    tokens,
    routes,
    gate_inner_weight,
    state_map_weight,
    step_size_weight,
    adapter_down_weight,
    adapter_up_weight,
    inner_conv_taps,
    state_map_taps,
    inner_conv_bias,
    state_map_conv_bias,
    step_size_bias,
    head_decay_rate,
    direct_head_scale,
    gated_norm_scale,
):
    n = lax.axis_size("exp")
    shards = lax.axis_size("seq")
    local, features = tokens.shape
    total = local * n
    width = gate_inner_weight.shape[2]
    experts = adapter_up_weight.shape[0]
    rank = 8
    per = local // CHUNK

    down = {0: adapter_down_weight.T}
    for k in range(2, n, 2):
        down[k] = swap(down[0], "exp", k)
    *pieces, note = pack(tokens, routes.reshape(1, local), max(per - 1, 1))
    notes = {0: note}
    far = {}
    for k in range(2, n, 2):
        notes[k] = swap(note, "exp", k)
    wz = gate_inner_weight.reshape(features, 2 * width)
    for q in range(per):
        if q and q == per - 1:
            late, wz = lax.optimization_barrier((tokens, wz))
            pieces.append(late[q * CHUNK :])
        for k in range(2, n, 2):
            far[k, q] = swap(pieces[q], "exp", k)
    sibling = swap(tokens, "exp", 1)
    for k in range(0, n, 2):
        down[k + 1] = swap(down[k], "exp", 1)
        notes[k + 1] = swap(notes[k], "exp", 1)
    downs = [down[k] for k in range(n)]
    notes = [notes[k] for k in range(n)]
    up = adapter_up_weight.reshape(experts, 2 * width)
    call = functools.partial(
        project, devices=n, wz=wz, wbc=state_map_weight, up=up, rank=rank,
        dtb=step_size_bias[None, :], rate=head_decay_rate[None, :],
    )
    z, *sums, lift, rows, tails, rim, wsm, masks = call(
        [tokens, sibling], notes=notes, dt_t=step_size_weight.T, downs=downs
    )
    gates = [gate_project([rows], [lift], wz, up, n)]
    rim = lax.ppermute(rim, "seq", [(i, (i + 1) % shards) for i in range(shards)])
    params = [
        inner_conv_taps, state_map_taps, inner_conv_bias[None, :], state_map_conv_bias[None, :],
    ]
    kept = run_states(total, z, sums, z, tails, rim, params, width, per, None, None)
    far_rows = {}
    for q in range(per):
        for k in range(2, n, 2):
            mine = far[k, q]
            other = swap(mine, "exp", 1)
            older = far_rows[k, q - 1][2] if q else z
            pieces = [[mine, other]] if (k, q) != (n - 2, per - 1) else [[mine], [other]]
            found = []
            for p, piece in enumerate(pieces):
                new_z, *sums, lift, rows = call(
                    piece,
                    route_from=tuple(
                        ((k + p + m) * local + q * CHUNK, CHUNK) for m in range(len(piece))
                    ),
                    routes=masks,
                    wsm=wsm,
                )
                kept = run_states(
                    total, new_z, sums, older, tails, rim, params, width, per, (k + p, q), kept
                )
                found.append((rows, lift))
            far_rows[k, q] = ([f[0] for f in found], [f[1] for f in found], new_z)
    xc, cum, cum_t, step_t, updates, totals = kept
    states, before, parts = stitch(updates, totals)
    for d, radix in stages(shards):
        last = 2 * d == shards
        got = {}
        for p, part in enumerate(parts):
            for k in range(1, radix):
                got[p, k] = swap(part[0], "seq", d * k)
        for p, part in enumerate(parts):
            arrived = [got[p, k] for k in range(1, radix)]
            if last:
                parts[p] = [arrived[0], *part[3:]]
            else:
                parts[p] = combine(d, arrived, *part[1:])
    entering = [x for part in parts for x in part]
    for k in range(2, n, 2):
        for q in range(per):
            gates.append(gate_project(far_rows[k, q][0], far_rows[k, q][1], wz, up, n))
    a, b, c = run_outputs(
        xc, cum, cum_t, step_t, before, states, gates, direct_head_scale[None, :], local
    )
    gated, mine = join(shards // 2, a, b, c, entering)
    others = []
    for k in range(1, n):
        others.append(swap(mine, "exp", k))
    return norm(gated, [mine, *others], gated_norm_scale[None, :], width * n)


def solution(mesh):
    in_specs = (
        P(("seq", "exp"), None),
        P(("seq", "exp"), None),
        P(None, None, "exp"),
        P(),
        P(None, "exp"),
        P(None, "exp"),
        P(None, None, "exp"),
        P(None, "exp"),
        P(),
        P("exp"),
        P(),
        P("exp"),
        P("exp"),
        P("exp"),
        P("exp"),
    )
    out_specs = P("seq", "exp")

    return jax.shard_map(body, mesh=mesh, in_specs=in_specs, out_specs=out_specs, check_vma=False)
```

```python
import functools

import jax
import jax.numpy as jnp
from jax import lax
from jax.experimental import pallas as pl
from jax.experimental.pallas import tpu as pltpu
from jax.sharding import PartitionSpec as P


STATE = 128
HEADDIM = 64
CHUNK = 128
HEADS_PAD = 16
LANES = 128
F32 = jnp.float32
BF16 = jnp.bfloat16


def swap(block, axis, mask):
    return lax.ppermute(block, axis, [(i, i ^ mask) for i in range(lax.axis_size(axis))])


def split3(value):
    hi = value.astype(BF16)
    rest = value - hi.astype(F32)
    mid = rest.astype(BF16)
    lo = (rest - mid.astype(F32)).astype(BF16)
    return hi, mid, lo


def split2(value):
    hi = value.astype(BF16)
    return hi, (value - hi.astype(F32)).astype(BF16)


def mm(a, b):
    return jnp.dot(a, b, preferred_element_type=F32)


def mm_nt(a, b):
    return lax.dot_general(a, b, (((1,), (1,)), ((), ())), preferred_element_type=F32)


def silu_of_double(half):
    return half + half * jnp.tanh(half)


def silu(v):
    return silu_of_double(0.5 * v)


def route_mask(e, route_row, experts_dev, rank):
    column = lax.broadcasted_iota(jnp.int32, (LANES, route_row.shape[1]), 0)
    per_dev = experts_dev * rank
    expert = ((column // per_dev) ^ e) * experts_dev + (column % per_dev) // rank
    return jnp.where(expert.astype(F32) == route_row, 1.0, 0.0)


VMEM = pl.BlockSpec(memory_space=pltpu.VMEM)


def up_rows(up_ref, e, devices, lanes):
    cols = up_ref.shape[0] // devices
    return jnp.concatenate(
        [up_ref[pl.ds(pl.multiple_of((e ^ r) * cols, cols), cols), lanes] for r in range(devices)], axis=0
    )


def pack_kernel(tokens_ref, route_ref, *refs):
    halves, (note_ref, tail, route, sems) = refs[:-4], refs[-4:]
    rows = halves[0].shape[0]
    copies = [
        pltpu.make_async_copy(tokens_ref.at[q * rows : (q + 1) * rows], half, sems.at[q])
        for q, half in enumerate(halves)
    ]
    last = tokens_ref.shape[0] - 8
    copies.append(pltpu.make_async_copy(tokens_ref.at[last:], tail, sems.at[len(halves)]))
    copies.append(pltpu.make_async_copy(route_ref, route, sems.at[len(halves) + 1]))
    for copy in copies[::-1]:
        copy.start()
    copies[-1].wait()
    copies[-2].wait()
    route = route[...].astype(F32)
    route = jnp.concatenate([route, jnp.zeros((1, tail.shape[1] - route.shape[1]), F32)], axis=1)
    row = lax.broadcasted_iota(jnp.int32, tail.shape, 0)
    note_ref[...] = jnp.where(row == 0, route, tail[...].astype(F32)).astype(BF16)
    for copy in copies[:-2]:
        copy.wait()


def pack(tokens, route_row, per):
    features = tokens.shape[1]
    anywhere = pl.BlockSpec(memory_space=pltpu.HBM)
    piece = jax.ShapeDtypeStruct((CHUNK, features), BF16)
    return pl.pallas_call(
        pack_kernel,
        out_shape=(piece,) * per + (jax.ShapeDtypeStruct((8, features), BF16),),
        in_specs=[anywhere, anywhere],
        out_specs=(VMEM,) * (per + 1),
        scratch_shapes=[
            pltpu.VMEM((8, features), BF16),
            pltpu.VMEM(route_row.shape, route_row.dtype),
            pltpu.SemaphoreType.DMA((per + 2,)),
        ],
        compiler_params=pltpu.CompilerParams(vmem_limit_bytes=4 << 20),
        name="pack",
    )(tokens, route_row)


def pad_lanes(row):
    pad = LANES - row.shape[1]
    return jnp.concatenate([row, jnp.zeros((row.shape[0], pad), F32)], axis=1)


def step_chain(raw, bias, rate):
    column = lambda row: jnp.broadcast_to(pad_lanes(row), (LANES, LANES)).T[:HEADS_PAD]
    raw = pad_lanes(raw).T[:HEADS_PAD] + column(bias)
    step = jnp.maximum(raw, 0.0) + jnp.log1p(jnp.exp(-jnp.abs(raw)))
    decay = -column(rate) * step
    rows = lax.broadcasted_iota(jnp.int32, (CHUNK, CHUNK), 0)
    cols = lax.broadcasted_iota(jnp.int32, (CHUNK, CHUNK), 1)
    upper = jnp.where(rows <= cols, 1.0, 0.0).astype(BF16)
    sums = mm(jnp.concatenate(split3(decay), axis=0), upper)
    cum_t = sums[:HEADS_PAD] + sums[HEADS_PAD : 2 * HEADS_PAD] + sums[2 * HEADS_PAD :]
    carried = jnp.exp(jnp.broadcast_to(cum_t[:, CHUNK - 1 :], cum_t.shape) - cum_t) * step
    blank = jnp.zeros((LANES - 2 * HEADS_PAD, CHUNK), F32)
    return jnp.concatenate([cum_t, carried, blank], axis=0).T, cum_t, step


def project_kernel(cfg, *refs):
    counts, route_from, devices, cols, rank, near = cfg
    x_refs, refs = refs[: len(counts)], refs[len(counts):]
    if near:
        n_refs, refs = refs[:devices], refs[devices:]
    else:
        route_ref, refs = refs[0], refs[1:]
    w_ref, wbc_ref, up_ref, dtb_ref, rate_ref = refs[:5]
    refs = refs[5:]
    if near:
        dt_ref, d_refs, refs = refs[0], refs[1 : 1 + devices], refs[1 + devices:]
        z_ref, cum_ref, cum_t_ref, step_t_ref, lift_ref, x_scr, tails_ref, rim_ref, wsm_t_ref, route_ref, lift_scr, wsm_ref = refs
    else:
        wsm_ref, z_ref, cum_ref, cum_t_ref, step_t_ref, lift_ref, x_scr = refs
        lift_scr = lift_ref
    e = lax.axis_index("exp")
    rows = sum(counts)

    at = 0
    for x_ref, n in zip(x_refs, counts):
        x_scr[at : at + n, :] = x_ref[...]
        at += n
    if near:
        for r in range(devices):
            x_scr[at + 8 * r : at + 8 * r + 8, :] = n_refs[r][...]
        wsm_ref[LANES:, :] = jnp.zeros((wsm_ref.shape[0] - LANES, wsm_ref.shape[1]), BF16)
        wsm_ref[LANES : LANES + dt_ref.shape[0], :] = dt_ref[...]
        for r in range(devices):
            wsm_ref[r * cols : (r + 1) * cols, :] = d_refs[r][...]
    if near:
        weights = jnp.concatenate([d[...] for d in d_refs], axis=0).astype(F32)
        wide = 512
        for at in range(0, weights.shape[1], wide):
            wsm_t_ref[at : at + wide, :LANES] = weights[:, at : at + wide].T.astype(BF16)
        small = mm_nt(x_scr[...], wsm_ref[...])
        steps = wsm_ref[LANES:, :].astype(F32)
        steps = jnp.concatenate([steps, jnp.zeros((LANES - 16, steps.shape[1]), F32)], axis=0)
        for at in range(0, weights.shape[1], wide):
            wsm_t_ref[at : at + wide, LANES:] = steps[:, at : at + wide].T.astype(BF16)
    else:
        small = mm(x_scr[...], wsm_ref[...])[:, : LANES + 16]

    def mask_of(r, lane):
        row = n_refs[r][0:1, lane : lane + LANES].astype(F32)
        return route_mask(e, row, cols // rank, rank).T

    masks = []
    if near:
        whole = route_ref.shape[0] // devices
        for r in range(devices):
            for lane in range(0, whole, LANES):
                mask = mask_of(r, lane)
                route_ref[r * whole + lane : r * whole + lane + LANES, :] = mask.astype(BF16)
                if r < 2:
                    masks.append(mask)
        for r in range(devices):
            masks.append(route_ref[(r + 1) * whole - 16 : (r + 1) * whole, :].astype(F32)[8:])
    else:
        masks = [route_ref[first : first + n, :].astype(F32) for first, n in route_from]
    lift = jnp.where(jnp.concatenate(masks, axis=0) > 0.5, small[:, :LANES], 0.0).astype(BF16)
    lift_scr[...] = lift
    for c in range(rows // CHUNK):
        here = slice(c * CHUNK, (c + 1) * CHUNK)
        both, cum_t, step_t = step_chain(small[here, LANES:], dtb_ref[...], rate_ref[...])
        cum_ref[here, :] = both
        cum_t_ref[c] = cum_t
        step_t_ref[c] = step_t
    if near:
        lift_ref[...] = lift[:rows]

    def put(lanes, value):
        z_ref[:, lanes] = value[:rows]
        if near:
            tails_ref[:, lanes] = value[rows:]

    width = z_ref.shape[1]
    inner = up_ref.shape[1] // 2
    tn = 256 if inner % 256 == 0 else 128
    for at in range(0, inner, tn):
        lanes = slice(inner + at, inner + at + tn)
        up = up_rows(up_ref, e, devices, lanes)
        put(slice(at, at + tn), mm(x_scr[...], w_ref[:, lanes]) + mm(lift_scr[...], up))
    for at in range(0, width - inner, tn):
        put(slice(inner + at, inner + at + tn), mm(x_scr[...], wbc_ref[:, at : at + tn]))
    if near:
        row = ((devices - 1) ^ e) * 8
        rim_ref[...] = tails_ref[pl.ds(pl.multiple_of(row, 8), 8), :]


def project(xs, wz, wbc, up, dtb, rate, rank, devices, notes=None, dt_t=None, downs=None, route_from=None, routes=None, wsm=None):
    counts = tuple(x.shape[0] for x in xs)
    rows = sum(counts)
    features = wz.shape[0]
    width = up.shape[1] // 2 + wbc.shape[1]
    near = wsm is None
    args = list(xs) + (list(notes) if near else [routes]) + [wz, wbc, up, dtb, rate]
    args += [dt_t, *downs] if near else [wsm]
    out_shape = [
        jax.ShapeDtypeStruct((rows, width), F32),
        jax.ShapeDtypeStruct((rows, LANES), F32),
        jax.ShapeDtypeStruct((rows // CHUNK, HEADS_PAD, CHUNK), F32),
        jax.ShapeDtypeStruct((rows // CHUNK, HEADS_PAD, CHUNK), F32),
        jax.ShapeDtypeStruct((rows, LANES), BF16),
    ]
    extra = 8 * devices if near else 0
    out_shape.append(jax.ShapeDtypeStruct((rows + extra, features), BF16))
    scratch = []
    if near:
        out_shape += [jax.ShapeDtypeStruct((extra, width), F32), jax.ShapeDtypeStruct((8, width), F32)]
        out_shape.append(jax.ShapeDtypeStruct((features, 2 * LANES), BF16))
        out_shape.append(jax.ShapeDtypeStruct((devices * counts[0], LANES), BF16))
        scratch.append(pltpu.VMEM((rows + extra, LANES), BF16))
        scratch.append(pltpu.VMEM((LANES + 16, features), BF16))
    cfg = (counts, route_from, devices, LANES // devices, rank, near)
    return pl.pallas_call(
        functools.partial(project_kernel, cfg),
        out_shape=tuple(out_shape),
        grid_spec=pltpu.PrefetchScalarGridSpec(
            num_scalar_prefetch=0,
            grid=(1,),
            in_specs=[VMEM] * len(args),
            out_specs=(VMEM,) * len(out_shape),
            scratch_shapes=scratch,
        ),
        cost_estimate=pl.CostEstimate(
            flops=2 * rows * features * (width + 256),
            transcendentals=0,
            bytes_accessed=2 * features * (width + rows) + 4 * rows * width,
        ),
        compiler_params=pltpu.CompilerParams(
            dimension_semantics=("arbitrary",), vmem_limit_bytes=16 << 20
        ),
        name="project",
    )(*args)


def gate_kernel(rows, devices, *refs):
    x_refs, lift_refs = refs[: len(rows)], refs[len(rows) : 2 * len(rows)]
    w_ref, up_ref, g_ref = refs[-3:]
    width = g_ref.shape[1]
    tn = 256 if width % 256 == 0 else 128
    for lane in range(0, width, tn):
        lanes = slice(lane, lane + tn)
        up = up_rows(up_ref, lax.axis_index("exp"), devices, lanes)
        at = 0
        for x_ref, lift_ref, n in zip(x_refs, lift_refs, rows):
            g_ref[at : at + n, lanes] = mm(x_ref[0:n, :], w_ref[:, lanes]) + mm(lift_ref[...], up)
            at += n


def gate_project(xs, lifts, wz, up, devices):
    counts = tuple(lift.shape[0] for lift in lifts)
    rows = sum(counts)
    features = wz.shape[0]
    width = up.shape[1] // 2
    args = list(xs) + list(lifts) + [wz, up]
    return pl.pallas_call(
        functools.partial(gate_kernel, counts, devices),
        out_shape=jax.ShapeDtypeStruct((rows, width), F32),
        in_specs=[VMEM] * len(args),
        out_specs=VMEM,
        cost_estimate=pl.CostEstimate(
            flops=2 * rows * features * width,
            transcendentals=0,
            bytes_accessed=2 * features * (width + rows) + 4 * rows * width,
        ),
        compiler_params=pltpu.CompilerParams(vmem_limit_bytes=12 << 20),
        name="gate_project",
    )(*args)


def spread(value, width):
    rows = value.shape[0]
    left = lax.broadcasted_iota(jnp.int32, (rows, LANES), 1) < HEADDIM
    parts = []
    for p in range(width // LANES):
        a = jnp.broadcast_to(value[:, 2 * p : 2 * p + 1], (rows, LANES))
        b = jnp.broadcast_to(value[:, 2 * p + 1 : 2 * p + 2], (rows, LANES))
        parts.append(jnp.where(left, a, b))
    return jnp.concatenate(parts, axis=1)


def state_kernel(
    cfg, z_all, sums_all, sums_t_all, steps_t_all, older_all, tails_ref, rim_ref,
    taps_ref, mtaps_ref, bias_ref, mbias_ref, *refs,
):
    width, per, far, where_am_i = cfg
    xc_all, cum_all, cum_t_all, step_t_all, update_all, total_all, ext = refs[-7:]
    e = lax.axis_index("exp")
    r, q = where_am_i(pl.program_id(0))
    block = r ^ e
    at = pl.program_id(0) * CHUNK
    there = pl.ds(pl.multiple_of(at, CHUNK), CHUNK)
    z_ref = z_all.at[there]
    older = r % 2 * CHUNK + CHUNK - 8 if far else jnp.maximum(at - 8, 0)
    prev_ref = older_all.at[pl.ds(pl.multiple_of(older, 8), 8)]
    chunk = block * per + q
    here = pl.ds(pl.multiple_of(chunk * CHUNK, CHUNK), CHUNK)
    xc_ref, cum_ref = xc_all.at[here], cum_all.at[here]
    cum_t_ref, step_t_ref = cum_t_all.at[pl.ds(chunk, 1)], step_t_all.at[pl.ds(chunk, 1)]
    update_ref, total_ref = update_all.at[pl.ds(chunk, 1)], total_all.at[pl.ds(chunk, 1)]
    before = pl.multiple_of((jnp.maximum(block - 1, 0) ^ e) * 8, 8)
    rim = jnp.where(lax.axis_index("seq") == 0, 0.0, rim_ref[...])
    first = jnp.where(block == 0, rim, tails_ref[pl.ds(before, 8), :])
    ext[0:8, :] = jnp.where(q == 0, first, prev_ref[...])
    ext[8 : 8 + CHUNK, :] = z_ref[...]
    taps = taps_ref.shape[0]
    outs = []
    for tr, br, lanes in (
        (taps_ref, bias_ref, slice(0, width)),
        (mtaps_ref, mbias_ref, slice(width, width + 2 * STATE)),
    ):
        halved = 0.5 * tr[...]
        acc = 0.5 * br[...] + halved[taps - 1 : taps, :] * ext[8 : 8 + CHUNK, lanes]
        for k in range(taps - 1):
            start = 8 - (taps - 1) + k
            acc = acc + halved[k : k + 1, :] * ext[start : start + CHUNK, lanes]
        out = silu_of_double(acc)
        xc_ref[:, lanes] = out
        outs.append(out)
    x, maps = outs

    both = sums_all[there, :]
    cum_ref[...] = both
    cum_t_ref[0] = sums_t_all[pl.ds(pl.program_id(0), 1)][0]
    step_t_ref[0] = steps_t_all[pl.ds(pl.program_id(0), 1)][0]
    total_ref[0] = jnp.broadcast_to(both[CHUNK - 1 : CHUNK, :], total_ref.shape[1:])

    xs = (spread(both[:, HEADS_PAD:], width) * x).astype(BF16)
    b_hi, b_lo = split2(maps[:, :STATE].T)
    update_ref[0] = mm(jnp.concatenate([b_hi, b_lo], axis=1), jnp.concatenate([xs, xs], axis=0))


def run_states(total, z, sums, older, tails, rim, params, width, per, far, buffers):
    wide = z.shape[1]
    chunks = total // CHUNK
    if far is None:
        steps = 2 * per
        at = lambda c: (c // per, c % per)
    else:
        steps = z.shape[0] // CHUNK
        at = lambda c: (far[0] + c, far[1])

    args = [z, *sums, older, tails, rim, *params]
    in_specs = [VMEM] * len(args)
    aliases = {}
    if buffers is not None:
        for n, buffer in enumerate(buffers):
            aliases[len(args)] = n
            args.append(buffer)
            in_specs.append(VMEM)
    return pl.pallas_call(
        functools.partial(state_kernel, (width, per, far is not None, at)),
        out_shape=(
            jax.ShapeDtypeStruct((total, wide), F32),
            jax.ShapeDtypeStruct((total, LANES), F32),
            jax.ShapeDtypeStruct((chunks, HEADS_PAD, CHUNK), F32),
            jax.ShapeDtypeStruct((chunks, HEADS_PAD, CHUNK), F32),
            jax.ShapeDtypeStruct((chunks, STATE, width), F32),
            jax.ShapeDtypeStruct((chunks, 8, LANES), F32),
        ),
        grid_spec=pltpu.PrefetchScalarGridSpec(
            num_scalar_prefetch=0,
            grid=(steps,),
            in_specs=in_specs,
            out_specs=(VMEM,) * 6,
            scratch_shapes=[pltpu.VMEM((CHUNK + 8, wide), F32)],
        ),
        input_output_aliases=aliases,
        cost_estimate=pl.CostEstimate(
            flops=2 * steps * CHUNK * width * 1000, transcendentals=steps * CHUNK * wide,
            bytes_accessed=12 * steps * CHUNK * wide,
        ),
        compiler_params=pltpu.CompilerParams(
            dimension_semantics=("arbitrary",), vmem_limit_bytes=12 << 20
        ),
        name="run_states",
    )(*args)


def part_lanes(width):
    middle = (width // LANES * 2 // 3) * LANES
    return [slice(0, middle), slice(middle, width)]


def stitch_kernel(width, update_ref, total_ref, entry_ref, before_ref, *refs):
    chunks = update_ref.shape[0]
    state = jnp.zeros(update_ref.shape[1:], F32)
    log = jnp.zeros(total_ref.shape[1:], F32)
    for c in range(chunks):
        entry_ref[c] = state.astype(BF16)
        before_ref[c] = log
        total = total_ref[c]
        state = spread(jnp.exp(total), width)[0:1, :] * state + update_ref[c]
        log = log + total
    wide = spread(log, width)
    for p, lanes in enumerate(part_lanes(width)):
        send_ref, group_ref, glog_ref, prefix_ref, plog_ref = refs[5 * p : 5 * p + 5]
        group_ref[...] = state[:, lanes]
        glog_ref[...] = wide[:, lanes]
        send_ref[0:STATE, :] = state[:, lanes].astype(BF16)
        send_ref[STATE : STATE + 8, :] = pack_logs(wide[:, lanes])
        prefix_ref[...] = jnp.zeros(prefix_ref.shape, F32)
        plog_ref[...] = jnp.zeros(plog_ref.shape, F32)


def stitch(updates, totals):
    _, state, width = updates.shape
    outs = [jax.ShapeDtypeStruct(updates.shape, BF16), jax.ShapeDtypeStruct(totals.shape, F32)]
    for lanes in part_lanes(width):
        wide = lanes.stop - lanes.start
        outs += [
            jax.ShapeDtypeStruct((state + 8, wide), BF16),
            jax.ShapeDtypeStruct((state, wide), F32),
            jax.ShapeDtypeStruct((8, wide), F32),
            jax.ShapeDtypeStruct((state, wide), F32),
            jax.ShapeDtypeStruct((8, wide), F32),
        ]
    entry, before, *rest = pl.pallas_call(
        functools.partial(stitch_kernel, width),
        out_shape=tuple(outs),
        in_specs=[VMEM, VMEM],
        out_specs=(VMEM,) * len(outs),
        compiler_params=pltpu.CompilerParams(vmem_limit_bytes=8 << 20),
        name="stitch",
    )(updates, totals)
    return entry, before, [rest[:5], rest[5:]]


def output_kernel(
    cfg, xc_all, cum_all, cum_t_all, step_t_all, before_all, local_all, direct_ref, *refs,
):
    width, per, gate_count, skip = cfg
    g_refs, (a_all, b_all, c_all) = refs[:gate_count], refs[-3:]
    turn = pl.program_id(0) + skip
    r, q = turn // per, turn % per
    c = (r ^ lax.axis_index("exp")) * per + q
    here = pl.ds(pl.multiple_of(c * CHUNK, CHUNK), CHUNK)
    near = pl.ds(pl.multiple_of(jnp.where(r < 2, r * per + q, 0) * CHUNK, CHUNK), CHUNK)
    far = pl.ds(pl.multiple_of(r % 2 * CHUNK, CHUNK), CHUNK)
    xc_ref, cum_ref = xc_all.at[here], cum_all.at[here]
    before_ref, local_ref = before_all.at[pl.ds(c, 1)], local_all.at[pl.ds(c, 1)]
    a_ref, b_ref, c_ref = a_all.at[here], b_all.at[here], c_all.at[here]
    bmap = xc_ref[:, width : width + STATE]
    cmap = xc_ref[:, width + STATE :]
    cum = cum_ref[...]
    b_hi, b_lo = split2(bmap)
    c_hi, c_lo = split2(cmap)
    c_ref[...] = c_hi
    gram = mm_nt(jnp.concatenate([c_hi, c_lo], axis=1), jnp.concatenate([b_hi, b_hi], axis=1))
    gram = gram + mm_nt(c_hi, b_lo)
    cum_t = cum_t_all[pl.ds(c, 1)][0]
    step_t = step_t_all[pl.ds(c, 1)][0]
    rows = lax.broadcasted_iota(jnp.int32, (CHUNK, CHUNK), 0)
    cols = lax.broadcasted_iota(jnp.int32, (CHUNK, CHUNK), 1)
    causal = rows >= cols
    left = cols < HEADDIM
    direct = pad_lanes(direct_ref[...])
    for p in range(width // LANES):
        lanes = slice(p * LANES, (p + 1) * LANES)
        ws, cs = [], []
        for h in (2 * p, 2 * p + 1):
            column = jnp.broadcast_to(cum[:, h : h + 1], (CHUNK, CHUNK))
            differ = jnp.where(causal, column - cum_t[h : h + 1, :], -jnp.inf)
            ws.append((jnp.exp(differ) * (gram * step_t[h : h + 1, :])).astype(BF16))
            cs.append(column)
        x = xc_ref[:, lanes]
        xb = jnp.concatenate([jnp.where(left, x, 0.0), jnp.where(left, 0.0, x)], axis=0)
        both = lambda v: jnp.where(
            left[0:1, :],
            jnp.broadcast_to(v[:, 2 * p : 2 * p + 1], (1, LANES)),
            jnp.broadcast_to(v[:, 2 * p + 1 : 2 * p + 2], (1, LANES)),
        )
        inside = mm(jnp.concatenate(ws, axis=1), xb.astype(BF16))
        fade = jnp.exp(jnp.where(left, cs[0], cs[1]))
        y = inside + fade * mm(c_hi, local_ref[0, :, lanes]) + both(direct) * x
        gate = g_refs[0][near, lanes]
        for k, g_ref in enumerate(g_refs[1:]):
            found = (r // 2 == k // per + 1) & (q == k % per)
            gate = jnp.where(found, g_ref[far, lanes], gate)
        gate = silu(gate)
        a_ref[:, lanes] = y * gate
        b_ref[:, lanes] = fade * jnp.exp(both(before_ref[0, 0:1, :])) * gate


def run_outputs(xc, cum, cum_t, step_t, before, local_states, gates, direct, local, skip, count, buffers):
    total, _ = xc.shape
    width = gates[0].shape[1]
    per = local // CHUNK
    args = [xc, cum, cum_t, step_t, before, local_states, direct, *gates]
    aliases = {len(args) + k: k for k in range(len(buffers))}
    return pl.pallas_call(
        functools.partial(output_kernel, (width, per, len(gates), skip)),
        out_shape=(
            jax.ShapeDtypeStruct((total, width), F32),
            jax.ShapeDtypeStruct((total, width), F32),
            jax.ShapeDtypeStruct((total, STATE), BF16),
        ),
        grid_spec=pltpu.PrefetchScalarGridSpec(
            num_scalar_prefetch=0,
            grid=(count,),
            in_specs=[VMEM] * (len(args) + len(buffers)),
            out_specs=(VMEM,) * 3,
        ),
        input_output_aliases=aliases,
        cost_estimate=pl.CostEstimate(
            flops=2 * total * width * 1500, transcendentals=total * width * 4, bytes_accessed=16 * total * width
        ),
        compiler_params=pltpu.CompilerParams(
            dimension_semantics=("arbitrary",), vmem_limit_bytes=12 << 20
        ),
        name="run_outputs",
    )(*args, *buffers)


def pack_logs(wide):
    hi, mid, lo = split3(wide)
    row = lax.broadcasted_iota(jnp.int32, wide.shape, 0)
    lo = jnp.where(row == 2, lo.astype(F32), 0.0)
    return jnp.where(row == 0, hi.astype(F32), jnp.where(row == 1, mid.astype(F32), lo)).astype(BF16)


def unpack(got_ref):
    other = got_ref[0:STATE, :].astype(F32)
    logs = got_ref[STATE : STATE + 8, :].astype(F32)
    log = logs[0:1, :] + logs[1:2, :] + logs[2:3, :]
    return other, log


def combine_kernel(
    d, radix, *refs,
):
    got_refs, refs = refs[: radix - 1], refs[radix - 1 :]
    group_ref, glog_ref, prefix_ref, plog_ref = refs[:4]
    send_ref, group_out, glog_out, prefix_out, plog_out, states, logs = refs[4:]
    mine = (lax.axis_index("seq") // d) % radix
    states[0] = group_ref[...]
    logs[0] = glog_ref[...]
    for k, got_ref in enumerate(got_refs):
        other, other_log = unpack(got_ref)
        states[k + 1] = other
        logs[k + 1] = jnp.broadcast_to(other_log, logs.shape[1:])
    total = jnp.zeros(group_ref.shape, F32)
    total_log = jnp.zeros((1, total.shape[1]), F32)
    early, early_log = total, total_log
    for m in range(radix):
        state = states[pl.ds(m ^ mine, 1)][0]
        log = logs[pl.ds(m ^ mine, 1)][0, 0:1]
        if m:
            early = jnp.where(mine == m, total, early)
            early_log = jnp.where(mine == m, total_log, early_log)
            state = jnp.exp(log) * total + state
        total = state
        total_log = total_log + log
    prefix_log = plog_ref[0:1, :]
    prefix_out[...] = prefix_ref[...] + jnp.exp(prefix_log) * early
    plog_out[...] = jnp.broadcast_to(prefix_log + early_log, plog_out.shape)
    new_log = jnp.broadcast_to(total_log, glog_out.shape)
    group_out[...] = total
    glog_out[...] = new_log
    send_ref[0:STATE, :] = total.astype(BF16)
    send_ref[STATE : STATE + 8, :] = pack_logs(new_log)


def combine(d, got, group, glog, prefix, plog):
    radix = len(got) + 1
    state = jax.ShapeDtypeStruct(group.shape, F32)
    log = jax.ShapeDtypeStruct(glog.shape, F32)
    return pl.pallas_call(
        functools.partial(combine_kernel, d, radix),
        out_shape=(jax.ShapeDtypeStruct(got[0].shape, BF16), state, log, state, log),
        grid_spec=pltpu.PrefetchScalarGridSpec(
            num_scalar_prefetch=0,
            grid=(1,),
            in_specs=[VMEM] * (radix + 3),
            out_specs=(VMEM,) * 5,
            scratch_shapes=[
                pltpu.VMEM((radix, *group.shape), F32),
                pltpu.VMEM((radix, *glog.shape), F32),
            ],
        ),
        compiler_params=pltpu.CompilerParams(vmem_limit_bytes=8 << 20),
        name="combine",
    )(*got, group, glog, prefix, plog)


def join_kernel(d, a_ref, b_ref, c_ref, *refs):
    o_ref, ss_ref, s_scr = refs[-3:]
    upper = (lax.axis_index("seq") & d) != 0
    for p, lanes in enumerate(part_lanes(o_ref.shape[1])):
        got_ref, prefix_ref, plog_ref = refs[3 * p : 3 * p + 3]
        other, _ = unpack(got_ref)
        prefix = prefix_ref[...]
        entering = jnp.where(upper, prefix + jnp.exp(plog_ref[0:1, :]) * other, prefix)
        s_scr[:, lanes] = entering.astype(BF16)

    part = 256
    ones = jnp.ones((8, 2 * LANES), BF16)
    for at in range(0, o_ref.shape[0], part):
        rows = slice(at, at + part)
        gated = a_ref[rows, :] + b_ref[rows, :] * mm(c_ref[rows, :], s_scr[...])
        o_ref[rows, :] = gated
        squared = gated * gated
        folded = sum(squared[:, k : k + LANES] for k in range(0, squared.shape[1], LANES))
        hi, lo = split2(folded)
        ss_ref[:, rows] = mm_nt(ones, jnp.concatenate([hi, lo], axis=1))[0:1]


def join(d, a, b, c, entering):
    total, width = a.shape
    return pl.pallas_call(
        functools.partial(join_kernel, d),
        out_shape=(jax.ShapeDtypeStruct((total, width), F32), jax.ShapeDtypeStruct((1, total), F32)),
        grid_spec=pltpu.PrefetchScalarGridSpec(
            num_scalar_prefetch=0,
            grid=(1,),
            in_specs=[VMEM] * (3 + len(entering)),
            out_specs=(VMEM, VMEM),
            scratch_shapes=[pltpu.VMEM((STATE, width), BF16)],
        ),
        compiler_params=pltpu.CompilerParams(
            dimension_semantics=("arbitrary",), vmem_limit_bytes=10 << 20
        ),
        name="join",
    )(a, b, c, *entering)


def norm_kernel(inner_width, g_ref, gain_ref, *refs):
    *squares_refs, o_hbm, o_ref, sems = refs
    rows, width = o_ref.shape
    copies = []
    for part in range(rows // LANES):
        here = slice(part * LANES, (part + 1) * LANES)
        squares = sum(r[:, here] for r in squares_refs)
        scale = lax.rsqrt(squares / inner_width + 1e-05)
        column = jnp.broadcast_to(scale, (LANES, LANES)).T
        for lane in range(width // LANES):
            lanes = slice(lane * LANES, (lane + 1) * LANES)
            o_ref[here, lanes] = (g_ref[here, lanes] * column * gain_ref[:, lanes]).astype(BF16)
        copies.append(pltpu.make_async_copy(o_ref.at[here], o_hbm.at[here], sems.at[part]))
        copies[-1].start()
    for copy in copies:
        copy.wait()


def norm(gated, squares, gain, inner_width):
    total, width = gated.shape
    return pl.pallas_call(
        functools.partial(norm_kernel, inner_width),
        out_shape=jax.ShapeDtypeStruct((total, width), BF16),
        in_specs=[VMEM] * (2 + len(squares)),
        out_specs=pl.BlockSpec(memory_space=pl.ANY),
        scratch_shapes=[
            pltpu.VMEM((total, width), BF16),
            pltpu.SemaphoreType.DMA((total // LANES,)),
        ],
        compiler_params=pltpu.CompilerParams(vmem_limit_bytes=8 << 20),
        name="norm",
    )(gated, gain, *squares)


def stages(shards):
    out, d = [], 1
    while d < shards:
        radix = 4 if 8 * d <= shards else 2
        out.append((d, radix))
        d *= radix
    return out


def body(
    tokens,
    routes,
    gate_inner_weight,
    state_map_weight,
    step_size_weight,
    adapter_down_weight,
    adapter_up_weight,
    inner_conv_taps,
    state_map_taps,
    inner_conv_bias,
    state_map_conv_bias,
    step_size_bias,
    head_decay_rate,
    direct_head_scale,
    gated_norm_scale,
):
    n = lax.axis_size("exp")
    shards = lax.axis_size("seq")
    local, features = tokens.shape
    total = local * n
    width = gate_inner_weight.shape[2]
    experts = adapter_up_weight.shape[0]
    rank = 8
    per = local // CHUNK

    down = {0: adapter_down_weight.T}
    for k in range(2, n, 2):
        down[k] = swap(down[0], "exp", k)
    *pieces, note = pack(tokens, routes.reshape(1, local), max(per - 1, 1))
    notes = {0: note}
    far = {}
    for k in range(2, n, 2):
        notes[k] = swap(note, "exp", k)
    wz = gate_inner_weight.reshape(features, 2 * width)
    for q in range(per):
        if q and q == per - 1:
            late, wz = lax.optimization_barrier((tokens, wz))
            pieces.append(late[q * CHUNK :])
        for k in range(2, n, 2):
            far[k, q] = swap(pieces[q], "exp", k)
    sibling = swap(tokens, "exp", 1)
    for k in range(0, n, 2):
        down[k + 1] = swap(down[k], "exp", 1)
        notes[k + 1] = swap(notes[k], "exp", 1)
    downs = [down[k] for k in range(n)]
    notes = [notes[k] for k in range(n)]
    up = adapter_up_weight.reshape(experts, 2 * width)
    call = functools.partial(
        project, devices=n, wz=wz, wbc=state_map_weight, up=up, rank=rank,
        dtb=step_size_bias[None, :], rate=head_decay_rate[None, :],
    )
    z, *sums, lift, rows, tails, rim, wsm, masks = call(
        [tokens, sibling], notes=notes, dt_t=step_size_weight.T, downs=downs
    )
    gates = [gate_project([rows], [lift], wz, up, n)]
    rim = lax.ppermute(rim, "seq", [(i, (i + 1) % shards) for i in range(shards)])
    params = [
        inner_conv_taps, state_map_taps, inner_conv_bias[None, :], state_map_conv_bias[None, :],
    ]
    kept = run_states(total, z, sums, z, tails, rim, params, width, per, None, None)
    far_rows = {}
    for q in range(per):
        for k in range(2, n, 2):
            mine = far[k, q]
            other = swap(mine, "exp", 1)
            older = far_rows[k, q - 1][2] if q else z
            pieces = [[mine, other]] if (k, q) != (n - 2, per - 1) else [[mine], [other]]
            found = []
            for p, piece in enumerate(pieces):
                new_z, *sums, lift, rows = call(
                    piece,
                    route_from=tuple(
                        ((k + p + m) * local + q * CHUNK, CHUNK) for m in range(len(piece))
                    ),
                    routes=masks,
                    wsm=wsm,
                )
                kept = run_states(
                    total, new_z, sums, older, tails, rim, params, width, per, (k + p, q), kept
                )
                found.append((rows, lift))
            far_rows[k, q] = ([f[0] for f in found], [f[1] for f in found], new_z)
    xc, cum, cum_t, step_t, updates, totals = kept
    states, before, parts = stitch(updates, totals)
    for d, radix in stages(shards):
        last = 2 * d == shards
        got = {}
        for p, part in enumerate(parts):
            for k in range(1, radix):
                got[p, k] = swap(part[0], "seq", d * k)
        for p, part in enumerate(parts):
            arrived = [got[p, k] for k in range(1, radix)]
            if last:
                parts[p] = [arrived[0], *part[3:]]
            else:
                parts[p] = combine(d, arrived, *part[1:])
    entering = [x for part in parts for x in part]
    for k in range(2, n, 2):
        for q in range(per):
            gates.append(gate_project(far_rows[k, q][0], far_rows[k, q][1], wz, up, n))
    abc = ()
    for skip, count, used in ((0, 2 * per, 1), (2 * per, (n - 2) * per, len(gates))):
        abc = run_outputs(
            xc, cum, cum_t, step_t, before, states, gates[:used], direct_head_scale[None, :],
            local, skip, count, abc,
        )
    a, b, c = abc
    gated, mine = join(shards // 2, a, b, c, entering)
    others = []
    for k in range(1, n):
        others.append(swap(mine, "exp", k))
    return norm(gated, [mine, *others], gated_norm_scale[None, :], width * n)


def solution(mesh):
    in_specs = (
        P(("seq", "exp"), None),
        P(("seq", "exp"), None),
        P(None, None, "exp"),
        P(),
        P(None, "exp"),
        P(None, "exp"),
        P(None, None, "exp"),
        P(None, "exp"),
        P(),
        P("exp"),
        P(),
        P("exp"),
        P("exp"),
        P("exp"),
        P("exp"),
    )
    out_specs = P("seq", "exp")

    return jax.shard_map(body, mesh=mesh, in_specs=in_specs, out_specs=out_specs, check_vma=False)
```
